32 devices in a mesh: groups: 1, seq: 16 (over z, y, core), head: 2 (over x).
Axes of the slice: x: 2, y: 2, z: 4, core: 2. Of those that a mesh axis runs over, the one named last changes fastest.
Arguments:
- x_proj: bfloat16 [12288, 8192], P(('groups', 'seq'), 'head'), may hold values from -6 to 6
- z_gate: bfloat16 [12288, 8192], P(('groups', 'seq'), 'head'), may hold values from -6 to 6
- bc_proj: bfloat16 [12288, 8, 256], P(('groups', 'seq'), 'head'), may hold values from -6 to 6
- dt_proj: bfloat16 [12288, 128], P(('groups', 'seq'), 'head'), may hold values from -5 to 5
- dt_bias: float32 [128], P('head'), may hold values from -4 to -1
- decay_log: float32 [128], P('head'), may hold values from -10 to 1
- skip_gain: float32 [128], P('head'), may hold values from 0.5 to 2
- conv_x: float32 [4, 8192], P(None, 'head'), may hold values from -3 to 3
- bias_x: float32 [8192], P('head'), may hold values from -3 to 3
- conv_bc: float32 [4, 8, 256], P(None, 'head'), may hold values from -3 to 3
- bias_bc: float32 [8, 256], P('head'), may hold values from -3 to 3
- norm_gain: float32 [8192], P('head'), may hold values from 0.5 to 1.5
- seg_lengths: int32 [4], P('groups'), may hold values from 1 to 6144, 12288 in all
Outputs:
- mixed: bfloat16 [12288, 8192], P(('groups', 'seq'), 'head')
The draws below stay inside these ranges and needn't reach their ends.
Inputs may be any that keep to these rules, and one draw needn't show every extreme that they name: `seg_lengths`: the 4 rollouts fill the pack of 12288 tokens in order; the longest has exactly 6144 tokens.
All inputs are finite; a program needn't handle non-finite values.
Results may differ from the reference program's by a relative error of at most 0.0049.
Values may be sent and summed in bfloat16 or wider, within the bound.
A program may use at most 256 MiB of HBM per device.

```python
import math
import jax
import jax.numpy as jnp
import numpy as np
from jax import lax

HEADS = 128
HEAD_DIM = 64
STATE = 128
GROUPS = 8
CONV = 4
BLOCK = 128
DI = 8192
SEQ = 12288
NSEG = 4
MOST = 6144


def draw_dt_proj(key, part):
    values = jax.random.truncated_normal(key, -5.0, 5.0, (SEQ, HEADS), jnp.float32)
    return values.astype(jnp.bfloat16)


def level_of(key, dims, pieces, least, largest):
    def one(position, blocks):
        heights = jax.random.uniform(jax.random.fold_in(jax.random.fold_in(key, 6), position), (blocks,), jnp.float32, least / len(pieces), largest / len(pieces))
        return jnp.repeat(jnp.exp(heights), dims[position] // blocks).reshape((-1,) + (1,) * (len(dims) - position - 1))

    factor_of = one(*pieces[0])
    for cut in pieces[1:]:
        factor_of = factor_of * one(*cut)
    return factor_of


def profile(number_of, total, limit, lean):
    loads = [(1 << 20) // math.isqrt(rank ** lean) + 1 for rank in range(2, number_of + 1)]
    spare, given = total - limit - (number_of - 1), [1] * (number_of - 1)
    while spare > 0:
        free = [i for i in range(number_of - 1) if given[i] < limit]
        pool, budget = sum([loads[i] for i in free]), spare
        for i in free:
            extra = min(limit - given[i], max(1, budget * loads[i] // pool), spare)
            given[i] = given[i] + extra
            spare = spare - extra
    return np.array([limit] + given)


def ragged_sizes(rng, count, total, most, lean):
    if count == 2:
        one = jax.random.randint(rng, (), max(1, total - most), min(most, total - 1) + 1)
        return jnp.stack([one, total - one])
    tallies = jnp.asarray(profile(count, total, most, lean), jnp.int32)
    couples = (count - 1) // 2
    giver, taker = tallies[1:1 + 2 * couples:2], tallies[2:2 + 2 * couples:2]
    slack = jnp.minimum(giver - 1, most - taker)
    moved = jax.random.randint(jax.random.fold_in(rng, 1), (couples,), 0, 1 << 20) % (slack + 1)
    tallies = tallies.at[1:1 + 2 * couples:2].set(giver - moved).at[2:2 + 2 * couples:2].set(taker + moved)
    return tallies[jax.random.permutation(jax.random.fold_in(rng, 2), count)]


def normal_values(stream_key, extent, scale, limit, pieces=(), kind=jnp.bfloat16):
    level = level_of(stream_key, extent, pieces, -0.22, 0.18) if pieces else 1.0
    drawn = jax.random.normal(stream_key, extent, jnp.float32) * scale * level
    return jnp.minimum(jnp.maximum(drawn, -limit), limit).astype(kind)


def setup_inputs(seed: int = 0, part: int = 0) -> dict:
    splits = jax.random.split(jax.random.key(seed), 14)
    part_splits = jax.random.split(jax.random.fold_in(splits[13], part), 14)
    x_proj = normal_values(part_splits[0], (SEQ, DI), 1.0, 6.0, ((0, 16), (1, 2)))
    z_gate = normal_values(part_splits[1], (SEQ, DI), 1.0, 6.0, ((0, 16), (1, 2)))
    bc_proj = normal_values(part_splits[2], (SEQ, GROUPS, 2 * STATE), 1.0, 6.0, ((0, 16), (1, 2)))
    dt_proj = draw_dt_proj(jax.random.fold_in(jax.random.fold_in(splits[13], part), 71), part)
    dt_bias = jnp.clip(-4.0 + 3.0 * jax.random.uniform(splits[4], (HEADS,), jnp.float32) ** level_of(splits[4], (HEADS,), ((0, 2),), -0.2, 0.2), -4.0, -1.0)
    decay_log = jnp.clip(-10.0 + 11.0 * jax.random.uniform(splits[5], (HEADS,), jnp.float32) ** level_of(splits[5], (HEADS,), ((0, 2),), -0.2, 0.2), -10.0, 1.0)
    skip_gain = jnp.clip(0.5 + 1.5 * jax.random.uniform(splits[6], (HEADS,), jnp.float32) ** level_of(splits[6], (HEADS,), ((0, 2),), -0.2, 0.2), 0.5, 2.0)
    conv_x = normal_values(splits[7], (CONV, DI), 0.5, 3.0, ((1, 2),), jnp.float32)
    bias_x = normal_values(splits[8], (DI,), 0.5, 3.0, ((0, 2),), jnp.float32)
    conv_bc = normal_values(splits[9], (CONV, GROUPS, 2 * STATE), 0.5, 3.0, ((1, 2),), jnp.float32)
    bias_bc = normal_values(splits[10], (GROUPS, 2 * STATE), 0.5, 3.0, ((0, 2),), jnp.float32)
    norm_gain = jnp.clip(1.0 + 0.1 * jax.random.normal(splits[11], (DI,), jnp.float32), 0.5, 1.5)
    seg_lengths = ragged_sizes(part_splits[12], NSEG, SEQ, MOST, 2).astype(jnp.int32)
    return {"x_proj": x_proj, "z_gate": z_gate, "bc_proj": bc_proj, "dt_proj": dt_proj, "dt_bias": dt_bias, "decay_log": decay_log, "skip_gain": skip_gain, "conv_x": conv_x, "bias_x": bias_x, "conv_bc": conv_bc, "bias_bc": bias_bc, "norm_gain": norm_gain, "seg_lengths": seg_lengths}


def segment_of(seg_lengths, positions):
    starts = jnp.cumsum(seg_lengths) - seg_lengths
    hits = (starts[None, :] <= positions[:, None]).astype(jnp.int32)
    return (lax.optimization_barrier(jnp.sum(hits, axis=1)) - 1).astype(jnp.int32)

def conv_mix(extended, ext_segment, weight, bias):
    lookback = weight.shape[0] - 1
    length = extended.shape[0] - lookback
    own_seg = ext_segment[lookback:]
    trailing = (1,) * (extended.ndim - 1)
    total = bias.astype(jnp.float32)[None]
    for tap_index in range(weight.shape[0]):
        valid = (ext_segment[tap_index:tap_index + length] == own_seg).astype(jnp.float32).reshape((length,) + trailing)
        total = total + weight[tap_index].astype(jnp.float32)[None] * extended[tap_index:tap_index + length].astype(jnp.float32) * valid
    return jax.nn.silu(total)

def gated_norm(values, gate, gain, groups_here):
    gated = values * jax.nn.silu(gate.astype(jnp.float32))
    length = gated.shape[0]
    grouped = gated.reshape(length, groups_here, -1)
    meansq = lax.optimization_barrier(jnp.mean(grouped * grouped, axis=2, keepdims=True))
    normed = (grouped * lax.rsqrt(meansq + 1e-05)).reshape(length, -1)
    return (normed * gain[None]).astype(jnp.bfloat16)

def state_read(c_part, grouped):
    upper = grouped.astype(jnp.bfloat16)
    lower = (grouped - upper.astype(jnp.float32)).astype(jnp.bfloat16)
    c_float = c_part.astype(jnp.float32)
    first = jnp.einsum('tgn,grpn->tgrp', c_float, upper.astype(jnp.float32))
    second = jnp.einsum('tgn,grpn->tgrp', c_float, lower.astype(jnp.float32))
    return first + second

def block_step(state, inputs):
    values, b_part, c_part, step_size, log_decay, segment, previous = inputs
    length, heads_here, head_width = values.shape
    groups_here = b_part.shape[1]
    repeat = heads_here // groups_here
    cumulative = jnp.cumsum(log_decay, axis=0)
    causal = jnp.arange(length)[:, None] >= jnp.arange(length)[None, :]
    allowed = causal & (segment[:, None] == segment[None, :])
    columns = cumulative.T
    spread = jnp.where(allowed[None], columns[:, :, None] - columns[:, None, :], -jnp.inf)
    scores = jnp.einsum('tgn,sgn->gts', c_part.astype(jnp.float32), b_part.astype(jnp.float32))
    scores = jnp.repeat(scores, repeat, axis=0)
    weights = (scores * jnp.exp(spread) * step_size.T[:, None, :]).astype(jnp.bfloat16)
    output = jnp.einsum('hts,shp->thp', weights.astype(jnp.float32), values.astype(jnp.float32))
    alive = (segment == previous).astype(jnp.float32)
    grouped = state.reshape(groups_here, repeat, head_width, -1)
    carried = state_read(c_part, grouped).reshape(length, heads_here, head_width)
    output = output + (jnp.exp(cumulative) * alive[:, None])[:, :, None] * carried
    same_end = (segment == segment[-1]).astype(jnp.float32)
    tail_weight = jnp.exp(cumulative[-1][None, :] - cumulative) * same_end[:, None] * step_size
    scaled = (values.astype(jnp.float32) * tail_weight[:, :, None]).astype(jnp.bfloat16)
    update = jnp.einsum('sgrp,sgn->grpn', scaled.reshape(length, groups_here, repeat, head_width).astype(jnp.float32), b_part.astype(jnp.float32))
    state = (jnp.exp(cumulative[-1]) * alive[-1])[:, None, None] * state + update.reshape(state.shape)
    return (state, output)

def reference(x_proj, z_gate, bc_proj, dt_proj, dt_bias, decay_log, skip_gain, conv_x, bias_x, conv_bc, bias_bc, norm_gain, seg_lengths):
    lookback = conv_x.shape[0] - 1
    positions = jnp.arange(-lookback, SEQ, dtype=jnp.int32)
    segments = segment_of(seg_lengths, positions)
    zero_x = jnp.zeros((lookback,) + x_proj.shape[1:], x_proj.dtype)
    zero_bc = jnp.zeros((lookback,) + bc_proj.shape[1:], bc_proj.dtype)
    mixed_x = conv_mix(jnp.concatenate([zero_x, x_proj]), segments, conv_x, bias_x).astype(jnp.bfloat16)
    mixed_bc = conv_mix(jnp.concatenate([zero_bc, bc_proj]), segments, conv_bc, bias_bc).astype(jnp.bfloat16)
    step_size = jax.nn.softplus(dt_proj.astype(jnp.float32) + dt_bias[None])
    log_decay = -jnp.exp(decay_log)[None] * step_size
    own_segment = segments[lookback:]
    block_count = SEQ // BLOCK
    block_prev = segments[lookback - 1::BLOCK][:block_count]
    values = mixed_x.reshape(SEQ, HEADS, HEAD_DIM)
    inputs = (values.reshape(block_count, BLOCK, HEADS, HEAD_DIM), mixed_bc[:, :, :STATE].reshape(block_count, BLOCK, GROUPS, STATE), mixed_bc[:, :, STATE:].reshape(block_count, BLOCK, GROUPS, STATE), step_size.reshape(block_count, BLOCK, HEADS), log_decay.reshape(block_count, BLOCK, HEADS), own_segment.reshape(block_count, BLOCK), block_prev)
    final_state, output = lax.scan(block_step, jnp.zeros((HEADS, HEAD_DIM, STATE), jnp.float32), inputs)
    output = output.reshape(SEQ, HEADS, HEAD_DIM) + skip_gain[None, :, None] * values.astype(jnp.float32)
    return gated_norm(output.reshape(SEQ, DI), z_gate, norm_gain, GROUPS)
```

```python
import functools

import jax
import jax.numpy as jnp
from jax import lax
from jax.experimental import pallas as pl
from jax.experimental.pallas import tpu as pltpu
from jax.sharding import PartitionSpec as P

HEAD_DIM = 64
STATE = 128
BLOCK = 128
LANES = 128
TAIL = 16
CHUNK = 256
VMEM_LIMIT = 60 << 20
LOG2E = 1.4426950408889634
MESH = pl.DeviceIdType.MESH
F32 = jnp.float32
BF16 = jnp.bfloat16


def silu_of_half(half):
    return half + half * jnp.tanh(half)


def mm(a, b, dims=((1,), (0,))):
    return lax.dot_general(a, b, (dims, ((), ())), preferred_element_type=F32)


def ids_of(starts, positions):
    found = jnp.full(positions.shape, -1, jnp.int32)
    for start in starts:
        found = jnp.where(positions >= start, start, found)
    return found


def id_of(starts, position):
    found = jnp.int32(-1)
    for start in starts:
        found = jnp.where(position >= start, start, found)
    return found


def column(row):
    n = row.shape[1]
    i = lax.broadcasted_iota(jnp.int32, (n, n), 0)
    j = lax.broadcasted_iota(jnp.int32, (n, n), 1)
    return jnp.sum(jnp.where(i == j, row, 0.0), axis=1, keepdims=True)


def fill_spread(e_ref):
    twice, wide = e_ref.shape
    row = lax.broadcasted_iota(jnp.int32, (twice, wide), 0)
    lane = lax.broadcasted_iota(jnp.int32, (twice, wide), 1)
    e_ref[...] = (lane // HEAD_DIM == row % (twice // 2)).astype(F32).astype(BF16)


def halves(value):
    hi = value.astype(BF16)
    lo = (value - hi.astype(F32)).astype(BF16)
    return jnp.concatenate([hi, lo], axis=0)


def expand(value, e_ref):
    return mm(halves(value), e_ref[...], ((0,), (0,)))


def shift_matrix(within):
    t = lax.broadcasted_iota(jnp.int32, (BLOCK, TAIL + BLOCK), 0)
    i = lax.broadcasted_iota(jnp.int32, (BLOCK, TAIL + BLOCK), 1)
    steps = [((i == t + (TAIL - 3 + k)) & (within >= 3 - k)).astype(F32) for k in range(3)]
    return jnp.concatenate(steps, axis=0).astype(BF16)


def conv_tile(src, shift, weights, bias):
    past = mm(shift, src)
    own = src[TAIL:, :].astype(F32)
    half = 0.5 * bias + (0.5 * weights[3]) * own
    for k in range(3):
        half = half + (0.5 * weights[k]) * past[k * BLOCK : (k + 1) * BLOCK]
    return silu_of_half(half).astype(BF16)


def prepare(
    seg_ref, dtp_ref, dtb_ref, dec_ref, skip_ref,
    ecarry_ref, shift_ref, mask_ref, tailw_ref, cfac_ref, ends_ref, lower_ref, cols_ref, skip_row, total_d, e_ref,
):
    heads, rows = dtp_ref.shape
    groups = total_d.shape[0]
    repeat = heads // groups
    wide = e_ref.shape[1]
    fill_spread(e_ref)
    skip = jnp.broadcast_to(column(skip_ref[...]), (heads, LANES))
    for g in range(groups):
        skip_row[:, g * wide : (g + 1) * wide] = expand(skip[g * repeat : (g + 1) * repeat], e_ref)[0:8]
    first = lax.axis_index("seq") * rows
    starts = [jnp.int32(0)]
    for j in range(seg_ref.shape[0] - 1):
        starts.append(starts[-1] + seg_ref[j])
    entered = id_of(starts, first - 1)
    bias = column(dtb_ref[...])
    rate = -LOG2E * column(jnp.exp(dec_ref[...]))
    s = lax.broadcasted_iota(jnp.int32, (BLOCK, BLOCK), 0)
    t = lax.broadcasted_iota(jnp.int32, (BLOCK, BLOCK), 1)
    upper = (s <= t).astype(F32).astype(BF16)
    base = jnp.zeros((heads, LANES), F32)
    for b in range(rows // BLOCK):
        cut = slice(b * BLOCK, (b + 1) * BLOCK)
        raw = dtp_ref[:, cut].astype(F32) + bias
        dt = jnp.maximum(raw, 0.0) + jnp.log1p(jnp.exp(-jnp.abs(raw)))
        rest = rate * dt
        parts = []
        for _ in range(3):
            parts.append(rest.astype(BF16))
            rest = rest - parts[-1].astype(F32)
        sums = mm(jnp.concatenate(parts, axis=0), upper)
        cum = sums[0:heads] + (sums[heads : 2 * heads] + sums[2 * heads : 3 * heads])
        at = first + b * BLOCK
        tall = at + s
        tall_id = ids_of(starts, tall)
        row_id = ids_of(starts, at + lax.broadcasted_iota(jnp.int32, (1, LANES), 1))
        before, end = id_of(starts, at - 1), id_of(starts, at + BLOCK - 1)
        same_end = (row_id == end).astype(F32)
        last = jnp.broadcast_to(cum[:, BLOCK - 1 : BLOCK], cum.shape)
        shift_ref[b] = shift_matrix((tall - tall_id)[:, 0:1])
        mask_ref[b] = ((t <= s) & (tall_id == row_id)).astype(F32)
        tailw_ref[b] = jnp.exp2(last - cum) * dt * same_end
        cfac_ref[b] = jnp.exp2(cum) * (row_id == before).astype(F32)
        ecarry_ref[:, cut] = jnp.exp2(base + cum) * (row_id == entered).astype(F32)
        ends_ref[b] = jnp.exp2(last) * (end == before).astype(F32)
        lower_ref[b] = cum - jnp.log2(dt)
        for g in range(groups):
            cols_ref[b * groups + g, :, 0:repeat] = jnp.transpose(cum[g * repeat : (g + 1) * repeat])
        base = base + last
    leaving = id_of(starts, first + rows - 1)
    whole = jnp.exp2(base) * (leaving == entered).astype(F32)
    for g in range(groups):
        total_d[g] = expand(whole[g * repeat : (g + 1) * repeat], e_ref)[0:8]


def states_of(
    g, b, xbuf, bbuf, wx_ref, bx_ref, wbc_ref, bbc_ref, shift_ref, tailw_ref, ends_ref, e_ref,
    xc, bpart, c_ref, entering, state,
):
    repeat = e_ref.shape[0] // 2
    wide = e_ref.shape[1]
    low = pl.multiple_of(b * BLOCK, BLOCK)
    rows, tall = pl.ds(low, BLOCK), pl.ds(low, TAIL + BLOCK)
    heads = pl.ds(pl.multiple_of(g * repeat, repeat), repeat)
    shift = shift_ref[b]
    weights = [wbc_ref[g, k : k + 1, :] for k in range(4)]
    bc = conv_tile(bbuf[g, tall, :], shift, weights, bbc_ref[g])
    bpart[g, rows, :] = bc[:, 0:STATE]
    c_ref[g, rows, :] = bc[:, STATE:]
    turned = jnp.transpose(bc[:, 0:STATE].astype(F32)).astype(BF16)
    tail = jnp.transpose(halves(tailw_ref[b, heads, :]).astype(F32)).astype(BF16)
    decay = expand(ends_ref[b, heads, 0:8], e_ref)
    for j in range(0, wide, CHUNK):
        cols = slice(j, j + CHUNK)
        weights = [wx_ref[g, k : k + 1, cols] for k in range(4)]
        value = conv_tile(xbuf[g, tall, cols], shift, weights, bx_ref[g, :, cols])
        xc[g, rows, cols] = value
        scaled = (value.astype(F32) * mm(tail, e_ref[:, cols])).astype(BF16)
        old = state[g, :, cols]
        entering[g, b, :, cols] = old.astype(BF16)
        state[g, :, cols] = decay[0:1, cols] * old + mm(turned, scaled)


def within_of(g, b, xc, bpart, c_ref, entering, mask_ref, cfac_ref, lower_ref, cols_ref, skip_row, e_ref, yv):
    groups = xc.shape[0]
    repeat = e_ref.shape[0] // 2
    wide = e_ref.shape[1]
    rows = pl.ds(pl.multiple_of(b * BLOCK, BLOCK), BLOCK)
    heads = pl.ds(pl.multiple_of(g * repeat, repeat), repeat)
    b_part, c_part = bpart[g, rows, :], c_ref[g, rows, :]
    scores = mm(c_part, b_part, ((1,), (1,))) * mask_ref[b]
    carry = jnp.transpose(halves(cfac_ref[b, heads, :]).astype(F32)).astype(BF16)
    columns = cols_ref[b * groups + g]
    lower = lower_ref[b, heads, :]
    left = lax.broadcasted_iota(jnp.int32, (BLOCK, LANES), 1) < HEAD_DIM
    for j in range(0, wide, CHUNK):
        cols = slice(j, j + CHUNK)
        carried = mm(c_part, entering[g, b, :, cols]) * mm(carry, e_ref[:, cols])
        for k in range(0, CHUNK, LANES):
            sl = slice(j + k, j + k + LANES)
            parts = []
            for h in ((j + k) // HEAD_DIM, (j + k) // HEAD_DIM + 1):
                spread = jnp.minimum(columns[:, h : h + 1] - lower[h : h + 1, :], 80.0)
                parts.append((scores * jnp.exp2(spread)).astype(BF16))
            value = xc[g, rows, sl]
            none = jnp.zeros_like(value)
            pair = jnp.concatenate([jnp.where(left, value, none), jnp.where(left, none, value)], axis=0)
            y = mm(jnp.concatenate(parts, axis=1), pair)
            skip = skip_row[0:1, pl.ds(pl.multiple_of(g * wide + j + k, LANES), LANES)]
            yv[g, rows, sl] = (y + carried[:, k : k + LANES] + skip * value.astype(F32)).astype(BF16)


def pack_d(d):
    hi = d.astype(BF16).astype(F32)
    return jnp.concatenate([hi, d - hi], axis=0).astype(BF16)


def unpack_d(packed):
    both = packed.astype(F32)
    return both[0:8] + both[8:16]


class Exchange:
    def __init__(self, state, total_d, hin, bufs, sems):
        self.state, self.total_d, self.hin = state, total_d, hin
        (self.give1, self.take1, self.give2, self.take2, self.zgive, self.ztake, self.back2, self.home2,
         self.back1, self.home1, self.half_s, self.half_d, self.e_s, self.e_d, self.p_s, self.p_d) = bufs
        self.sem1, self.sem2, self.semz, self.sem4, self.sem5 = sems
        peers = lax.axis_size("seq")
        me = lax.axis_index("seq")
        self.me, self.peers = me, peers
        self.core, self.pair, self.link, self.links = lax.rem(me, 2), lax.rem(me // 2, 2), me // 4, peers // 4
        self.low1, self.low2 = self.core == 0, self.pair == 0
        self.near, self.far = me + 1 - 2 * self.core, me + 2 - 4 * self.pair
        self.half = state.shape[2] // 2
        self.quarter = self.half // 2
        self.rounds = max(1, (self.links - 1).bit_length())
        self.count = 6 + self.rounds

    def copy(self, src, dst, sems, peer):
        return pltpu.make_async_remote_copy(
            src_ref=src, dst_ref=dst, send_sem=sems.at[0], recv_sem=sems.at[1],
            device_id={"seq": peer}, device_id_type=MESH,
        )

    def copy1(self, g):
        return self.copy(self.give1.at[g], self.take1.at[g], self.sem1.at[g], self.near)

    def copy2(self, g):
        return self.copy(self.give2.at[g], self.take2.at[g], self.sem2.at[g], self.far)

    def copyz(self, r, g):
        return self.copy(self.zgive.at[r, g], self.ztake.at[r, g], self.semz.at[r, g], self.me + (4 << r))

    def copy4(self, g):
        return self.copy(self.back2.at[g], self.home2.at[g], self.sem4.at[g], self.far)

    def copy5(self, g):
        return self.copy(self.back1.at[g], self.home1.at[g], self.sem5.at[g], self.near)

    def greet(self):
        me, link = self.me, self.link
        found = [(None, self.near), (None, self.far), (me >= 1, me - 1), (me + 1 < self.peers, me + 1)]
        for r in range(self.rounds):
            found += [(link >= 1 << r, me - (4 << r)), (link + (1 << r) < self.links, me + (4 << r))]
        barrier = pltpu.get_barrier_semaphore()
        expected = jnp.int32(0)
        for known, peer in found:
            if known is None:
                pl.semaphore_signal(barrier, inc=1, device_id={"seq": peer}, device_id_type=MESH)
                expected = expected + 1
            else:
                expected = expected + known.astype(jnp.int32)

                @pl.when(known)
                def _():
                    pl.semaphore_signal(barrier, inc=1, device_id={"seq": peer}, device_id_type=MESH)

        pl.semaphore_wait(barrier, expected)

    def half_lanes(self, which):
        return pl.ds(pl.multiple_of(which * self.half, LANES), self.half)

    def lanes(self, q):
        return pl.ds(pl.multiple_of(self.core * self.half + q * self.quarter, LANES), self.quarter)

    def inner(self, q):
        return pl.ds(pl.multiple_of(q * self.quarter, LANES), self.quarter)

    def stage(self, k, g):
        if k == 0:
            self.begin(g)
        elif k == 1:
            self.cores(g)
        elif k == 2:
            self.chips(g)
        elif k < 3 + self.rounds:
            self.along(k - 3, g)
        elif k == 3 + self.rounds:
            self.enter(g)
        elif k == 4 + self.rounds:
            self.share(g)
        else:
            self.finish(g)

    def begin(self, g):
        other = self.half_lanes(1 - self.core)
        self.give1[g, 0:STATE, :] = self.state[g, :, other].astype(BF16)
        self.give1[g, STATE:, :] = pack_d(self.total_d[g, :, other])
        self.copy1(g).start()

    def of_chip(self, g, q):
        mine, other = self.state[g, :, self.lanes(q)], self.take1[g, 0:STATE, self.inner(q)].astype(F32)
        d_mine, d_other = self.total_d[g, :, self.lanes(q)], unpack_d(self.take1[g, STATE:, self.inner(q)])
        late = jnp.where(self.low1, d_other, d_mine)[0:1]
        total = late * jnp.where(self.low1, mine, other) + jnp.where(self.low1, other, mine)
        return total, d_mine * d_other

    def cores(self, g):
        self.copy1(g).wait()
        total, d = self.of_chip(g, 1 - self.pair)
        self.give2[g, 0:STATE, :] = total.astype(BF16)
        self.give2[g, STATE:, :] = pack_d(d)
        self.copy2(g).start()
        total, d = self.of_chip(g, self.pair)
        self.half_s[g] = total
        self.half_d[g] = d

    def chips(self, g):
        self.copy2(g).wait()
        mine, other = self.half_s[g], self.take2[g, 0:STATE, :].astype(F32)
        d_mine, d_other = self.half_d[g], unpack_d(self.take2[g, STATE:, :])
        late = jnp.where(self.low2, d_other, d_mine)[0:1]
        self.p_s[g] = late * jnp.where(self.low2, mine, other) + jnp.where(self.low2, other, mine)
        self.p_d[g] = d_mine * d_other
        self.e_s[g] = jnp.zeros(self.e_s.shape[1:], F32)
        self.e_d[g] = jnp.ones(self.e_d.shape[1:], F32)
        self.pass_on(0, g)

    def pass_on(self, r, g):
        @pl.when(self.link + (1 << r) < self.links)
        def _():
            self.zgive[r, g, 0:STATE, :] = self.p_s[g].astype(BF16)
            self.zgive[r, g, STATE:, :] = pack_d(self.p_d[g])
            self.copyz(r, g).start()

    def along(self, r, g):
        @pl.when(self.link >= 1 << r)
        def _():
            self.copyz(r, g).wait_recv()
            got, d = self.ztake[r, g, 0:STATE, :].astype(F32), unpack_d(self.ztake[r, g, STATE:, :])
            self.e_s[g] = self.e_d[g, 0:1, :] * got + self.e_s[g]
            self.e_d[g] = self.e_d[g] * d
            if r + 1 < self.rounds:
                self.p_s[g] = self.p_d[g, 0:1, :] * got + self.p_s[g]
                self.p_d[g] = self.p_d[g] * d

        if r + 1 < self.rounds:
            self.pass_on(r + 1, g)

    def hand_over(self, g, q, into):
        mine, other = self.state[g, :, self.lanes(q)], self.take1[g, 0:STATE, self.inner(q)].astype(F32)
        d_mine, d_other = self.total_d[g, :, self.lanes(q)], unpack_d(self.take1[g, STATE:, self.inner(q)])
        early = jnp.where(self.low1, d_mine, d_other)[0:1]
        passed = early * into + jnp.where(self.low1, mine, other)
        self.hin[g, :, self.lanes(q)] = jnp.where(self.low1, into, passed).astype(BF16)
        self.back1[g, :, self.inner(q)] = jnp.where(self.low1, passed, into).astype(BF16)

    def enter(self, g):
        into = self.e_s[g]
        mine, other = self.half_s[g], self.take2[g, 0:STATE, :].astype(F32)
        d_mine, d_other = self.half_d[g], unpack_d(self.take2[g, STATE:, :])
        early = jnp.where(self.low2, d_mine, d_other)[0:1]
        passed = early * into + jnp.where(self.low2, mine, other)
        self.back2[g] = jnp.where(self.low2, passed, into).astype(BF16)
        self.copy4(g).start()
        self.hand_over(g, self.pair, jnp.where(self.low2, into, passed))

    def share(self, g):
        self.copy4(g).wait()
        self.hand_over(g, 1 - self.pair, self.home2[g].astype(F32))
        self.copy5(g).start()

    def finish(self, g):
        self.copy5(g).wait()
        self.hin[g, :, self.half_lanes(1 - self.core)] = self.home1[g]
        for r in range(self.rounds):

            @pl.when(self.link + (1 << r) < self.links)
            def _():
                self.copyz(r, g).wait_send()


def mixer_kernel(
    seg_ref, x_ref, bc_ref, dtp_ref, dtb_ref, dec_ref, skip_ref, wx_ref, bx_ref, wbc_ref, bbc_ref,
    y_ref, c_ref, hin_ref, ecarry_ref,
    xbuf, bbuf, xtail, btail, xc, bpart, entering, state, total_d, yv,
    shift_ref, mask_ref, tailw_ref, cfac_ref, ends_ref, lower_ref, cols_ref, skip_row, e_ref,
    give1, take1, give2, take2, zgive, ztake, back2, home2, back1, home1,
    half_s, half_d, e_s, e_d, p_s, p_d,
    sem1, sem2, semz, sem4, sem5, semx, semb, semt, semy,
):
    groups, _, wide = xbuf.shape
    rows = x_ref.shape[0]
    blocks = rows // BLOCK
    step = 2 - blocks % 2
    turns = blocks // step
    exchange = Exchange(
        state, total_d, hin_ref,
        (give1, take1, give2, take2, zgive, ztake, back2, home2, back1, home1, half_s, half_d, e_s, e_d, p_s, p_d),
        (sem1, sem2, semz, sem4, sem5),
    )
    me, peers = exchange.me, exchange.peers

    def load_x(g):
        return pltpu.make_async_copy(
            x_ref.at[:, g * wide : (g + 1) * wide], xbuf.at[g, pl.ds(TAIL, rows), :], semx.at[g]
        )

    def load_b(g):
        return pltpu.make_async_copy(
            bc_ref.at[:, g * 2 * STATE : (g + 1) * 2 * STATE], bbuf.at[g, pl.ds(TAIL, rows), :], semb.at[g]
        )

    for g in range(groups):
        load_b(g).start()
        load_x(g).start()
    tails = [
        exchange.copy(x_ref.at[pl.ds(rows - TAIL, TAIL), :], xtail, semt.at[0], me + 1),
        exchange.copy(bc_ref.at[pl.ds(rows - TAIL, TAIL), :], btail, semt.at[1], me + 1),
    ]
    exchange.greet()

    @pl.when(me + 1 < peers)
    def _():
        for tail in tails:
            tail.start()

    prepare(
        seg_ref, dtp_ref, dtb_ref, dec_ref, skip_ref,
        ecarry_ref, shift_ref, mask_ref, tailw_ref, cfac_ref, ends_ref, lower_ref, cols_ref, skip_row, total_d, e_ref,
    )
    state[...] = jnp.zeros(state.shape, F32)

    @pl.when(me == 0)
    def _():
        xtail[...] = jnp.zeros(xtail.shape, BF16)
        btail[...] = jnp.zeros(btail.shape, BF16)

    @pl.when(me > 0)
    def _():
        for tail in tails:
            tail.wait_recv()

    for g in range(groups):
        load_b(g).wait()
        load_x(g).wait()
        xbuf[g, 0:TAIL, :] = xtail[:, g * wide : (g + 1) * wide]
        bbuf[g, 0:TAIL, :] = btail[:, g * 2 * STATE : (g + 1) * 2 * STATE]

    def stages(i, which):
        for k in which:
            n = i - (turns - 1) - k

            @pl.when((n >= 0) & (lax.rem(n, turns) == 0) & (n < groups * turns))
            def _():
                exchange.stage(k, lax.div(n, turns))

    def first_part(i, carry):
        g, p = lax.div(i, turns), lax.rem(i, turns)
        for b in range(step):
            states_of(
                g, step * p + b, xbuf, bbuf, wx_ref, bx_ref, wbc_ref, bbc_ref, shift_ref, tailw_ref, ends_ref, e_ref,
                xc, bpart, c_ref, entering, state,
            )
        stages(i, range(exchange.count))
        return carry

    def store(i):
        g, p = lax.div(i, turns), lax.rem(i, turns)
        part = pl.ds(pl.multiple_of(p * step * BLOCK, BLOCK), step * BLOCK)
        return pltpu.make_async_copy(
            yv.at[g, part, :], y_ref.at[part, pl.ds(pl.multiple_of(g * wide, LANES), wide)], semy.at[i]
        )

    def second_part(i, carry):
        g, p = lax.div(i, turns), lax.rem(i, turns)
        for b in range(step):
            within_of(
                g, step * p + b, xc, bpart, c_ref, entering,
                mask_ref, cfac_ref, lower_ref, cols_ref, skip_row, e_ref, yv,
            )
        store(i).start()
        stages(i + groups * turns, range(1, exchange.count))
        return carry

    lax.fori_loop(0, groups * turns, first_part, 0)
    lax.fori_loop(0, groups * turns, second_part, 0)
    left = exchange.count - 1 - groups * turns
    for i in range(max(0, left)):
        stages(jnp.int32(2 * groups * turns + i), range(1, exchange.count))
    for i in range(groups * turns):
        store(jnp.int32(i)).wait()

    @pl.when(me + 1 < peers)
    def _():
        for tail in tails:
            tail.wait_send()


def output_kernel(y_ref, c_ref, z_ref, hin_ref, ecarry_ref, gain_ref, out_ref, e_ref, gated):
    @pl.when((pl.program_id(0) == 0) & (pl.program_id(1) == 0))
    def _():
        fill_spread(e_ref)

    wide = y_ref.shape[1]
    for r in range(0, y_ref.shape[0], BLOCK):
        rows = slice(r, r + BLOCK)
        carry = jnp.transpose(halves(ecarry_ref[:, rows]).astype(F32)).astype(BF16)
        c_part = c_ref[0, rows, :]
        squares = jnp.zeros((BLOCK, LANES), F32)
        for j in range(0, wide, CHUNK):
            cols = slice(j, j + CHUNK)
            carried = mm(c_part, hin_ref[0, :, cols]) * mm(carry, e_ref[:, cols])
            full = y_ref[rows, cols].astype(F32) + carried
            held = full * silu_of_half(0.5 * z_ref[rows, cols].astype(F32))
            gated[rows, cols] = held
            for k in range(0, CHUNK, LANES):
                squares = squares + held[:, k : k + LANES] * held[:, k : k + LANES]
        mean = jnp.sum(squares, axis=1, keepdims=True) * (1.0 / wide)
        scale = jnp.broadcast_to(lax.rsqrt(mean + 1e-05), (BLOCK, LANES))
        for j in range(0, wide, LANES):
            sl = slice(j, j + LANES)
            out_ref[rows, sl] = (gated[rows, sl] * scale * gain_ref[0:1, sl]).astype(BF16)


def shards(
    x_proj, z_gate, bc_proj, dt_proj, dt_bias, decay_log, skip_gain,
    conv_x, bias_x, conv_bc, bias_bc, norm_gain, seg_lengths,
):
    rows, channels = x_proj.shape
    taps = conv_x.shape[0]
    heads = dt_proj.shape[1]
    groups = bc_proj.shape[1]
    repeat = heads // groups
    wide = channels // groups
    blocks = rows // BLOCK
    step = 2 - blocks % 2
    turns = blocks // step
    links = lax.axis_size("seq") // 4
    rounds = max(1, (links - 1).bit_length())
    bc = bc_proj.reshape(rows, groups * 2 * STATE)
    vmem = pl.BlockSpec(memory_space=pltpu.VMEM)
    anywhere = pl.BlockSpec(memory_space=pl.ANY)
    half, quarter = wide // 2, wide // 4
    scratch = lambda kind, *shape: pltpu.VMEM(shape, kind)
    dma = lambda *shape: pltpu.SemaphoreType.DMA(shape)
    per_block = (blocks, heads, BLOCK)
    y, c, hin, ecarry = pl.pallas_call(
        mixer_kernel,
        in_specs=[pl.BlockSpec(memory_space=pltpu.SMEM), anywhere, anywhere] + [vmem] * 8,
        out_specs=[anywhere, vmem, vmem, vmem],
        out_shape=[
            jax.ShapeDtypeStruct((rows, channels), BF16),
            jax.ShapeDtypeStruct((groups, rows, STATE), BF16),
            jax.ShapeDtypeStruct((groups, STATE, wide), BF16),
            jax.ShapeDtypeStruct((heads, rows), F32),
        ],
        scratch_shapes=[
            scratch(BF16, groups, TAIL + rows, wide), scratch(BF16, groups, TAIL + rows, 2 * STATE),
            scratch(BF16, TAIL, channels), scratch(BF16, TAIL, groups * 2 * STATE),
            scratch(BF16, groups, rows, wide), scratch(BF16, groups, rows, STATE),
            scratch(BF16, groups, blocks, STATE, wide), scratch(F32, groups, STATE, wide), scratch(F32, groups, 8, wide),
            scratch(BF16, groups, rows, wide),
            scratch(BF16, blocks, 3 * BLOCK, TAIL + BLOCK), scratch(F32, blocks, BLOCK, BLOCK),
            scratch(F32, *per_block), scratch(F32, *per_block), scratch(F32, *per_block), scratch(F32, *per_block),
            scratch(F32, blocks * groups, BLOCK, LANES), scratch(F32, 8, channels), scratch(BF16, 2 * repeat, wide),
            scratch(BF16, groups, STATE + 16, half), scratch(BF16, groups, STATE + 16, half),
            scratch(BF16, groups, STATE + 16, quarter), scratch(BF16, groups, STATE + 16, quarter),
            scratch(BF16, rounds, groups, STATE + 16, quarter), scratch(BF16, rounds, groups, STATE + 16, quarter),
            scratch(BF16, groups, STATE, quarter), scratch(BF16, groups, STATE, quarter),
            scratch(BF16, groups, STATE, half), scratch(BF16, groups, STATE, half),
            scratch(F32, groups, STATE, quarter), scratch(F32, groups, 8, quarter),
            scratch(F32, groups, STATE, quarter), scratch(F32, groups, 8, quarter),
            scratch(F32, groups, STATE, quarter), scratch(F32, groups, 8, quarter),
            dma(groups, 2), dma(groups, 2), dma(rounds, groups, 2), dma(groups, 2), dma(groups, 2),
            dma(groups), dma(groups), dma(2, 2), dma(groups * turns),
        ],
        compiler_params=pltpu.CompilerParams(
            collective_id=0, has_side_effects=True, vmem_limit_bytes=VMEM_LIMIT
        ),
        name="mixer",
    )(
        seg_lengths, x_proj, bc, dt_proj.T, dt_bias[None], decay_log[None], skip_gain[None],
        conv_x.reshape(taps, groups, wide).transpose(1, 0, 2), bias_x.reshape(groups, 1, wide),
        conv_bc.transpose(1, 0, 2), bias_bc[:, None],
    )

    tall = pl.BlockSpec((step * BLOCK, wide), lambda g, b: (b, g))
    return pl.pallas_call(
        output_kernel,
        grid=(groups, turns),
        in_specs=[
            tall, pl.BlockSpec((1, step * BLOCK, STATE), lambda g, b: (g, b, 0)), tall,
            pl.BlockSpec((1, STATE, wide), lambda g, b: (g, 0, 0)),
            pl.BlockSpec((repeat, step * BLOCK), lambda g, b: (g, b)),
            pl.BlockSpec((1, wide), lambda g, b: (0, g)),
        ],
        out_specs=tall,
        out_shape=jax.ShapeDtypeStruct((rows, channels), BF16),
        scratch_shapes=[scratch(BF16, 2 * repeat, wide), scratch(F32, step * BLOCK, wide)],
        compiler_params=pltpu.CompilerParams(
            dimension_semantics=("arbitrary", "arbitrary"), vmem_limit_bytes=VMEM_LIMIT
        ),
        name="outputs",
    )(y, c, z_gate, hin, ecarry, norm_gain[None])


def solution(mesh):
    return jax.shard_map(
        shards,
        mesh=mesh,
        in_specs=(
            P(("groups", "seq"), "head"),
            P(("groups", "seq"), "head"),
            P(("groups", "seq"), "head", None),
            P(("groups", "seq"), "head"),
            P("head"),
            P("head"),
            P("head"),
            P(None, "head"),
            P("head"),
            P(None, "head", None),
            P("head", None),
            P("head"),
            P("groups"),
        ),
        out_specs=P(("groups", "seq"), "head"),
        check_vma=False,
    )
```

```python
import functools

import jax
import jax.numpy as jnp
from jax import lax
from jax.experimental import pallas as pl
from jax.experimental.pallas import tpu as pltpu
from jax.sharding import PartitionSpec as P

HEAD_DIM = 64
STATE = 128
BLOCK = 128
LANES = 128
TAIL = 16
CHUNK = 256
PIECE = 16
SPACING = 2
VMEM_LIMIT = 60 << 20
LOG2E = 1.4426950408889634
MESH = pl.DeviceIdType.MESH
F32 = jnp.float32
BF16 = jnp.bfloat16


def silu_of_half(half):
    return half + half * jnp.tanh(half)


def mm(a, b, dims=((1,), (0,))):
    return lax.dot_general(a, b, (dims, ((), ())), preferred_element_type=F32)


def ids_of(starts, positions):
    found = jnp.full(positions.shape, -1, jnp.int32)
    for start in starts:
        found = jnp.where(positions >= start, start, found)
    return found


def id_of(starts, position):
    found = jnp.int32(-1)
    for start in starts:
        found = jnp.where(position >= start, start, found)
    return found


def column(row):
    n = row.shape[1]
    i = lax.broadcasted_iota(jnp.int32, (n, n), 0)
    j = lax.broadcasted_iota(jnp.int32, (n, n), 1)
    return jnp.sum(jnp.where(i == j, row, 0.0), axis=1, keepdims=True)


def fill_spread(e_ref):
    twice, wide = e_ref.shape
    row = lax.broadcasted_iota(jnp.int32, (twice, wide), 0)
    lane = lax.broadcasted_iota(jnp.int32, (twice, wide), 1)
    e_ref[...] = (lane // HEAD_DIM == row % (twice // 2)).astype(F32).astype(BF16)


def halves(value):
    hi = value.astype(BF16)
    lo = (value - hi.astype(F32)).astype(BF16)
    return jnp.concatenate([hi, lo], axis=0)


def expand(value, e_ref):
    return mm(halves(value), e_ref[...], ((0,), (0,)))


def shift_matrix(within):
    t = lax.broadcasted_iota(jnp.int32, (BLOCK, TAIL + BLOCK), 0)
    i = lax.broadcasted_iota(jnp.int32, (BLOCK, TAIL + BLOCK), 1)
    steps = [((i == t + (TAIL - 3 + k)) & (within >= 3 - k)).astype(F32) for k in range(3)]
    order = [steps[k][r : r + PIECE] for r in range(0, BLOCK, PIECE) for k in range(3)]
    return jnp.concatenate(order, axis=0).astype(BF16)


def conv_pieces(past, own, halfw):
    for r in range(0, BLOCK, PIECE):
        half = halfw[4] + halfw[3] * own[TAIL + r : TAIL + r + PIECE, :].astype(F32)
        for k in range(3):
            at = 3 * r + k * PIECE
            half = half + halfw[k] * past[at : at + PIECE]
        yield slice(r, r + PIECE), silu_of_half(half)


def pipelined(units):
    for u in range(len(units) + 2):
        for phase in range(3):
            if 0 <= u - phase < len(units):
                units[u - phase][phase]()


def prepare(
    seg_ref, dtp_ref, dtb_ref, dec_ref, skip_ref, wx_ref, bx_ref, wbc_ref, bbc_ref,
    ecarry_ref, shift_ref, mask_ref, tailw_ref, cfac_ref, ends_ref, lower_ref, cols_ref, skip_row, total_d, e_ref,
    hwx_ref, hwbc_ref,
):
    heads, rows = dtp_ref.shape
    groups = total_d.shape[0]
    repeat = heads // groups
    wide = e_ref.shape[1]
    fill_spread(e_ref)
    for g in range(groups):
        cols = slice(g * wide, (g + 1) * wide)
        for k in range(4):
            hwx_ref[g, k : k + 1, :] = 0.5 * wx_ref[k : k + 1, cols]
            hwbc_ref[g, k : k + 1, :] = 0.5 * wbc_ref[k, g : g + 1, :]
        hwx_ref[g, 4:5, :] = 0.5 * bx_ref[0:1, cols]
        hwbc_ref[g, 4:5, :] = 0.5 * bbc_ref[g : g + 1, :]
    skip = jnp.broadcast_to(column(skip_ref[...]), (heads, LANES))
    for g in range(groups):
        skip_row[:, g * wide : (g + 1) * wide] = expand(skip[g * repeat : (g + 1) * repeat], e_ref)[0:8]
    first = lax.axis_index("seq") * rows
    starts = [jnp.int32(0)]
    for j in range(seg_ref.shape[0] - 1):
        starts.append(starts[-1] + seg_ref[j])
    entered = id_of(starts, first - 1)
    bias = column(dtb_ref[...])
    rate = -LOG2E * column(jnp.exp(dec_ref[...]))
    s = lax.broadcasted_iota(jnp.int32, (BLOCK, BLOCK), 0)
    t = lax.broadcasted_iota(jnp.int32, (BLOCK, BLOCK), 1)
    upper = (s <= t).astype(F32).astype(BF16)
    base = jnp.zeros((heads, LANES), F32)
    for b in range(rows // BLOCK):
        cut = slice(b * BLOCK, (b + 1) * BLOCK)
        raw = dtp_ref[:, cut].astype(F32) + bias
        dt = jnp.maximum(raw, 0.0) + jnp.log1p(jnp.exp(-jnp.abs(raw)))
        rest = rate * dt
        parts = []
        for _ in range(3):
            parts.append(rest.astype(BF16))
            rest = rest - parts[-1].astype(F32)
        sums = mm(jnp.concatenate(parts, axis=0), upper)
        cum = sums[0:heads] + (sums[heads : 2 * heads] + sums[2 * heads : 3 * heads])
        at = first + b * BLOCK
        tall = at + s
        tall_id = ids_of(starts, tall)
        row_id = ids_of(starts, at + lax.broadcasted_iota(jnp.int32, (1, LANES), 1))
        before, end = id_of(starts, at - 1), id_of(starts, at + BLOCK - 1)
        same_end = (row_id == end).astype(F32)
        last = jnp.broadcast_to(cum[:, BLOCK - 1 : BLOCK], cum.shape)
        shift_ref[b] = shift_matrix((tall - tall_id)[:, 0:1])
        mask_ref[b] = ((t <= s) & (tall_id == row_id)).astype(F32)
        tailw_ref[b] = jnp.exp2(last - cum) * dt * same_end
        cfac_ref[b] = jnp.exp2(cum) * (row_id == before).astype(F32)
        ecarry_ref[:, cut] = 0.5 * jnp.exp2(base + cum) * (row_id == entered).astype(F32)
        ends_ref[b] = jnp.exp2(last) * (end == before).astype(F32)
        lower_ref[b] = cum - jnp.log2(dt)
        for g in range(groups):
            cols_ref[b * groups + g, :, 0:repeat] = jnp.transpose(cum[g * repeat : (g + 1) * repeat])
        base = base + last
    leaving = id_of(starts, first + rows - 1)
    whole = jnp.exp2(base) * (leaving == entered).astype(F32)
    for g in range(groups):
        total_d[g] = expand(whole[g * repeat : (g + 1) * repeat], e_ref)[0:8]


def states_of(
    g, b, xbuf, bbuf, hwx_ref, hwbc_ref, shift_ref, tailw_ref, ends_ref, e_ref,
    xc, bpart, c_ref, entering, state,
):
    repeat = e_ref.shape[0] // 2
    wide = e_ref.shape[1]
    low = pl.multiple_of(b * BLOCK, BLOCK)
    rows, tall = pl.ds(low, BLOCK), pl.ds(low, TAIL + BLOCK)
    heads = pl.ds(pl.multiple_of(g * repeat, repeat), repeat)
    shared = {}

    def pairs_begin():
        shared["shift"] = shift_ref[b]
        shared["own"] = bbuf[g, tall, :]
        shared["past"] = mm(shared["shift"], shared["own"])
        shared["tail"] = jnp.transpose(halves(tailw_ref[b, heads, :]).astype(F32)).astype(BF16)

    def pairs_work():
        halfw = [hwbc_ref[g, k : k + 1, :] for k in range(5)]
        bc = jnp.concatenate([piece for _, piece in conv_pieces(shared["past"], shared["own"], halfw)], axis=0)
        shared["turned"] = jnp.transpose(bc[:, 0:STATE]).astype(BF16)
        bpart[g, rows, :] = bc[:, 0:STATE].astype(BF16)
        c_ref[g, rows, :] = bc[:, STATE:].astype(BF16)

    def pairs_end():
        pass

    def unit(j):
        cols = slice(j, j + CHUNK)
        mine = {}

        def begin():
            mine["own"] = xbuf[g, tall, cols]
            mine["past"] = mm(shared["shift"], mine["own"])
            mine["spread"] = mm(shared["tail"], e_ref[:, cols])
            mine["decay"] = expand(ends_ref[b, heads, 0:8], e_ref.at[:, cols])

        def work():
            halfw = [hwx_ref[g, k : k + 1, cols] for k in range(5)]
            kept, scaled = [], []
            for cut, piece in conv_pieces(mine["past"], mine["own"], halfw):
                piece = piece.astype(BF16)
                kept.append(piece)
                scaled.append((piece.astype(F32) * mine["spread"][cut]).astype(BF16))
            mine["update"] = mm(shared["turned"], jnp.concatenate(scaled, axis=0))
            xc[g, rows, cols] = jnp.concatenate(kept, axis=0)

        def end():
            old = state[g, :, cols]
            entering[g, b, :, cols] = old.astype(BF16)
            state[g, :, cols] = mine["decay"][0:1] * old + mine["update"]

        return begin, work, end

    return [(pairs_begin, pairs_work, pairs_end)] + [unit(j) for j in range(0, wide, CHUNK)]


def within_of(g, b, xc, bpart, c_ref, entering, mask_ref, cfac_ref, lower_ref, cols_ref, skip_row, e_ref, yv):
    groups = xc.shape[0]
    repeat = e_ref.shape[0] // 2
    wide = e_ref.shape[1]
    rows = pl.ds(pl.multiple_of(b * BLOCK, BLOCK), BLOCK)
    heads = pl.ds(pl.multiple_of(g * repeat, repeat), repeat)
    b_part, c_part = bpart[g, rows, :], c_ref[g, rows, :]
    scores = mm(c_part, b_part, ((1,), (1,))) * mask_ref[b]
    carry = jnp.transpose(halves(cfac_ref[b, heads, :]).astype(F32)).astype(BF16)
    columns = cols_ref[b * groups + g]
    lower = lower_ref[b, heads, :]
    left = lax.broadcasted_iota(jnp.int32, (BLOCK, LANES), 1) < HEAD_DIM
    for j in range(0, wide, CHUNK):
        cols = slice(j, j + CHUNK)
        carried = mm(c_part, entering[g, b, :, cols]) * mm(carry, e_ref[:, cols])
        for k in range(0, CHUNK, LANES):
            sl = slice(j + k, j + k + LANES)
            parts = []
            for h in ((j + k) // HEAD_DIM, (j + k) // HEAD_DIM + 1):
                spread = jnp.minimum(columns[:, h : h + 1] - lower[h : h + 1, :], 80.0)
                parts.append((scores * jnp.exp2(spread)).astype(BF16))
            value = xc[g, rows, sl]
            none = jnp.zeros_like(value)
            pair = jnp.concatenate([jnp.where(left, value, none), jnp.where(left, none, value)], axis=0)
            y = mm(jnp.concatenate(parts, axis=1), pair)
            skip = skip_row[0:1, pl.ds(pl.multiple_of(g * wide + j + k, LANES), LANES)]
            yv[g, rows, sl] = (0.5 * (y + carried[:, k : k + LANES] + skip * value.astype(F32))).astype(BF16)


def pack_d(d):
    hi = d.astype(BF16).astype(F32)
    return jnp.concatenate([hi, d - hi], axis=0).astype(BF16)


def unpack_d(packed):
    both = packed.astype(F32)
    return both[0:8] + both[8:16]


class Exchange:
    def __init__(self, state, total_d, hin, bufs, sems):
        self.state, self.total_d, self.hin = state, total_d, hin
        (self.give1, self.take1, self.give2, self.take2, self.zgive, self.ztake, self.back2, self.home2,
         self.back1, self.home1, self.half_s, self.half_d, self.e_s, self.e_d, self.p_s, self.p_d) = bufs
        self.sem1, self.sem2, self.semz, self.sem4, self.sem5 = sems
        peers = lax.axis_size("seq")
        me = lax.axis_index("seq")
        self.me, self.peers = me, peers
        self.core, self.pair, self.link, self.links = lax.rem(me, 2), lax.rem(me // 2, 2), me // 4, peers // 4
        self.low1, self.low2 = self.core == 0, self.pair == 0
        self.near, self.far = me + 1 - 2 * self.core, me + 2 - 4 * self.pair
        self.half = state.shape[2] // 2
        self.quarter = self.half // 2
        self.rounds = max(1, (self.links - 1).bit_length())
        self.count = 6 + self.rounds

    def copy(self, src, dst, sems, peer):
        return pltpu.make_async_remote_copy(
            src_ref=src, dst_ref=dst, send_sem=sems.at[0], recv_sem=sems.at[1],
            device_id={"seq": peer}, device_id_type=MESH,
        )

    def copy1(self, g):
        return self.copy(self.give1.at[g], self.take1.at[g], self.sem1.at[g], self.near)

    def copy2(self, g):
        return self.copy(self.give2.at[g], self.take2.at[g], self.sem2.at[g], self.far)

    def copyz(self, r, g):
        return self.copy(self.zgive.at[r, g], self.ztake.at[r, g], self.semz.at[r, g], self.me + (4 << r))

    def copy4(self, g):
        return self.copy(self.back2.at[g], self.home2.at[g], self.sem4.at[g], self.far)

    def copy5(self, g):
        return self.copy(self.back1.at[g], self.home1.at[g], self.sem5.at[g], self.near)

    def greet(self):
        me, link = self.me, self.link
        found = [(None, self.near), (None, self.far), (me >= 1, me - 1), (me + 1 < self.peers, me + 1)]
        for r in range(self.rounds):
            found += [(link >= 1 << r, me - (4 << r)), (link + (1 << r) < self.links, me + (4 << r))]
        barrier = pltpu.get_barrier_semaphore()
        expected = jnp.int32(0)
        for known, peer in found:
            if known is None:
                pl.semaphore_signal(barrier, inc=1, device_id={"seq": peer}, device_id_type=MESH)
                expected = expected + 1
            else:
                expected = expected + known.astype(jnp.int32)

                @pl.when(known)
                def _():
                    pl.semaphore_signal(barrier, inc=1, device_id={"seq": peer}, device_id_type=MESH)

        pl.semaphore_wait(barrier, expected)

    def half_lanes(self, which):
        return pl.ds(pl.multiple_of(which * self.half, LANES), self.half)

    def lanes(self, q):
        return pl.ds(pl.multiple_of(self.core * self.half + q * self.quarter, LANES), self.quarter)

    def inner(self, q):
        return pl.ds(pl.multiple_of(q * self.quarter, LANES), self.quarter)

    def stage(self, k, g):
        if k == 0:
            self.begin(g)
        elif k == 1:
            self.cores(g)
        elif k == 2:
            self.chips(g)
        elif k < 3 + self.rounds:
            self.along(k - 3, g)
        elif k == 3 + self.rounds:
            self.enter(g)
        elif k == 4 + self.rounds:
            self.share(g)
        else:
            self.finish(g)

    def begin(self, g):
        other = self.half_lanes(1 - self.core)
        self.give1[g, 0:STATE, :] = self.state[g, :, other].astype(BF16)
        self.give1[g, STATE:, :] = pack_d(self.total_d[g, :, other])
        self.copy1(g).start()

    def of_chip(self, g, q):
        mine, other = self.state[g, :, self.lanes(q)], self.take1[g, 0:STATE, self.inner(q)].astype(F32)
        d_mine, d_other = self.total_d[g, :, self.lanes(q)], unpack_d(self.take1[g, STATE:, self.inner(q)])
        late = jnp.where(self.low1, d_other, d_mine)[0:1]
        total = late * jnp.where(self.low1, mine, other) + jnp.where(self.low1, other, mine)
        return total, d_mine * d_other

    def cores(self, g):
        self.copy1(g).wait()
        total, d = self.of_chip(g, 1 - self.pair)
        self.give2[g, 0:STATE, :] = total.astype(BF16)
        self.give2[g, STATE:, :] = pack_d(d)
        self.copy2(g).start()
        total, d = self.of_chip(g, self.pair)
        self.half_s[g] = total
        self.half_d[g] = d

    def chips(self, g):
        self.copy2(g).wait()
        mine, other = self.half_s[g], self.take2[g, 0:STATE, :].astype(F32)
        d_mine, d_other = self.half_d[g], unpack_d(self.take2[g, STATE:, :])
        late = jnp.where(self.low2, d_other, d_mine)[0:1]
        self.p_s[g] = late * jnp.where(self.low2, mine, other) + jnp.where(self.low2, other, mine)
        self.p_d[g] = d_mine * d_other
        self.e_s[g] = jnp.zeros(self.e_s.shape[1:], F32)
        self.e_d[g] = jnp.ones(self.e_d.shape[1:], F32)
        self.pass_on(0, g)

    def pass_on(self, r, g):
        @pl.when(self.link + (1 << r) < self.links)
        def _():
            self.zgive[r, g, 0:STATE, :] = self.p_s[g].astype(BF16)
            self.zgive[r, g, STATE:, :] = pack_d(self.p_d[g])
            self.copyz(r, g).start()

    def along(self, r, g):
        @pl.when(self.link >= 1 << r)
        def _():
            self.copyz(r, g).wait_recv()
            got, d = self.ztake[r, g, 0:STATE, :].astype(F32), unpack_d(self.ztake[r, g, STATE:, :])
            self.e_s[g] = self.e_d[g, 0:1, :] * got + self.e_s[g]
            self.e_d[g] = self.e_d[g] * d
            if r + 1 < self.rounds:
                self.p_s[g] = self.p_d[g, 0:1, :] * got + self.p_s[g]
                self.p_d[g] = self.p_d[g] * d

        if r + 1 < self.rounds:
            self.pass_on(r + 1, g)

    def hand_over(self, g, q, into):
        mine, other = self.state[g, :, self.lanes(q)], self.take1[g, 0:STATE, self.inner(q)].astype(F32)
        d_mine, d_other = self.total_d[g, :, self.lanes(q)], unpack_d(self.take1[g, STATE:, self.inner(q)])
        early = jnp.where(self.low1, d_mine, d_other)[0:1]
        passed = early * into + jnp.where(self.low1, mine, other)
        self.hin[g, :, self.lanes(q)] = jnp.where(self.low1, into, passed).astype(BF16)
        self.back1[g, :, self.inner(q)] = jnp.where(self.low1, passed, into).astype(BF16)

    def enter(self, g):
        into = self.e_s[g]
        mine, other = self.half_s[g], self.take2[g, 0:STATE, :].astype(F32)
        d_mine, d_other = self.half_d[g], unpack_d(self.take2[g, STATE:, :])
        early = jnp.where(self.low2, d_mine, d_other)[0:1]
        passed = early * into + jnp.where(self.low2, mine, other)
        self.back2[g] = jnp.where(self.low2, passed, into).astype(BF16)
        self.copy4(g).start()
        self.hand_over(g, self.pair, jnp.where(self.low2, into, passed))

    def share(self, g):
        self.copy4(g).wait()
        self.hand_over(g, 1 - self.pair, self.home2[g].astype(F32))
        self.copy5(g).start()

    def finish(self, g):
        self.copy5(g).wait()
        self.hin[g, :, self.half_lanes(1 - self.core)] = self.home1[g]
        for r in range(self.rounds):

            @pl.when(self.link + (1 << r) < self.links)
            def _():
                self.copyz(r, g).wait_send()


def mixer_kernel(
    seg_ref, x_ref, bc_ref, dtp_ref, dtb_ref, dec_ref, skip_ref, wx_ref, bx_ref, wbc_ref, bbc_ref,
    y_ref, c_ref, hin_ref, ecarry_ref,
    xbuf, bbuf, xtail, btail, xc, bpart, entering, state, total_d, yv,
    shift_ref, mask_ref, tailw_ref, cfac_ref, ends_ref, lower_ref, cols_ref, skip_row, e_ref, hwx_ref, hwbc_ref,
    give1, take1, give2, take2, zgive, ztake, back2, home2, back1, home1,
    half_s, half_d, e_s, e_d, p_s, p_d,
    sem1, sem2, semz, sem4, sem5, semx, semb, semt, semy,
):
    groups, _, wide = xbuf.shape
    rows = x_ref.shape[0]
    blocks = rows // BLOCK
    step = 2 - blocks % 2
    turns = blocks // step
    exchange = Exchange(
        state, total_d, hin_ref,
        (give1, take1, give2, take2, zgive, ztake, back2, home2, back1, home1, half_s, half_d, e_s, e_d, p_s, p_d),
        (sem1, sem2, semz, sem4, sem5),
    )
    me, peers = exchange.me, exchange.peers

    def lanes_of(g, width):
        return pl.ds(pl.multiple_of(g * width, LANES), width)

    def load_x(g):
        return pltpu.make_async_copy(
            x_ref.at[:, lanes_of(g, wide)], xbuf.at[g, pl.ds(TAIL, rows), :], semx.at[g]
        )

    def load_b(g):
        return pltpu.make_async_copy(
            bc_ref.at[:, lanes_of(g, 2 * STATE)], bbuf.at[g, pl.ds(TAIL, rows), :], semb.at[g]
        )

    for g in range(groups):
        load_b(g).start()
        load_x(g).start()
    tails = [
        exchange.copy(x_ref.at[pl.ds(rows - TAIL, TAIL), :], xtail, semt.at[0], me + 1),
        exchange.copy(bc_ref.at[pl.ds(rows - TAIL, TAIL), :], btail, semt.at[1], me + 1),
    ]
    exchange.greet()

    @pl.when(me + 1 < peers)
    def _():
        for tail in tails:
            tail.start()

    prepare(
        seg_ref, dtp_ref, dtb_ref, dec_ref, skip_ref, wx_ref, bx_ref, wbc_ref, bbc_ref,
        ecarry_ref, shift_ref, mask_ref, tailw_ref, cfac_ref, ends_ref, lower_ref, cols_ref, skip_row, total_d, e_ref,
        hwx_ref, hwbc_ref,
    )
    state[...] = jnp.zeros(state.shape, F32)

    @pl.when(me == 0)
    def _():
        xtail[...] = jnp.zeros(xtail.shape, BF16)
        btail[...] = jnp.zeros(btail.shape, BF16)

    @pl.when(me > 0)
    def _():
        for tail in tails:
            tail.wait_recv()

    def stages(i, which):
        for k in which:
            n = i - (turns - 1) - SPACING * k

            @pl.when((n >= 0) & (lax.rem(n, turns) == 0) & (n < groups * turns))
            def _():
                exchange.stage(k, lax.div(n, turns))

    def first_part(i, carry):
        g, p = lax.div(i, turns), lax.rem(i, turns)

        @pl.when(p == 0)
        def _():
            load_b(g).wait()
            load_x(g).wait()
            xbuf[g, 0:TAIL, :] = xtail[:, lanes_of(g, wide)]
            bbuf[g, 0:TAIL, :] = btail[:, lanes_of(g, 2 * STATE)]

        units = []
        for b in range(step):
            units += states_of(
                g, step * p + b, xbuf, bbuf, hwx_ref, hwbc_ref, shift_ref, tailw_ref, ends_ref, e_ref,
                xc, bpart, c_ref, entering, state,
            )
        pipelined(units)
        stages(i, range(exchange.count))
        return carry

    def store(i):
        g, p = lax.div(i, turns), lax.rem(i, turns)
        part = pl.ds(pl.multiple_of(p * step * BLOCK, BLOCK), step * BLOCK)
        return pltpu.make_async_copy(
            yv.at[g, part, :], y_ref.at[part, pl.ds(pl.multiple_of(g * wide, LANES), wide)], semy.at[i]
        )

    def second_part(i, carry):
        g, p = lax.div(i, turns), lax.rem(i, turns)
        for b in range(step):
            within_of(
                g, step * p + b, xc, bpart, c_ref, entering,
                mask_ref, cfac_ref, lower_ref, cols_ref, skip_row, e_ref, yv,
            )
        store(i).start()
        stages(i + groups * turns, range(1, exchange.count))
        return carry

    lax.fori_loop(0, groups * turns, first_part, 0)
    lax.fori_loop(0, groups * turns, second_part, 0)
    for i in range(2 * groups * turns, (groups + 1) * turns + SPACING * exchange.count):
        for k in range(1, exchange.count):
            n = i - (turns - 1) - SPACING * k
            if n >= 0 and n % turns == 0 and n < groups * turns:
                exchange.stage(k, n // turns)
    for i in range(groups * turns):
        store(jnp.int32(i)).wait()

    @pl.when(me + 1 < peers)
    def _():
        for tail in tails:
            tail.wait_send()


def output_kernel(
    y_ref, c_ref, z_ref, hin_ref, ecarry_ref, gain_ref, out_ref, e_ref, ybuf, zbuf, obuf, gated, semy, semz, semo,
):
    groups, _, wide = hin_ref.shape
    rows = z_ref.shape[0]
    turns, part = ybuf.shape[1], ybuf.shape[2]
    repeat = e_ref.shape[0] // 2

    def window(ref, i):
        g, p = lax.div(i, turns), lax.rem(i, turns)
        return ref.at[pl.ds(pl.multiple_of(p * part, part), part), pl.ds(pl.multiple_of(g * wide, LANES), wide)]

    def slot(ref, i):
        return ref.at[lax.div(i, turns), lax.rem(i, turns)]

    def loads(i):
        return (
            pltpu.make_async_copy(window(z_ref, i), slot(zbuf, i), semz.at[i]),
            pltpu.make_async_copy(window(y_ref, i), slot(ybuf, i), semy.at[i]),
        )

    def store(i):
        return pltpu.make_async_copy(slot(obuf, i), window(out_ref, i), semo.at[i])

    for i in range(groups * turns):
        for load in loads(jnp.int32(i)):
            load.start()
    fill_spread(e_ref)

    def step(i, carry):
        g, p = lax.div(i, turns), lax.rem(i, turns)
        for load in loads(i):
            load.wait()
        heads = pl.ds(pl.multiple_of(g * repeat, repeat), repeat)
        for r in range(0, part, BLOCK):
            here = slice(r, r + BLOCK)
            tokens = pl.ds(pl.multiple_of(p * part + r, BLOCK), BLOCK)
            weights = jnp.transpose(halves(ecarry_ref[heads, tokens]).astype(F32)).astype(BF16)
            c_part = c_ref[g, tokens, :]
            squares = jnp.zeros((BLOCK, LANES), F32)
            for j in range(0, wide, CHUNK):
                cols = slice(j, j + CHUNK)
                carried = mm(c_part, hin_ref[g, :, cols]) * mm(weights, e_ref[:, cols])
                full = ybuf[g, p, here, cols].astype(F32) + carried
                z = zbuf[g, p, here, cols].astype(F32)
                scaled = full * z
                held = scaled + scaled * jnp.tanh(0.5 * z)
                gated[here, cols] = held
                for k in range(0, CHUNK, LANES):
                    squares = squares + held[:, k : k + LANES] * held[:, k : k + LANES]
            mean = jnp.sum(squares, axis=1, keepdims=True) * (1.0 / wide)
            scale = jnp.broadcast_to(lax.rsqrt(mean + 1e-05), (BLOCK, LANES))
            for j in range(0, wide, LANES):
                sl = slice(j, j + LANES)
                gain = gain_ref[0:1, pl.ds(pl.multiple_of(g * wide + j, LANES), LANES)]
                obuf[g, p, here, sl] = (gated[here, sl] * scale * gain).astype(BF16)
        store(i).start()
        return carry

    lax.fori_loop(0, groups * turns, step, 0)
    for i in range(groups * turns):
        store(jnp.int32(i)).wait()


def shards(
    x_proj, z_gate, bc_proj, dt_proj, dt_bias, decay_log, skip_gain,
    conv_x, bias_x, conv_bc, bias_bc, norm_gain, seg_lengths,
):
    rows, channels = x_proj.shape
    heads = dt_proj.shape[1]
    groups = bc_proj.shape[1]
    repeat = heads // groups
    wide = channels // groups
    blocks = rows // BLOCK
    step = 2 - blocks % 2
    turns = blocks // step
    links = lax.axis_size("seq") // 4
    rounds = max(1, (links - 1).bit_length())
    bc = bc_proj.reshape(rows, groups * 2 * STATE)
    vmem = pl.BlockSpec(memory_space=pltpu.VMEM)
    anywhere = pl.BlockSpec(memory_space=pl.ANY)
    half, quarter = wide // 2, wide // 4
    scratch = lambda kind, *shape: pltpu.VMEM(shape, kind)
    dma = lambda *shape: pltpu.SemaphoreType.DMA(shape)
    per_block = (blocks, heads, BLOCK)
    y, c, hin, ecarry = pl.pallas_call(
        mixer_kernel,
        in_specs=[pl.BlockSpec(memory_space=pltpu.SMEM), anywhere, anywhere] + [vmem] * 8,
        out_specs=[anywhere, vmem, vmem, vmem],
        out_shape=[
            jax.ShapeDtypeStruct((rows, channels), BF16),
            jax.ShapeDtypeStruct((groups, rows, STATE), BF16),
            jax.ShapeDtypeStruct((groups, STATE, wide), BF16),
            jax.ShapeDtypeStruct((heads, rows), F32),
        ],
        scratch_shapes=[
            scratch(BF16, groups, TAIL + rows, wide), scratch(BF16, groups, TAIL + rows, 2 * STATE),
            scratch(BF16, TAIL, channels), scratch(BF16, TAIL, groups * 2 * STATE),
            scratch(BF16, groups, rows, wide), scratch(BF16, groups, rows, STATE),
            scratch(BF16, groups, blocks, STATE, wide), scratch(F32, groups, STATE, wide), scratch(F32, groups, 8, wide),
            scratch(BF16, groups, rows, wide),
            scratch(BF16, blocks, 3 * BLOCK, TAIL + BLOCK), scratch(F32, blocks, BLOCK, BLOCK),
            scratch(F32, *per_block), scratch(F32, *per_block), scratch(F32, *per_block), scratch(F32, *per_block),
            scratch(F32, blocks * groups, BLOCK, LANES), scratch(F32, 8, channels), scratch(BF16, 2 * repeat, wide),
            scratch(F32, groups, 8, wide), scratch(F32, groups, 8, 2 * STATE),
            scratch(BF16, groups, STATE + 16, half), scratch(BF16, groups, STATE + 16, half),
            scratch(BF16, groups, STATE + 16, quarter), scratch(BF16, groups, STATE + 16, quarter),
            scratch(BF16, rounds, groups, STATE + 16, quarter), scratch(BF16, rounds, groups, STATE + 16, quarter),
            scratch(BF16, groups, STATE, quarter), scratch(BF16, groups, STATE, quarter),
            scratch(BF16, groups, STATE, half), scratch(BF16, groups, STATE, half),
            scratch(F32, groups, STATE, quarter), scratch(F32, groups, 8, quarter),
            scratch(F32, groups, STATE, quarter), scratch(F32, groups, 8, quarter),
            scratch(F32, groups, STATE, quarter), scratch(F32, groups, 8, quarter),
            dma(groups, 2), dma(groups, 2), dma(rounds, groups, 2), dma(groups, 2), dma(groups, 2),
            dma(groups), dma(groups), dma(2, 2), dma(groups * turns),
        ],
        compiler_params=pltpu.CompilerParams(
            collective_id=0, has_side_effects=True, vmem_limit_bytes=VMEM_LIMIT
        ),
        name="mixer",
    )(
        seg_lengths, x_proj, bc, dt_proj.T, dt_bias[None], decay_log[None], skip_gain[None],
        conv_x, bias_x[None], conv_bc, bias_bc,
    )

    tiles = (groups, turns, step * BLOCK, wide)
    return pl.pallas_call(
        output_kernel,
        in_specs=[anywhere, vmem, anywhere, vmem, vmem, vmem],
        out_specs=anywhere,
        out_shape=jax.ShapeDtypeStruct((rows, channels), BF16),
        scratch_shapes=[
            scratch(BF16, 2 * repeat, wide), scratch(BF16, *tiles), scratch(BF16, *tiles), scratch(BF16, *tiles),
            scratch(F32, step * BLOCK, wide), dma(groups * turns), dma(groups * turns), dma(groups * turns),
        ],
        compiler_params=pltpu.CompilerParams(vmem_limit_bytes=VMEM_LIMIT),
        name="outputs",
    )(y, c, z_gate, hin, ecarry, norm_gain[None])


def solution(mesh):
    return jax.shard_map(
        shards,
        mesh=mesh,
        in_specs=(
            P(("groups", "seq"), "head"),
            P(("groups", "seq"), "head"),
            P(("groups", "seq"), "head", None),
            P(("groups", "seq"), "head"),
            P("head"),
            P("head"),
            P("head"),
            P(None, "head"),
            P("head"),
            P(None, "head", None),
            P("head", None),
            P("head"),
            P("groups"),
        ),
        out_specs=P(("groups", "seq"), "head"),
        check_vma=False,
    )
```

```python
import functools

import jax
import jax.numpy as jnp
from jax import lax
from jax.experimental import pallas as pl
from jax.experimental.pallas import tpu as pltpu
from jax.sharding import PartitionSpec as P

HEAD_DIM = 64
STATE = 128
BLOCK = 128
LANES = 128
TAIL = 16
CHUNK = 256
PIECE = 16
FIRST_LIMIT = 40 << 20
SECOND_LIMIT = 32 << 20
LOG2E = 1.4426950408889634
MESH = pl.DeviceIdType.MESH
F32 = jnp.float32
BF16 = jnp.bfloat16


def silu_of_half(half):
    return half + half * jnp.tanh(half)


def mm(a, b, dims=((1,), (0,))):
    return lax.dot_general(a, b, (dims, ((), ())), preferred_element_type=F32)


def ids_of(starts, positions):
    found = jnp.full(positions.shape, -1, jnp.int32)
    for start in starts:
        found = jnp.where(positions >= start, start, found)
    return found


def id_of(starts, position):
    found = jnp.int32(-1)
    for start in starts:
        found = jnp.where(position >= start, start, found)
    return found


def column(row):
    n = row.shape[1]
    i = lax.broadcasted_iota(jnp.int32, (n, n), 0)
    j = lax.broadcasted_iota(jnp.int32, (n, n), 1)
    return jnp.sum(jnp.where(i == j, row, 0.0), axis=1, keepdims=True)


def fill_spread(e_ref):
    twice, wide = e_ref.shape
    row = lax.broadcasted_iota(jnp.int32, (twice, wide), 0)
    lane = lax.broadcasted_iota(jnp.int32, (twice, wide), 1)
    e_ref[...] = (lane // HEAD_DIM == row % (twice // 2)).astype(F32).astype(BF16)


def halves(value):
    hi = value.astype(BF16)
    lo = (value - hi.astype(F32)).astype(BF16)
    return jnp.concatenate([hi, lo], axis=0)


def expand(value, e_ref):
    return mm(halves(value), e_ref[...], ((0,), (0,)))


def shift_matrix(within):
    t = lax.broadcasted_iota(jnp.int32, (BLOCK, TAIL + BLOCK), 0)
    i = lax.broadcasted_iota(jnp.int32, (BLOCK, TAIL + BLOCK), 1)
    steps = [((i == t + (TAIL - 3 + k)) & (within >= 3 - k)).astype(F32) for k in range(3)]
    order = [steps[k][r : r + PIECE] for r in range(0, BLOCK, PIECE) for k in range(3)]
    return jnp.concatenate(order, axis=0).astype(BF16)


def conv_pieces(past, own, halfw):
    for r in range(0, BLOCK, PIECE):
        half = halfw[4] + halfw[3] * own[TAIL + r : TAIL + r + PIECE, :].astype(F32)
        for k in range(3):
            at = 3 * r + k * PIECE
            half = half + halfw[k] * past[at : at + PIECE]
        yield slice(r, r + PIECE), silu_of_half(half)


def pipelined(units):
    for u in range(len(units) + 2):
        for phase in range(3):
            if 0 <= u - phase < len(units):
                units[u - phase][phase]()


def prepare(
    seg_ref, dtp_ref, dtb_ref, dec_ref, skip_ref, wx_ref, bx_ref, wbc_ref, bbc_ref,
    ecarry_ref, shift_ref, mask_ref, tailw_ref, cfac_ref, ends_ref, lower_ref, cols_ref, skip_row, total_d, e_ref,
    hwx_ref, hwbc_ref,
):
    heads, rows = dtp_ref.shape
    groups = total_d.shape[0]
    repeat = heads // groups
    wide = e_ref.shape[1]
    fill_spread(e_ref)
    for g in range(groups):
        cols = slice(g * wide, (g + 1) * wide)
        for k in range(4):
            hwx_ref[g, k : k + 1, :] = 0.5 * wx_ref[k : k + 1, cols]
            hwbc_ref[g, k : k + 1, :] = 0.5 * wbc_ref[k, g : g + 1, :]
        hwx_ref[g, 4:5, :] = 0.5 * bx_ref[0:1, cols]
        hwbc_ref[g, 4:5, :] = 0.5 * bbc_ref[g : g + 1, :]
    skip = jnp.broadcast_to(column(skip_ref[...]), (heads, LANES))
    for g in range(groups):
        skip_row[:, g * wide : (g + 1) * wide] = expand(skip[g * repeat : (g + 1) * repeat], e_ref)[0:8]
    first = lax.axis_index("seq") * rows
    starts = [jnp.int32(0)]
    for j in range(seg_ref.shape[0] - 1):
        starts.append(starts[-1] + seg_ref[j])
    entered = id_of(starts, first - 1)
    bias = column(dtb_ref[...])
    rate = -LOG2E * column(jnp.exp(dec_ref[...]))
    s = lax.broadcasted_iota(jnp.int32, (BLOCK, BLOCK), 0)
    t = lax.broadcasted_iota(jnp.int32, (BLOCK, BLOCK), 1)
    upper = (s <= t).astype(F32).astype(BF16)
    base = jnp.zeros((heads, LANES), F32)
    for b in range(rows // BLOCK):
        cut = slice(b * BLOCK, (b + 1) * BLOCK)
        raw = dtp_ref[:, cut].astype(F32) + bias
        dt = jnp.maximum(raw, 0.0) + jnp.log1p(jnp.exp(-jnp.abs(raw)))
        rest = rate * dt
        parts = []
        for _ in range(3):
            parts.append(rest.astype(BF16))
            rest = rest - parts[-1].astype(F32)
        sums = mm(jnp.concatenate(parts, axis=0), upper)
        cum = sums[0:heads] + (sums[heads : 2 * heads] + sums[2 * heads : 3 * heads])
        at = first + b * BLOCK
        tall = at + s
        tall_id = ids_of(starts, tall)
        row_id = ids_of(starts, at + lax.broadcasted_iota(jnp.int32, (1, LANES), 1))
        before, end = id_of(starts, at - 1), id_of(starts, at + BLOCK - 1)
        same_end = (row_id == end).astype(F32)
        last = jnp.broadcast_to(cum[:, BLOCK - 1 : BLOCK], cum.shape)
        shift_ref[b] = shift_matrix((tall - tall_id)[:, 0:1])
        mask_ref[b] = ((t <= s) & (tall_id == row_id)).astype(F32)
        tailw_ref[b] = jnp.exp2(last - cum) * dt * same_end
        cfac_ref[b] = jnp.exp2(cum) * (row_id == before).astype(F32)
        ecarry_ref[:, cut] = 0.5 * jnp.exp2(base + cum) * (row_id == entered).astype(F32)
        ends_ref[b] = jnp.exp2(last) * (end == before).astype(F32)
        lower_ref[b] = cum - jnp.log2(dt)
        for g in range(groups):
            cols_ref[b * groups + g, :, 0:repeat] = jnp.transpose(cum[g * repeat : (g + 1) * repeat])
        base = base + last
    leaving = id_of(starts, first + rows - 1)
    whole = jnp.exp2(base) * (leaving == entered).astype(F32)
    for g in range(groups):
        total_d[g] = expand(whole[g * repeat : (g + 1) * repeat], e_ref)[0:8]


def states_of(
    g, b, xbuf, bbuf, hwx_ref, hwbc_ref, shift_ref, tailw_ref, ends_ref, e_ref,
    xc, bpart, c_ref, entering, state,
):
    repeat = e_ref.shape[0] // 2
    wide = e_ref.shape[1]
    low = pl.multiple_of(b * BLOCK, BLOCK)
    rows, tall = pl.ds(low, BLOCK), pl.ds(low, TAIL + BLOCK)
    heads = pl.ds(pl.multiple_of(g * repeat, repeat), repeat)
    shared = {}

    def pairs_begin():
        shared["shift"] = shift_ref[b]
        shared["own"] = bbuf[g, tall, :]
        shared["past"] = mm(shared["shift"], shared["own"])
        shared["tail"] = jnp.transpose(halves(tailw_ref[b, heads, :]).astype(F32)).astype(BF16)

    def pairs_work():
        halfw = [hwbc_ref[g, k : k + 1, :] for k in range(5)]
        bc = jnp.concatenate([piece for _, piece in conv_pieces(shared["past"], shared["own"], halfw)], axis=0)
        shared["turned"] = jnp.transpose(bc[:, 0:STATE]).astype(BF16)
        bpart[g, rows, :] = bc[:, 0:STATE].astype(BF16)
        c_ref[g, rows, :] = bc[:, STATE:].astype(BF16)

    def pairs_end():
        pass

    def unit(j):
        cols = slice(j, j + CHUNK)
        mine = {}

        def begin():
            mine["own"] = xbuf[g, tall, cols]
            mine["past"] = mm(shared["shift"], mine["own"])
            mine["spread"] = mm(shared["tail"], e_ref[:, cols])
            mine["decay"] = expand(ends_ref[b, heads, 0:8], e_ref.at[:, cols])

        def work():
            halfw = [hwx_ref[g, k : k + 1, cols] for k in range(5)]
            kept, scaled = [], []
            for cut, piece in conv_pieces(mine["past"], mine["own"], halfw):
                piece = piece.astype(BF16)
                kept.append(piece)
                scaled.append((piece.astype(F32) * mine["spread"][cut]).astype(BF16))
            mine["update"] = mm(shared["turned"], jnp.concatenate(scaled, axis=0))
            xc[g, rows, cols] = jnp.concatenate(kept, axis=0)

        def end():
            old = state[g, :, cols]
            entering[g, b, :, cols] = old.astype(BF16)
            state[g, :, cols] = mine["decay"][0:1] * old + mine["update"]

        return begin, work, end

    return [(pairs_begin, pairs_work, pairs_end)] + [unit(j) for j in range(0, wide, CHUNK)]


def within_of(g, b, xc, bpart, c_ref, entering, mask_ref, cfac_ref, lower_ref, cols_ref, skip_row, e_ref, mid):
    groups = xc.shape[0]
    repeat = e_ref.shape[0] // 2
    wide = e_ref.shape[1]
    rows = pl.ds(pl.multiple_of(b * BLOCK, BLOCK), BLOCK)
    heads = pl.ds(pl.multiple_of(g * repeat, repeat), repeat)
    b_part, c_part = bpart[g, rows, :], c_ref[g, rows, :]
    scores = mm(c_part, b_part, ((1,), (1,))) * mask_ref[b]
    carry = jnp.transpose(halves(cfac_ref[b, heads, :]).astype(F32)).astype(BF16)
    columns = cols_ref[b * groups + g]
    lower = lower_ref[b, heads, :]
    left = lax.broadcasted_iota(jnp.int32, (BLOCK, LANES), 1) < HEAD_DIM
    for j in range(0, wide, CHUNK):
        cols = slice(j, j + CHUNK)
        carried = mm(c_part, entering[g, b, :, cols]) * mm(carry, e_ref[:, cols])
        for k in range(0, CHUNK, LANES):
            sl = slice(j + k, j + k + LANES)
            parts = []
            for h in ((j + k) // HEAD_DIM, (j + k) // HEAD_DIM + 1):
                spread = jnp.minimum(columns[:, h : h + 1] - lower[h : h + 1, :], 80.0)
                parts.append((scores * jnp.exp2(spread)).astype(BF16))
            value = xc[g, rows, sl]
            none = jnp.zeros_like(value)
            pair = jnp.concatenate([jnp.where(left, value, none), jnp.where(left, none, value)], axis=0)
            y = mm(jnp.concatenate(parts, axis=1), pair)
            skip = skip_row[0:1, pl.ds(pl.multiple_of(g * wide + j + k, LANES), LANES)]
            mid[g, rows, sl] = (0.5 * (y + carried[:, k : k + LANES] + skip * value.astype(F32))).astype(BF16)


def stage_times(links):
    times = [0, 2, 5]
    for r in range(max(1, (links - 1).bit_length())):
        times.append(times[-1] + 4 + min(r, 1))
    return times + [times[-1] + 4, times[-1] + 6]


def early_groups(groups, turns, links):
    last = stage_times(links)[-1]
    return sum((g + 1) * turns - 1 + last < (2 * groups + g) * turns for g in range(groups - 1))


def pack_d(d):
    hi = d.astype(BF16).astype(F32)
    return jnp.concatenate([hi, d - hi], axis=0).astype(BF16)


def unpack_d(packed):
    both = packed.astype(F32)
    return both[0:8] + both[8:16]


class Exchange:
    def __init__(self, state, total_d, hin, bufs, sems):
        self.state, self.total_d, self.hin = state, total_d, hin
        (self.give1, self.take1, self.give2, self.take2, self.zgive, self.ztake, self.back2, self.home2,
         self.back1, self.home1, self.half_s, self.half_d, self.e_s, self.e_d, self.p_s, self.p_d) = bufs
        self.sem1, self.sem2, self.semz, self.sem4, self.sem5 = sems
        peers = lax.axis_size("seq")
        me = lax.axis_index("seq")
        self.me, self.peers = me, peers
        self.core, self.pair, self.link, self.links = lax.rem(me, 2), lax.rem(me // 2, 2), me // 4, peers // 4
        self.low1, self.low2 = self.core == 0, self.pair == 0
        self.near, self.far = me + 1 - 2 * self.core, me + 2 - 4 * self.pair
        self.half = state.shape[2] // 2
        self.quarter = self.half // 2
        self.rounds = max(1, (self.links - 1).bit_length())

    def copy(self, src, dst, sems, peer):
        return pltpu.make_async_remote_copy(
            src_ref=src, dst_ref=dst, send_sem=sems.at[0], recv_sem=sems.at[1],
            device_id={"seq": peer}, device_id_type=MESH,
        )

    def copy1(self, g):
        return self.copy(self.give1.at[g], self.take1.at[g], self.sem1.at[g], self.near)

    def copy2(self, g):
        return self.copy(self.give2.at[g], self.take2.at[g], self.sem2.at[g], self.far)

    def copyz(self, r, g):
        return self.copy(self.zgive.at[r, g], self.ztake.at[r, g], self.semz.at[r, g], self.me + (4 << r))

    def copy4(self, g):
        return self.copy(self.back2.at[g], self.home2.at[g], self.sem4.at[g], self.far)

    def copy5(self, g):
        return self.copy(self.back1.at[g], self.home1.at[g], self.sem5.at[g], self.near)

    def greet(self):
        me, link = self.me, self.link
        found = [(None, self.near), (None, self.far), (me >= 1, me - 1), (me + 1 < self.peers, me + 1)]
        for r in range(self.rounds):
            found += [(link >= 1 << r, me - (4 << r)), (link + (1 << r) < self.links, me + (4 << r))]
        barrier = pltpu.get_barrier_semaphore()
        expected = jnp.int32(0)
        for known, peer in found:
            if known is None:
                pl.semaphore_signal(barrier, inc=1, device_id={"seq": peer}, device_id_type=MESH)
                expected = expected + 1
            else:
                expected = expected + known.astype(jnp.int32)

                @pl.when(known)
                def _():
                    pl.semaphore_signal(barrier, inc=1, device_id={"seq": peer}, device_id_type=MESH)

        pl.semaphore_wait(barrier, expected)

    def half_lanes(self, which):
        return pl.ds(pl.multiple_of(which * self.half, LANES), self.half)

    def lanes(self, q):
        return pl.ds(pl.multiple_of(self.core * self.half + q * self.quarter, LANES), self.quarter)

    def inner(self, q):
        return pl.ds(pl.multiple_of(q * self.quarter, LANES), self.quarter)

    def stage(self, k, g):
        if k == 0:
            self.begin(g)
        elif k == 1:
            self.cores(g)
        elif k == 2:
            self.chips(g)
        elif k < 3 + self.rounds:
            self.along(k - 3, g)
            if k == 2 + self.rounds:
                self.enter(g)
        elif k == 3 + self.rounds:
            self.share(g)
        else:
            self.finish(g)

    def begin(self, g):
        other = self.half_lanes(1 - self.core)
        self.give1[g, 0:STATE, :] = self.state[g, :, other].astype(BF16)
        self.give1[g, STATE:, :] = pack_d(self.total_d[g, :, other])
        self.copy1(g).start()

    def of_chip(self, g, q):
        mine, other = self.state[g, :, self.lanes(q)], self.take1[g, 0:STATE, self.inner(q)].astype(F32)
        d_mine, d_other = self.total_d[g, :, self.lanes(q)], unpack_d(self.take1[g, STATE:, self.inner(q)])
        late = jnp.where(self.low1, d_other, d_mine)[0:1]
        total = late * jnp.where(self.low1, mine, other) + jnp.where(self.low1, other, mine)
        return total, d_mine * d_other

    def cores(self, g):
        self.copy1(g).wait()
        total, d = self.of_chip(g, 1 - self.pair)
        self.give2[g, 0:STATE, :] = total.astype(BF16)
        self.give2[g, STATE:, :] = pack_d(d)
        self.copy2(g).start()
        total, d = self.of_chip(g, self.pair)
        self.half_s[g] = total
        self.half_d[g] = d

    def chips(self, g):
        self.copy2(g).wait()
        mine, other = self.half_s[g], self.take2[g, 0:STATE, :].astype(F32)
        d_mine, d_other = self.half_d[g], unpack_d(self.take2[g, STATE:, :])
        late = jnp.where(self.low2, d_other, d_mine)[0:1]
        self.p_s[g] = late * jnp.where(self.low2, mine, other) + jnp.where(self.low2, other, mine)
        self.p_d[g] = d_mine * d_other
        self.e_s[g] = jnp.zeros(self.e_s.shape[1:], F32)
        self.e_d[g] = jnp.ones(self.e_d.shape[1:], F32)
        self.pass_on(0, g)

    def pass_on(self, r, g):
        @pl.when(self.link + (1 << r) < self.links)
        def _():
            self.zgive[r, g, 0:STATE, :] = self.p_s[g].astype(BF16)
            self.zgive[r, g, STATE:, :] = pack_d(self.p_d[g])
            self.copyz(r, g).start()

    def along(self, r, g):
        @pl.when(self.link >= 1 << r)
        def _():
            self.copyz(r, g).wait_recv()
            got, d = self.ztake[r, g, 0:STATE, :].astype(F32), unpack_d(self.ztake[r, g, STATE:, :])
            self.e_s[g] = self.e_d[g, 0:1, :] * got + self.e_s[g]
            self.e_d[g] = self.e_d[g] * d
            if r + 1 < self.rounds:
                self.p_s[g] = self.p_d[g, 0:1, :] * got + self.p_s[g]
                self.p_d[g] = self.p_d[g] * d

        if r + 1 < self.rounds:
            self.pass_on(r + 1, g)

    def hand_over(self, g, q, into):
        mine, other = self.state[g, :, self.lanes(q)], self.take1[g, 0:STATE, self.inner(q)].astype(F32)
        d_mine, d_other = self.total_d[g, :, self.lanes(q)], unpack_d(self.take1[g, STATE:, self.inner(q)])
        early = jnp.where(self.low1, d_mine, d_other)[0:1]
        passed = early * into + jnp.where(self.low1, mine, other)
        self.hin[g, :, self.lanes(q)] = jnp.where(self.low1, into, passed).astype(BF16)
        self.back1[g, :, self.inner(q)] = jnp.where(self.low1, passed, into).astype(BF16)

    def enter(self, g):
        into = self.e_s[g]
        mine, other = self.half_s[g], self.take2[g, 0:STATE, :].astype(F32)
        d_mine, d_other = self.half_d[g], unpack_d(self.take2[g, STATE:, :])
        early = jnp.where(self.low2, d_mine, d_other)[0:1]
        passed = early * into + jnp.where(self.low2, mine, other)
        self.back2[g] = jnp.where(self.low2, passed, into).astype(BF16)
        self.copy4(g).start()
        self.hand_over(g, self.pair, jnp.where(self.low2, into, passed))

    def share(self, g):
        self.copy4(g).wait()
        self.hand_over(g, 1 - self.pair, self.home2[g].astype(F32))
        self.copy5(g).start()

    def finish(self, g):
        self.copy5(g).wait()
        self.hin[g, :, self.half_lanes(1 - self.core)] = self.home1[g]
        for r in range(self.rounds):

            @pl.when(self.link + (1 << r) < self.links)
            def _():
                self.copyz(r, g).wait_send()


def mixer_kernel(
    seg_ref, x_ref, bc_ref, z_ref, dtp_ref, dtb_ref, dec_ref, skip_ref, wx_ref, bx_ref, wbc_ref, bbc_ref, gain_ref,
    mid, zlate, c_ref, hin_ref, ecarry_ref,
    xbuf, bbuf, xtail, btail, xc, bpart, entering, state, total_d, held,
    shift_ref, mask_ref, tailw_ref, cfac_ref, ends_ref, lower_ref, cols_ref, skip_row, e_ref, hwx_ref, hwbc_ref,
    give1, take1, give2, take2, zgive, ztake, back2, home2, back1, home1,
    half_s, half_d, e_s, e_d, p_s, p_d,
    sem1, sem2, semz, sem4, sem5, semx, semb, semt, semg,
):
    groups, _, wide = xbuf.shape
    rows = x_ref.shape[0]
    blocks = rows // BLOCK
    step = 2 - blocks % 2
    turns = blocks // step
    repeat = e_ref.shape[0] // 2
    late = zlate.shape[0]
    early = groups - late
    exchange = Exchange(
        state, total_d, hin_ref,
        (give1, take1, give2, take2, zgive, ztake, back2, home2, back1, home1, half_s, half_d, e_s, e_d, p_s, p_d),
        (sem1, sem2, semz, sem4, sem5),
    )
    me, peers = exchange.me, exchange.peers
    times = stage_times(exchange.links)

    def lanes_of(g, width):
        return pl.ds(pl.multiple_of(g * width, LANES), width)

    def load_x(g):
        return pltpu.make_async_copy(
            x_ref.at[:, lanes_of(g, wide)], xbuf.at[g, pl.ds(TAIL, rows), :], semx.at[g]
        )

    def load_b(g):
        return pltpu.make_async_copy(
            bc_ref.at[:, lanes_of(g, 2 * STATE)], bbuf.at[g, pl.ds(TAIL, rows), :], semb.at[g]
        )

    def load_z(g):
        where = zlate.at[g - early] if g >= early else xbuf.at[g, pl.ds(TAIL, rows), :]
        return pltpu.make_async_copy(z_ref.at[:, lanes_of(g, wide)], where, semg.at[g])

    load_b(0).start()
    load_x(0).start()
    tails = [
        exchange.copy(x_ref.at[pl.ds(rows - TAIL, TAIL), :], xtail, semt.at[0], me + 1),
        exchange.copy(bc_ref.at[pl.ds(rows - TAIL, TAIL), :], btail, semt.at[1], me + 1),
    ]
    exchange.greet()

    @pl.when(me + 1 < peers)
    def _():
        for tail in tails:
            tail.start()

    for g in range(early, groups):
        load_z(g).start()
    prepare(
        seg_ref, dtp_ref, dtb_ref, dec_ref, skip_ref, wx_ref, bx_ref, wbc_ref, bbc_ref,
        ecarry_ref, shift_ref, mask_ref, tailw_ref, cfac_ref, ends_ref, lower_ref, cols_ref, skip_row, total_d, e_ref,
        hwx_ref, hwbc_ref,
    )

    @pl.when(me == 0)
    def _():
        xtail[...] = jnp.zeros(xtail.shape, BF16)
        btail[...] = jnp.zeros(btail.shape, BF16)

    @pl.when(me > 0)
    def _():
        for tail in tails:
            tail.wait_recv()

    def stages(i, which):
        for k in which:
            n = i - (turns - 1) - times[k]

            @pl.when((n >= 0) & (lax.rem(n, turns) == 0) & (n < groups * turns))
            def _():
                exchange.stage(k, lax.div(n, turns))

    def first_part(i, carry):
        g, p = lax.div(i, turns), lax.rem(i, turns)

        @pl.when(p == 0)
        def _():
            @pl.when(g + 1 < groups)
            def _():
                load_b(g + 1).start()
                load_x(g + 1).start()

            state[g] = jnp.zeros(state.shape[1:], F32)
            load_b(g).wait()
            load_x(g).wait()
            xbuf[g, 0:TAIL, :] = xtail[:, lanes_of(g, wide)]
            bbuf[g, 0:TAIL, :] = btail[:, lanes_of(g, 2 * STATE)]

        units = []
        for b in range(step):
            units += states_of(
                g, step * p + b, xbuf, bbuf, hwx_ref, hwbc_ref, shift_ref, tailw_ref, ends_ref, e_ref,
                xc, bpart, c_ref, entering, state,
            )
        pipelined(units)
        stages(i, range(len(times)))
        return carry

    def second_part(i, carry):
        g, p = lax.div(i, turns), lax.rem(i, turns)
        for b in range(step):
            within_of(
                g, step * p + b, xc, bpart, c_ref, entering,
                mask_ref, cfac_ref, lower_ref, cols_ref, skip_row, e_ref, mid,
            )
        stages(i + groups * turns, range(1, len(times)))
        return carry

    def third_part(i, carry):
        g, p = lax.div(i, turns), lax.rem(i, turns)
        heads = pl.ds(pl.multiple_of(g * repeat, repeat), repeat)
        for b in range(step):
            low = (step * p + b) * BLOCK
            tokens = pl.ds(pl.multiple_of(low, BLOCK), BLOCK)
            gate(
                mid.at[g, tokens, :], xbuf.at[g, pl.ds(pl.multiple_of(low + TAIL, TAIL), BLOCK), :],
                c_ref[g, tokens, :], hin_ref.at[g], ecarry_ref[heads, tokens], gain_ref.at[:, lanes_of(g, wide)],
                e_ref, held.at[b * BLOCK : (b + 1) * BLOCK], mid.at[g, tokens, :],
            )
        stages(i + 2 * groups * turns, range(1, len(times)))
        return carry

    lax.fori_loop(0, groups * turns, first_part, 0)
    for g in range(early):
        load_z(g).start()
    lax.fori_loop(0, groups * turns, second_part, 0)
    for g in range(early):
        load_z(g).wait()
    if early:
        lax.fori_loop(0, early * turns, third_part, 0)
    for i in range((2 * groups + early) * turns, groups * turns + times[-1]):
        for k in range(1, len(times)):
            n = i - (turns - 1) - times[k]
            if n >= 0 and n % turns == 0 and n < groups * turns:
                exchange.stage(k, n // turns)
    for g in range(early, groups):
        load_z(g).wait()

    @pl.when(me + 1 < peers)
    def _():
        for tail in tails:
            tail.wait_send()


def gate(y_ref, z_ref, c_part, hin_ref, weights, gain_ref, e_ref, held_ref, out_ref):
    wide = y_ref.shape[1]
    turned = jnp.transpose(halves(weights).astype(F32)).astype(BF16)
    squares = jnp.zeros((BLOCK, LANES), F32)
    for j in range(0, wide, CHUNK):
        cols = slice(j, j + CHUNK)
        carried = mm(c_part, hin_ref[:, cols]) * mm(turned, e_ref[:, cols])
        for r in range(0, BLOCK, PIECE):
            here = slice(r, r + PIECE)
            full = y_ref[here, cols].astype(F32) + carried[here]
            z = z_ref[here, cols]
            scaled = full * z.astype(F32)
            held_ref[here, cols] = scaled + scaled * jnp.tanh((z * BF16(0.5)).astype(F32))
        for k in range(0, CHUNK, LANES):
            held = held_ref[:, j + k : j + k + LANES]
            squares = squares + held * held
    mean = jnp.sum(squares, axis=1, keepdims=True) * (1.0 / wide)
    scale = jnp.broadcast_to(lax.rsqrt(mean + 1e-05), (BLOCK, LANES))
    for j in range(0, wide, LANES):
        sl = slice(j, j + LANES)
        out_ref[:, sl] = (held_ref[:, sl] * scale * gain_ref[0:1, sl]).astype(BF16)


def output_kernel(
    mid_ref, z_ref, c_ref, hin_ref, ecarry_ref, gain_ref, out_ref, e_ref, obuf, held, semo, semd,
):
    groups, rows, wide = mid_ref.shape
    late, turns, part = obuf.shape[0:3]
    early = groups - late
    repeat = e_ref.shape[0] // 2

    def done(g):
        return pltpu.make_async_copy(mid_ref.at[g], out_ref.at[:, g * wide : (g + 1) * wide], semd.at[g])

    def store(i):
        l, p = lax.div(i, turns), lax.rem(i, turns)
        lanes = pl.ds(pl.multiple_of((early + l) * wide, LANES), wide)
        return pltpu.make_async_copy(
            obuf.at[l, p], out_ref.at[pl.ds(pl.multiple_of(p * part, part), part), lanes], semo.at[i]
        )

    for g in range(early):
        done(g).start()
    fill_spread(e_ref)

    def step(i, carry):
        l, p = lax.div(i, turns), lax.rem(i, turns)
        g = early + l
        heads = pl.ds(pl.multiple_of(g * repeat, repeat), repeat)
        for r in range(0, part, BLOCK):
            tokens = pl.ds(pl.multiple_of(p * part + r, BLOCK), BLOCK)
            gate(
                mid_ref.at[g, tokens, :], z_ref.at[l, tokens, :], c_ref[g, tokens, :], hin_ref.at[g],
                ecarry_ref[heads, tokens], gain_ref.at[:, pl.ds(pl.multiple_of(g * wide, LANES), wide)],
                e_ref, held.at[r : r + BLOCK], obuf.at[l, p, r : r + BLOCK, :],
            )
        store(i).start()
        return carry

    lax.fori_loop(0, late * turns, step, 0)
    for i in range(late * turns):
        store(jnp.int32(i)).wait()
    for g in range(early):
        done(g).wait()


def shards(
    x_proj, z_gate, bc_proj, dt_proj, dt_bias, decay_log, skip_gain,
    conv_x, bias_x, conv_bc, bias_bc, norm_gain, seg_lengths,
):
    rows, channels = x_proj.shape
    heads = dt_proj.shape[1]
    groups = bc_proj.shape[1]
    repeat = heads // groups
    wide = channels // groups
    blocks = rows // BLOCK
    step = 2 - blocks % 2
    turns = blocks // step
    links = lax.axis_size("seq") // 4
    rounds = max(1, (links - 1).bit_length())
    bc = bc_proj.reshape(rows, groups * 2 * STATE)
    vmem = pl.BlockSpec(memory_space=pltpu.VMEM)
    anywhere = pl.BlockSpec(memory_space=pl.ANY)
    half, quarter = wide // 2, wide // 4
    scratch = lambda kind, *shape: pltpu.VMEM(shape, kind)
    dma = lambda *shape: pltpu.SemaphoreType.DMA(shape)
    per_block = (blocks, heads, BLOCK)
    early = early_groups(groups, turns, links)
    mid, zlate, c, hin, ecarry = pl.pallas_call(
        mixer_kernel,
        in_specs=[pl.BlockSpec(memory_space=pltpu.SMEM), anywhere, anywhere, anywhere] + [vmem] * 9,
        out_specs=[vmem] * 5,
        out_shape=[
            jax.ShapeDtypeStruct((groups, rows, wide), BF16),
            jax.ShapeDtypeStruct((groups - early, rows, wide), BF16),
            jax.ShapeDtypeStruct((groups, rows, STATE), BF16),
            jax.ShapeDtypeStruct((groups, STATE, wide), BF16),
            jax.ShapeDtypeStruct((heads, rows), F32),
        ],
        scratch_shapes=[
            scratch(BF16, groups, TAIL + rows, wide), scratch(BF16, groups, TAIL + rows, 2 * STATE),
            scratch(BF16, TAIL, channels), scratch(BF16, TAIL, groups * 2 * STATE),
            scratch(BF16, groups, rows, wide), scratch(BF16, groups, rows, STATE),
            scratch(BF16, groups, blocks, STATE, wide), scratch(F32, groups, STATE, wide), scratch(F32, groups, 8, wide),
            scratch(F32, step * BLOCK, wide),
            scratch(BF16, blocks, 3 * BLOCK, TAIL + BLOCK), scratch(F32, blocks, BLOCK, BLOCK),
            scratch(F32, *per_block), scratch(F32, *per_block), scratch(F32, *per_block), scratch(F32, *per_block),
            scratch(F32, blocks * groups, BLOCK, LANES), scratch(F32, 8, channels), scratch(BF16, 2 * repeat, wide),
            scratch(F32, groups, 8, wide), scratch(F32, groups, 8, 2 * STATE),
            scratch(BF16, groups, STATE + 16, half), scratch(BF16, groups, STATE + 16, half),
            scratch(BF16, groups, STATE + 16, quarter), scratch(BF16, groups, STATE + 16, quarter),
            scratch(BF16, rounds, groups, STATE + 16, quarter), scratch(BF16, rounds, groups, STATE + 16, quarter),
            scratch(BF16, groups, STATE, quarter), scratch(BF16, groups, STATE, quarter),
            scratch(BF16, groups, STATE, half), scratch(BF16, groups, STATE, half),
            scratch(F32, groups, STATE, quarter), scratch(F32, groups, 8, quarter),
            scratch(F32, groups, STATE, quarter), scratch(F32, groups, 8, quarter),
            scratch(F32, groups, STATE, quarter), scratch(F32, groups, 8, quarter),
            dma(groups, 2), dma(groups, 2), dma(rounds, groups, 2), dma(groups, 2), dma(groups, 2),
            dma(groups), dma(groups), dma(2, 2), dma(groups),
        ],
        compiler_params=pltpu.CompilerParams(
            collective_id=0, has_side_effects=True, vmem_limit_bytes=FIRST_LIMIT
        ),
        name="mixer",
    )(
        seg_lengths, x_proj, bc, z_gate, dt_proj.T, dt_bias[None], decay_log[None], skip_gain[None],
        conv_x, bias_x[None], conv_bc, bias_bc, norm_gain[None],
    )

    late = groups - early
    return pl.pallas_call(
        output_kernel,
        in_specs=[vmem] * 6,
        out_specs=anywhere,
        out_shape=jax.ShapeDtypeStruct((rows, channels), BF16),
        scratch_shapes=[
            scratch(BF16, 2 * repeat, wide), scratch(BF16, late, turns, step * BLOCK, wide),
            scratch(F32, step * BLOCK, wide), dma(late * turns), dma(groups),
        ],
        compiler_params=pltpu.CompilerParams(vmem_limit_bytes=SECOND_LIMIT),
        name="outputs",
    )(mid, zlate, c, hin, ecarry, norm_gain[None])


def solution(mesh):
    return jax.shard_map(
        shards,
        mesh=mesh,
        in_specs=(
            P(("groups", "seq"), "head"),
            P(("groups", "seq"), "head"),
            P(("groups", "seq"), "head", None),
            P(("groups", "seq"), "head"),
            P("head"),
            P("head"),
            P("head"),
            P(None, "head"),
            P("head"),
            P(None, "head", None),
            P("head", None),
            P("head"),
            P("groups"),
        ),
        out_specs=P(("groups", "seq"), "head"),
        check_vma=False,
    )
```

```python
import functools

import jax
import jax.numpy as jnp
from jax import lax
from jax.experimental import pallas as pl
from jax.experimental.pallas import tpu as pltpu
from jax.sharding import PartitionSpec as P

HEAD_DIM = 64
STATE = 128
BLOCK = 128
LANES = 128
TAIL = 16
CHUNK = 256
PIECE = 16
FIRST_LIMIT = 40 << 20
SECOND_LIMIT = 32 << 20
LOG2E = 1.4426950408889634
MESH = pl.DeviceIdType.MESH
F32 = jnp.float32
BF16 = jnp.bfloat16


def silu_of_half(half):
    return half + half * jnp.tanh(half)


def mm(a, b, dims=((1,), (0,))):
    return lax.dot_general(a, b, (dims, ((), ())), preferred_element_type=F32)


def ids_of(starts, positions):
    found = jnp.full(positions.shape, -1, jnp.int32)
    for start in starts:
        found = jnp.where(positions >= start, start, found)
    return found


def id_of(starts, position):
    found = jnp.int32(-1)
    for start in starts:
        found = jnp.where(position >= start, start, found)
    return found


def column(row):
    n = row.shape[1]
    i = lax.broadcasted_iota(jnp.int32, (n, n), 0)
    j = lax.broadcasted_iota(jnp.int32, (n, n), 1)
    return jnp.sum(jnp.where(i == j, row, 0.0), axis=1, keepdims=True)


def fill_spread(e_ref):
    twice, wide = e_ref.shape
    row = lax.broadcasted_iota(jnp.int32, (twice, wide), 0)
    lane = lax.broadcasted_iota(jnp.int32, (twice, wide), 1)
    e_ref[...] = (lane // HEAD_DIM == row % (twice // 2)).astype(F32).astype(BF16)


def halves(value):
    hi = value.astype(BF16)
    lo = (value - hi.astype(F32)).astype(BF16)
    return jnp.concatenate([hi, lo], axis=0)


def expand(value, e_ref):
    return mm(halves(value), e_ref[...], ((0,), (0,)))


def shift_matrix(within):
    t = lax.broadcasted_iota(jnp.int32, (BLOCK, TAIL + BLOCK), 0)
    i = lax.broadcasted_iota(jnp.int32, (BLOCK, TAIL + BLOCK), 1)
    steps = [((i == t + (TAIL - 3 + k)) & (within >= 3 - k)).astype(F32) for k in range(3)]
    order = [steps[k][r : r + PIECE] for r in range(0, BLOCK, PIECE) for k in range(3)]
    return jnp.concatenate(order, axis=0).astype(BF16)


def conv_pieces(past, own, halfw):
    for r in range(0, BLOCK, PIECE):
        half = halfw[4] + halfw[3] * own[TAIL + r : TAIL + r + PIECE, :].astype(F32)
        for k in range(3):
            at = 3 * r + k * PIECE
            half = half + halfw[k] * past[at : at + PIECE]
        yield slice(r, r + PIECE), silu_of_half(half)


def pipelined(units):
    for u in range(len(units) + 2):
        for phase in range(3):
            if 0 <= u - phase < len(units):
                units[u - phase][phase]()


def prepare(
    seg_ref, dtp_ref, dtb_ref, dec_ref, skip_ref, wx_ref, bx_ref, wbc_ref, bbc_ref,
    ecarry_ref, shift_ref, mask_ref, tailw_ref, cfac_ref, ends_ref, lower_ref, cols_ref, skip_row, total_d, e_ref,
    hwx_ref, hwbc_ref,
):
    heads, rows = dtp_ref.shape
    groups = total_d.shape[0]
    repeat = heads // groups
    wide = e_ref.shape[1]
    fill_spread(e_ref)
    for g in range(groups):
        cols = slice(g * wide, (g + 1) * wide)
        for k in range(4):
            hwx_ref[g, k : k + 1, :] = 0.5 * wx_ref[k : k + 1, cols]
            hwbc_ref[g, k : k + 1, :] = 0.5 * wbc_ref[k, g : g + 1, :]
        hwx_ref[g, 4:5, :] = 0.5 * bx_ref[0:1, cols]
        hwbc_ref[g, 4:5, :] = 0.5 * bbc_ref[g : g + 1, :]
    skip = jnp.broadcast_to(column(skip_ref[...]), (heads, LANES))
    for g in range(groups):
        skip_row[:, g * wide : (g + 1) * wide] = expand(skip[g * repeat : (g + 1) * repeat], e_ref)[0:8]
    first = lax.axis_index("seq") * rows
    starts = [jnp.int32(0)]
    for j in range(seg_ref.shape[0] - 1):
        starts.append(starts[-1] + seg_ref[j])
    entered = id_of(starts, first - 1)
    bias = column(dtb_ref[...])
    rate = -LOG2E * column(jnp.exp(dec_ref[...]))
    s = lax.broadcasted_iota(jnp.int32, (BLOCK, BLOCK), 0)
    t = lax.broadcasted_iota(jnp.int32, (BLOCK, BLOCK), 1)
    upper = (s <= t).astype(F32).astype(BF16)
    base = jnp.zeros((heads, LANES), F32)
    for b in range(rows // BLOCK):
        cut = slice(b * BLOCK, (b + 1) * BLOCK)
        raw = dtp_ref[:, cut].astype(F32) + bias
        dt = jnp.maximum(raw, 0.0) + jnp.log1p(jnp.exp(-jnp.abs(raw)))
        rest = rate * dt
        parts = []
        for _ in range(3):
            parts.append(rest.astype(BF16))
            rest = rest - parts[-1].astype(F32)
        sums = mm(jnp.concatenate(parts, axis=0), upper)
        cum = sums[0:heads] + (sums[heads : 2 * heads] + sums[2 * heads : 3 * heads])
        at = first + b * BLOCK
        tall = at + s
        tall_id = ids_of(starts, tall)
        row_id = ids_of(starts, at + lax.broadcasted_iota(jnp.int32, (1, LANES), 1))
        before, end = id_of(starts, at - 1), id_of(starts, at + BLOCK - 1)
        same_end = (row_id == end).astype(F32)
        last = jnp.broadcast_to(cum[:, BLOCK - 1 : BLOCK], cum.shape)
        shift_ref[b] = shift_matrix((tall - tall_id)[:, 0:1])
        mask_ref[b] = ((t <= s) & (tall_id == row_id)).astype(F32)
        tailw_ref[b] = jnp.exp2(last - cum) * dt * same_end
        cfac_ref[b] = jnp.exp2(cum) * (row_id == before).astype(F32)
        ecarry_ref[:, cut] = 0.5 * jnp.exp2(base + cum) * (row_id == entered).astype(F32)
        ends_ref[b] = jnp.exp2(last) * (end == before).astype(F32)
        lower_ref[b] = cum - jnp.log2(dt)
        for g in range(groups):
            cols_ref[b * groups + g, :, 0:repeat] = jnp.transpose(cum[g * repeat : (g + 1) * repeat])
        base = base + last
    leaving = id_of(starts, first + rows - 1)
    whole = jnp.exp2(base) * (leaving == entered).astype(F32)
    for g in range(groups):
        total_d[g] = expand(whole[g * repeat : (g + 1) * repeat], e_ref)[0:8]


def states_of(
    g, b, xbuf, bbuf, hwx_ref, hwbc_ref, shift_ref, tailw_ref, ends_ref, e_ref,
    xc, bpart, c_ref, entering, state,
):
    repeat = e_ref.shape[0] // 2
    wide = e_ref.shape[1]
    low = pl.multiple_of(b * BLOCK, BLOCK)
    rows, tall = pl.ds(low, BLOCK), pl.ds(low, TAIL + BLOCK)
    heads = pl.ds(pl.multiple_of(g * repeat, repeat), repeat)
    shared = {}

    def pairs_begin():
        shared["shift"] = shift_ref[b]
        shared["own"] = bbuf[g, tall, :]
        shared["past"] = mm(shared["shift"], shared["own"])
        shared["tail"] = jnp.transpose(halves(tailw_ref[b, heads, :]).astype(F32)).astype(BF16)

    def pairs_work():
        halfw = [hwbc_ref[g, k : k + 1, :] for k in range(5)]
        bc = jnp.concatenate([piece for _, piece in conv_pieces(shared["past"], shared["own"], halfw)], axis=0)
        shared["turned"] = jnp.transpose(bc[:, 0:STATE]).astype(BF16)
        bpart[g, rows, :] = bc[:, 0:STATE].astype(BF16)
        c_ref[g, rows, :] = bc[:, STATE:].astype(BF16)

    def pairs_end():
        pass

    def unit(j):
        cols = slice(j, j + CHUNK)
        mine = {}

        def begin():
            mine["own"] = xbuf[g, tall, cols]
            mine["past"] = mm(shared["shift"], mine["own"])
            mine["spread"] = mm(shared["tail"], e_ref[:, cols])
            mine["decay"] = expand(ends_ref[b, heads, 0:8], e_ref.at[:, cols])

        def work():
            halfw = [hwx_ref[g, k : k + 1, cols] for k in range(5)]
            kept, scaled = [], []
            for cut, piece in conv_pieces(mine["past"], mine["own"], halfw):
                piece = piece.astype(BF16)
                kept.append(piece)
                scaled.append((piece.astype(F32) * mine["spread"][cut]).astype(BF16))
            mine["update"] = mm(shared["turned"], jnp.concatenate(scaled, axis=0))
            xc[g, rows, cols] = jnp.concatenate(kept, axis=0)

        def end():
            old = state[g, :, cols]
            entering[g, b, :, cols] = old.astype(BF16)
            state[g, :, cols] = mine["decay"][0:1] * old + mine["update"]

        return begin, work, end

    return [(pairs_begin, pairs_work, pairs_end)] + [unit(j) for j in range(0, wide, CHUNK)]


def within_of(g, b, xc, bpart, c_ref, entering, mask_ref, cfac_ref, lower_ref, cols_ref, skip_row, e_ref, mid):
    groups = xc.shape[0]
    repeat = e_ref.shape[0] // 2
    wide = e_ref.shape[1]
    rows = pl.ds(pl.multiple_of(b * BLOCK, BLOCK), BLOCK)
    heads = pl.ds(pl.multiple_of(g * repeat, repeat), repeat)
    b_part, c_part = bpart[g, rows, :], c_ref[g, rows, :]
    scores = mm(c_part, b_part, ((1,), (1,))) * mask_ref[b]
    carry = jnp.transpose(halves(cfac_ref[b, heads, :]).astype(F32)).astype(BF16)
    columns = cols_ref[b * groups + g]
    lower = lower_ref[b, heads, :]
    left = lax.broadcasted_iota(jnp.int32, (BLOCK, LANES), 1) < HEAD_DIM
    for j in range(0, wide, CHUNK):
        cols = slice(j, j + CHUNK)
        carried = mm(c_part, entering[g, b, :, cols]) * mm(carry, e_ref[:, cols])
        for k in range(0, CHUNK, LANES):
            sl = slice(j + k, j + k + LANES)
            parts = []
            for h in ((j + k) // HEAD_DIM, (j + k) // HEAD_DIM + 1):
                spread = jnp.minimum(columns[:, h : h + 1] - lower[h : h + 1, :], 80.0)
                parts.append((scores * jnp.exp2(spread)).astype(BF16))
            value = xc[g, rows, sl]
            none = jnp.zeros_like(value)
            pair = jnp.concatenate([jnp.where(left, value, none), jnp.where(left, none, value)], axis=0)
            y = mm(jnp.concatenate(parts, axis=1), pair)
            skip = skip_row[0:1, pl.ds(pl.multiple_of(g * wide + j + k, LANES), LANES)]
            mid[g, rows, sl] = (0.5 * (y + carried[:, k : k + LANES] + skip * value.astype(F32))).astype(BF16)


def stage_times(links):
    times = [0, 2, 5]
    for r in range(max(1, (links - 1).bit_length())):
        times.append(times[-1] + 4 + min(r, 1))
    return times + [times[-1] + 4, times[-1] + 6]


def early_groups(groups, turns, links):
    last = stage_times(links)[-1]
    return sum((g + 1) * turns - 1 + last < (2 * groups + g) * turns for g in range(groups - 1))


def pack_d(d):
    hi = d.astype(BF16).astype(F32)
    return jnp.concatenate([hi, d - hi], axis=0).astype(BF16)


def unpack_d(packed):
    both = packed.astype(F32)
    return both[0:8] + both[8:16]


class Exchange:
    def __init__(self, state, total_d, hin, bufs, sems):
        self.state, self.total_d, self.hin = state, total_d, hin
        (self.give1, self.take1, self.give2, self.take2, self.zgive, self.ztake, self.back2, self.home2,
         self.back1, self.home1, self.half_s, self.half_d, self.e_s, self.e_d, self.p_s, self.p_d) = bufs
        self.sem1, self.sem2, self.semz, self.sem4, self.sem5 = sems
        peers = lax.axis_size("seq")
        me = lax.axis_index("seq")
        self.me, self.peers = me, peers
        self.core, self.pair, self.link, self.links = lax.rem(me, 2), lax.rem(me // 2, 2), me // 4, peers // 4
        self.low1, self.low2 = self.core == 0, self.pair == 0
        self.near, self.far = me + 1 - 2 * self.core, me + 2 - 4 * self.pair
        self.half = state.shape[2] // 2
        self.quarter = self.half // 2
        self.rounds = max(1, (self.links - 1).bit_length())

    def copy(self, src, dst, sems, peer):
        return pltpu.make_async_remote_copy(
            src_ref=src, dst_ref=dst, send_sem=sems.at[0], recv_sem=sems.at[1],
            device_id={"seq": peer}, device_id_type=MESH,
        )

    def copy1(self, g):
        return self.copy(self.give1.at[g], self.take1.at[g], self.sem1.at[g], self.near)

    def copy2(self, g):
        return self.copy(self.give2.at[g], self.take2.at[g], self.sem2.at[g], self.far)

    def copyz(self, r, g):
        return self.copy(self.zgive.at[r, g], self.ztake.at[r, g], self.semz.at[r, g], self.me + (4 << r))

    def copy4(self, g):
        return self.copy(self.back2.at[g], self.home2.at[g], self.sem4.at[g], self.far)

    def copy5(self, g):
        return self.copy(self.back1.at[g], self.home1.at[g], self.sem5.at[g], self.near)

    def greet(self):
        me, link = self.me, self.link
        found = [(None, self.near), (None, self.far), (me >= 1, me - 1), (me + 1 < self.peers, me + 1)]
        for r in range(self.rounds):
            found += [(link >= 1 << r, me - (4 << r)), (link + (1 << r) < self.links, me + (4 << r))]
        barrier = pltpu.get_barrier_semaphore()
        expected = jnp.int32(0)
        for known, peer in found:
            if known is None:
                pl.semaphore_signal(barrier, inc=1, device_id={"seq": peer}, device_id_type=MESH)
                expected = expected + 1
            else:
                expected = expected + known.astype(jnp.int32)

                @pl.when(known)
                def _():
                    pl.semaphore_signal(barrier, inc=1, device_id={"seq": peer}, device_id_type=MESH)

        pl.semaphore_wait(barrier, expected)

    def half_lanes(self, which):
        return pl.ds(pl.multiple_of(which * self.half, LANES), self.half)

    def lanes(self, q):
        return pl.ds(pl.multiple_of(self.core * self.half + q * self.quarter, LANES), self.quarter)

    def inner(self, q):
        return pl.ds(pl.multiple_of(q * self.quarter, LANES), self.quarter)

    def stage(self, k, g):
        if k == 0:
            self.begin(g)
        elif k == 1:
            self.cores(g)
        elif k == 2:
            self.chips(g)
        elif k < 3 + self.rounds:
            self.along(k - 3, g)
            if k == 2 + self.rounds:
                self.enter(g)
        elif k == 3 + self.rounds:
            self.share(g)
        else:
            self.finish(g)

    def begin(self, g):
        other = self.half_lanes(1 - self.core)
        self.give1[g, 0:STATE, :] = self.state[g, :, other].astype(BF16)
        self.give1[g, STATE:, :] = pack_d(self.total_d[g, :, other])
        self.copy1(g).start()

    def of_chip(self, g, q):
        mine, other = self.state[g, :, self.lanes(q)], self.take1[g, 0:STATE, self.inner(q)].astype(F32)
        d_mine, d_other = self.total_d[g, :, self.lanes(q)], unpack_d(self.take1[g, STATE:, self.inner(q)])
        late = jnp.where(self.low1, d_other, d_mine)[0:1]
        total = late * jnp.where(self.low1, mine, other) + jnp.where(self.low1, other, mine)
        return total, d_mine * d_other

    def cores(self, g):
        self.copy1(g).wait()
        total, d = self.of_chip(g, 1 - self.pair)
        self.give2[g, 0:STATE, :] = total.astype(BF16)
        self.give2[g, STATE:, :] = pack_d(d)
        self.copy2(g).start()
        total, d = self.of_chip(g, self.pair)
        self.half_s[g] = total
        self.half_d[g] = d

    def chips(self, g):
        self.copy2(g).wait()
        mine, other = self.half_s[g], self.take2[g, 0:STATE, :].astype(F32)
        d_mine, d_other = self.half_d[g], unpack_d(self.take2[g, STATE:, :])
        late = jnp.where(self.low2, d_other, d_mine)[0:1]
        self.p_s[g] = late * jnp.where(self.low2, mine, other) + jnp.where(self.low2, other, mine)
        self.p_d[g] = d_mine * d_other
        self.e_s[g] = jnp.zeros(self.e_s.shape[1:], F32)
        self.e_d[g] = jnp.ones(self.e_d.shape[1:], F32)
        self.pass_on(0, g)

    def pass_on(self, r, g):
        @pl.when(self.link + (1 << r) < self.links)
        def _():
            self.zgive[r, g, 0:STATE, :] = self.p_s[g].astype(BF16)
            self.zgive[r, g, STATE:, :] = pack_d(self.p_d[g])
            self.copyz(r, g).start()

    def along(self, r, g):
        @pl.when(self.link >= 1 << r)
        def _():
            self.copyz(r, g).wait_recv()
            got, d = self.ztake[r, g, 0:STATE, :].astype(F32), unpack_d(self.ztake[r, g, STATE:, :])
            self.e_s[g] = self.e_d[g, 0:1, :] * got + self.e_s[g]
            self.e_d[g] = self.e_d[g] * d
            if r + 1 < self.rounds:
                self.p_s[g] = self.p_d[g, 0:1, :] * got + self.p_s[g]
                self.p_d[g] = self.p_d[g] * d

        if r + 1 < self.rounds:
            self.pass_on(r + 1, g)

    def hand_over(self, g, q, into):
        mine, other = self.state[g, :, self.lanes(q)], self.take1[g, 0:STATE, self.inner(q)].astype(F32)
        d_mine, d_other = self.total_d[g, :, self.lanes(q)], unpack_d(self.take1[g, STATE:, self.inner(q)])
        early = jnp.where(self.low1, d_mine, d_other)[0:1]
        passed = early * into + jnp.where(self.low1, mine, other)
        self.hin[g, :, self.lanes(q)] = jnp.where(self.low1, into, passed).astype(BF16)
        self.back1[g, :, self.inner(q)] = jnp.where(self.low1, passed, into).astype(BF16)

    def enter(self, g):
        into = self.e_s[g]
        mine, other = self.half_s[g], self.take2[g, 0:STATE, :].astype(F32)
        d_mine, d_other = self.half_d[g], unpack_d(self.take2[g, STATE:, :])
        early = jnp.where(self.low2, d_mine, d_other)[0:1]
        passed = early * into + jnp.where(self.low2, mine, other)
        self.back2[g] = jnp.where(self.low2, passed, into).astype(BF16)
        self.copy4(g).start()
        self.hand_over(g, self.pair, jnp.where(self.low2, into, passed))

    def share(self, g):
        self.copy4(g).wait()
        self.hand_over(g, 1 - self.pair, self.home2[g].astype(F32))
        self.copy5(g).start()

    def finish(self, g):
        self.copy5(g).wait()
        self.hin[g, :, self.half_lanes(1 - self.core)] = self.home1[g]
        for r in range(self.rounds):

            @pl.when(self.link + (1 << r) < self.links)
            def _():
                self.copyz(r, g).wait_send()


def mixer_kernel(
    seg_in, x_ref, bc_ref, z_ref, dtp_in, dtb_in, dec_in, skip_in, wx_in, bx_in, wbc_in, bbc_in, gain_in,
    mid, zlate, c_ref, hin_ref, ecarry_ref, gain_ref,
    seg_ref, dtp_ref, dtb_ref, dec_ref, skip_ref, wx_ref, bx_ref, wbc_ref, bbc_ref,
    xbuf, bbuf, xtail, btail, xc, bpart, entering, state, total_d, held,
    shift_ref, mask_ref, tailw_ref, cfac_ref, ends_ref, lower_ref, cols_ref, skip_row, e_ref, hwx_ref, hwbc_ref,
    give1, take1, give2, take2, zgive, ztake, back2, home2, back1, home1,
    half_s, half_d, e_s, e_d, p_s, p_d,
    sem1, sem2, semz, sem4, sem5, semx, semb, semt, semg, semw,
):
    groups, _, wide = xbuf.shape
    rows = x_ref.shape[0]
    blocks = rows // BLOCK
    step = 2 - blocks % 2
    turns = blocks // step
    repeat = e_ref.shape[0] // 2
    late = zlate.shape[0]
    early = groups - late
    exchange = Exchange(
        state, total_d, hin_ref,
        (give1, take1, give2, take2, zgive, ztake, back2, home2, back1, home1, half_s, half_d, e_s, e_d, p_s, p_d),
        (sem1, sem2, semz, sem4, sem5),
    )
    me, peers = exchange.me, exchange.peers
    times = stage_times(exchange.links)

    def lanes_of(g, width):
        return pl.ds(pl.multiple_of(g * width, LANES), width)

    def load_x(g):
        return pltpu.make_async_copy(
            x_ref.at[:, lanes_of(g, wide)], xbuf.at[g, pl.ds(TAIL, rows), :], semx.at[g]
        )

    def load_b(g):
        return pltpu.make_async_copy(
            bc_ref.at[:, lanes_of(g, 2 * STATE)], bbuf.at[g, pl.ds(TAIL, rows), :], semb.at[g]
        )

    def load_z(g):
        where = zlate.at[g - early] if g >= early else xbuf.at[g, pl.ds(TAIL, rows), :]
        return pltpu.make_async_copy(z_ref.at[:, lanes_of(g, wide)], where, semg.at[g])

    small = [
        pltpu.make_async_copy(src, dst, semw.at[n])
        for n, (src, dst) in enumerate((
            (seg_in, seg_ref), (dtp_in, dtp_ref), (dtb_in, dtb_ref), (dec_in, dec_ref), (skip_in, skip_ref),
            (wx_in, wx_ref), (bx_in, bx_ref), (wbc_in, wbc_ref), (bbc_in, bbc_ref), (gain_in, gain_ref),
        ))
    ]
    for load in small:
        load.start()
    load_b(0).start()
    load_x(0).start()
    tails = [
        exchange.copy(x_ref.at[pl.ds(rows - TAIL, TAIL), :], xtail, semt.at[0], me + 1),
        exchange.copy(bc_ref.at[pl.ds(rows - TAIL, TAIL), :], btail, semt.at[1], me + 1),
    ]
    exchange.greet()

    @pl.when(me + 1 < peers)
    def _():
        for tail in tails:
            tail.start()

    for load in small:
        load.wait()
    prepare(
        seg_ref, dtp_ref, dtb_ref, dec_ref, skip_ref, wx_ref, bx_ref, wbc_ref, bbc_ref,
        ecarry_ref, shift_ref, mask_ref, tailw_ref, cfac_ref, ends_ref, lower_ref, cols_ref, skip_row, total_d, e_ref,
        hwx_ref, hwbc_ref,
    )

    @pl.when(me == 0)
    def _():
        xtail[...] = jnp.zeros(xtail.shape, BF16)
        btail[...] = jnp.zeros(btail.shape, BF16)

    @pl.when(me > 0)
    def _():
        for tail in tails:
            tail.wait_recv()

    def stages(i, which):
        for k in which:
            n = i - (turns - 1) - times[k]

            @pl.when((n >= 0) & (lax.rem(n, turns) == 0) & (n < groups * turns))
            def _():
                exchange.stage(k, lax.div(n, turns))

    def first_part(i, carry):
        g, p = lax.div(i, turns), lax.rem(i, turns)

        @pl.when(p == 0)
        def _():
            @pl.when(g + 1 < groups)
            def _():
                load_b(g + 1).start()
                load_x(g + 1).start()

            state[g] = jnp.zeros(state.shape[1:], F32)
            load_b(g).wait()
            load_x(g).wait()
            xbuf[g, 0:TAIL, :] = xtail[:, lanes_of(g, wide)]
            bbuf[g, 0:TAIL, :] = btail[:, lanes_of(g, 2 * STATE)]

        units = []
        for b in range(step):
            units += states_of(
                g, step * p + b, xbuf, bbuf, hwx_ref, hwbc_ref, shift_ref, tailw_ref, ends_ref, e_ref,
                xc, bpart, c_ref, entering, state,
            )
        pipelined(units)
        stages(i, range(len(times)))
        return carry

    def second_part(i, carry):
        g, p = lax.div(i, turns), lax.rem(i, turns)
        for b in range(step):
            within_of(
                g, step * p + b, xc, bpart, c_ref, entering,
                mask_ref, cfac_ref, lower_ref, cols_ref, skip_row, e_ref, mid,
            )
        stages(i + groups * turns, range(1, len(times)))
        return carry

    def third_part(i, carry):
        g, p = lax.div(i, turns), lax.rem(i, turns)
        heads = pl.ds(pl.multiple_of(g * repeat, repeat), repeat)
        for b in range(step):
            low = (step * p + b) * BLOCK
            tokens = pl.ds(pl.multiple_of(low, BLOCK), BLOCK)
            gate(
                mid.at[g, tokens, :], xbuf.at[g, pl.ds(pl.multiple_of(low + TAIL, TAIL), BLOCK), :],
                c_ref[g, tokens, :], hin_ref.at[g], ecarry_ref[heads, tokens], gain_ref.at[:, lanes_of(g, wide)],
                e_ref, held.at[b * BLOCK : (b + 1) * BLOCK], mid.at[g, tokens, :],
            )
        stages(i + 2 * groups * turns, range(1, len(times)))
        return carry

    lax.fori_loop(0, groups * turns, first_part, 0)
    for g in range(groups):
        load_z(g).start()
    lax.fori_loop(0, groups * turns, second_part, 0)
    for g in range(early):
        load_z(g).wait()
    if early:
        lax.fori_loop(0, early * turns, third_part, 0)
    for i in range((2 * groups + early) * turns, groups * turns + times[-1]):
        for k in range(1, len(times)):
            n = i - (turns - 1) - times[k]
            if n >= 0 and n % turns == 0 and n < groups * turns:
                exchange.stage(k, n // turns)
    for g in range(early, groups):
        load_z(g).wait()

    @pl.when(me + 1 < peers)
    def _():
        for tail in tails:
            tail.wait_send()


def gate(y_ref, z_ref, c_part, hin_ref, weights, gain_ref, e_ref, held_ref, out_ref):
    wide = y_ref.shape[1]
    turned = jnp.transpose(halves(weights).astype(F32)).astype(BF16)
    squares = jnp.zeros((BLOCK, LANES), F32)
    for j in range(0, wide, CHUNK):
        cols = slice(j, j + CHUNK)
        carried = mm(c_part, hin_ref[:, cols]) * mm(turned, e_ref[:, cols])
        for r in range(0, BLOCK, PIECE):
            here = slice(r, r + PIECE)
            full = y_ref[here, cols].astype(F32) + carried[here]
            z = z_ref[here, cols]
            scaled = full * z.astype(F32)
            held_ref[here, cols] = scaled + scaled * jnp.tanh((z * BF16(0.5)).astype(F32))
        for k in range(0, CHUNK, LANES):
            held = held_ref[:, j + k : j + k + LANES]
            squares = squares + held * held
    mean = jnp.sum(squares, axis=1, keepdims=True) * (1.0 / wide)
    scale = jnp.broadcast_to(lax.rsqrt(mean + 1e-05), (BLOCK, LANES))
    for j in range(0, wide, LANES):
        sl = slice(j, j + LANES)
        out_ref[:, sl] = (held_ref[:, sl] * scale * gain_ref[0:1, sl]).astype(BF16)


def output_kernel(
    mid_ref, z_ref, c_ref, hin_ref, ecarry_ref, gain_ref, out_ref, e_ref, obuf, held, semo, semd,
):
    groups, rows, wide = mid_ref.shape
    late, turns, part = obuf.shape[0:3]
    early = groups - late
    repeat = e_ref.shape[0] // 2

    def done(g):
        return pltpu.make_async_copy(mid_ref.at[g], out_ref.at[:, g * wide : (g + 1) * wide], semd.at[g])

    def store(i):
        l, p = lax.div(i, turns), lax.rem(i, turns)
        lanes = pl.ds(pl.multiple_of((early + l) * wide, LANES), wide)
        return pltpu.make_async_copy(
            obuf.at[l, p], out_ref.at[pl.ds(pl.multiple_of(p * part, part), part), lanes], semo.at[i]
        )

    for g in range(early):
        done(g).start()
    fill_spread(e_ref)

    def step(i, carry):
        l, p = lax.div(i, turns), lax.rem(i, turns)
        g = early + l
        heads = pl.ds(pl.multiple_of(g * repeat, repeat), repeat)
        for r in range(0, part, BLOCK):
            tokens = pl.ds(pl.multiple_of(p * part + r, BLOCK), BLOCK)
            gate(
                mid_ref.at[g, tokens, :], z_ref.at[l, tokens, :], c_ref[g, tokens, :], hin_ref.at[g],
                ecarry_ref[heads, tokens], gain_ref.at[:, pl.ds(pl.multiple_of(g * wide, LANES), wide)],
                e_ref, held.at[r : r + BLOCK], obuf.at[l, p, r : r + BLOCK, :],
            )
        store(i).start()
        return carry

    lax.fori_loop(0, late * turns, step, 0)
    for i in range(late * turns):
        store(jnp.int32(i)).wait()
    for g in range(early):
        done(g).wait()


def shards(
    x_proj, z_gate, bc_proj, dt_proj, dt_bias, decay_log, skip_gain,
    conv_x, bias_x, conv_bc, bias_bc, norm_gain, seg_lengths,
):
    rows, channels = x_proj.shape
    heads = dt_proj.shape[1]
    groups = bc_proj.shape[1]
    repeat = heads // groups
    wide = channels // groups
    blocks = rows // BLOCK
    step = 2 - blocks % 2
    turns = blocks // step
    links = lax.axis_size("seq") // 4
    rounds = max(1, (links - 1).bit_length())
    bc = bc_proj.reshape(rows, groups * 2 * STATE)
    vmem = pl.BlockSpec(memory_space=pltpu.VMEM)
    anywhere = pl.BlockSpec(memory_space=pl.ANY)
    pin = lambda array: pltpu.with_memory_space_constraint(array, pltpu.HBM)
    outside = pl.BlockSpec(memory_space=pltpu.HBM)
    half, quarter = wide // 2, wide // 4
    scratch = lambda kind, *shape: pltpu.VMEM(shape, kind)
    dma = lambda *shape: pltpu.SemaphoreType.DMA(shape)
    per_block = (blocks, heads, BLOCK)
    early = early_groups(groups, turns, links)
    mid, zlate, c, hin, ecarry, gain = pl.pallas_call(
        mixer_kernel,
        in_specs=[outside, anywhere, anywhere, anywhere] + [outside] * 9,
        out_specs=[vmem] * 6,
        out_shape=[
            jax.ShapeDtypeStruct((groups, rows, wide), BF16),
            jax.ShapeDtypeStruct((groups - early, rows, wide), BF16),
            jax.ShapeDtypeStruct((groups, rows, STATE), BF16),
            jax.ShapeDtypeStruct((groups, STATE, wide), BF16),
            jax.ShapeDtypeStruct((heads, rows), F32),
            jax.ShapeDtypeStruct((1, channels), F32),
        ],
        scratch_shapes=[
            pltpu.SMEM(seg_lengths.shape, jnp.int32), scratch(BF16, heads, rows),
            scratch(F32, 1, heads), scratch(F32, 1, heads), scratch(F32, 1, heads),
            scratch(F32, *conv_x.shape), scratch(F32, 1, channels), scratch(F32, *conv_bc.shape), scratch(F32, *bias_bc.shape),
            scratch(BF16, groups, TAIL + rows, wide), scratch(BF16, groups, TAIL + rows, 2 * STATE),
            scratch(BF16, TAIL, channels), scratch(BF16, TAIL, groups * 2 * STATE),
            scratch(BF16, groups, rows, wide), scratch(BF16, groups, rows, STATE),
            scratch(BF16, groups, blocks, STATE, wide), scratch(F32, groups, STATE, wide), scratch(F32, groups, 8, wide),
            scratch(F32, step * BLOCK, wide),
            scratch(BF16, blocks, 3 * BLOCK, TAIL + BLOCK), scratch(F32, blocks, BLOCK, BLOCK),
            scratch(F32, *per_block), scratch(F32, *per_block), scratch(F32, *per_block), scratch(F32, *per_block),
            scratch(F32, blocks * groups, BLOCK, LANES), scratch(F32, 8, channels), scratch(BF16, 2 * repeat, wide),
            scratch(F32, groups, 8, wide), scratch(F32, groups, 8, 2 * STATE),
            scratch(BF16, groups, STATE + 16, half), scratch(BF16, groups, STATE + 16, half),
            scratch(BF16, groups, STATE + 16, quarter), scratch(BF16, groups, STATE + 16, quarter),
            scratch(BF16, rounds, groups, STATE + 16, quarter), scratch(BF16, rounds, groups, STATE + 16, quarter),
            scratch(BF16, groups, STATE, quarter), scratch(BF16, groups, STATE, quarter),
            scratch(BF16, groups, STATE, half), scratch(BF16, groups, STATE, half),
            scratch(F32, groups, STATE, quarter), scratch(F32, groups, 8, quarter),
            scratch(F32, groups, STATE, quarter), scratch(F32, groups, 8, quarter),
            scratch(F32, groups, STATE, quarter), scratch(F32, groups, 8, quarter),
            dma(groups, 2), dma(groups, 2), dma(rounds, groups, 2), dma(groups, 2), dma(groups, 2),
            dma(groups), dma(groups), dma(2, 2), dma(groups), dma(10),
        ],
        compiler_params=pltpu.CompilerParams(
            collective_id=0, has_side_effects=True, vmem_limit_bytes=FIRST_LIMIT
        ),
        name="mixer",
    )(
        pin(seg_lengths), x_proj, bc, z_gate, pin(dt_proj.T), pin(dt_bias[None]), pin(decay_log[None]), pin(skip_gain[None]),
        pin(conv_x), pin(bias_x[None]), pin(conv_bc), pin(bias_bc), pin(norm_gain[None]),
    )

    late = groups - early
    return pl.pallas_call(
        output_kernel,
        in_specs=[vmem] * 6,
        out_specs=anywhere,
        out_shape=jax.ShapeDtypeStruct((rows, channels), BF16),
        scratch_shapes=[
            scratch(BF16, 2 * repeat, wide), scratch(BF16, late, turns, step * BLOCK, wide),
            scratch(F32, step * BLOCK, wide), dma(late * turns), dma(groups),
        ],
        compiler_params=pltpu.CompilerParams(vmem_limit_bytes=SECOND_LIMIT),
        name="outputs",
    )(mid, zlate, c, hin, ecarry, gain)


def solution(mesh):
    return jax.shard_map(
        shards,
        mesh=mesh,
        in_specs=(
            P(("groups", "seq"), "head"),
            P(("groups", "seq"), "head"),
            P(("groups", "seq"), "head", None),
            P(("groups", "seq"), "head"),
            P("head"),
            P("head"),
            P("head"),
            P(None, "head"),
            P("head"),
            P(None, "head", None),
            P("head", None),
            P("head"),
            P("groups"),
        ),
        out_specs=P(("groups", "seq"), "head"),
        check_vma=False,
    )
```

```python
import functools

import jax
import jax.numpy as jnp
from jax import lax
from jax.experimental import pallas as pl
from jax.experimental.pallas import tpu as pltpu
from jax.sharding import PartitionSpec as P

HEAD_DIM = 64
STATE = 128
BLOCK = 128
LANES = 128
TAIL = 16
CHUNK = 256
PIECE = 16
FIRST_LIMIT = 40 << 20
SECOND_LIMIT = 32 << 20
LOG2E = 1.4426950408889634
MESH = pl.DeviceIdType.MESH
F32 = jnp.float32
BF16 = jnp.bfloat16


def silu_of_half(half):
    return half + half * jnp.tanh(half)


def mm(a, b, dims=((1,), (0,))):
    return lax.dot_general(a, b, (dims, ((), ())), preferred_element_type=F32)


def ids_of(starts, positions):
    found = jnp.full(positions.shape, -1, jnp.int32)
    for start in starts:
        found = jnp.where(positions >= start, start, found)
    return found


def id_of(starts, position):
    found = jnp.int32(-1)
    for start in starts:
        found = jnp.where(position >= start, start, found)
    return found


def column(row):
    n = row.shape[1]
    i = lax.broadcasted_iota(jnp.int32, (n, n), 0)
    j = lax.broadcasted_iota(jnp.int32, (n, n), 1)
    return jnp.sum(jnp.where(i == j, row, 0.0), axis=1, keepdims=True)


def fill_spread(e_ref):
    twice, wide = e_ref.shape
    row = lax.broadcasted_iota(jnp.int32, (twice, wide), 0)
    lane = lax.broadcasted_iota(jnp.int32, (twice, wide), 1)
    e_ref[...] = (lane // HEAD_DIM == row % (twice // 2)).astype(F32).astype(BF16)


def halves(value):
    hi = value.astype(BF16)
    lo = (value - hi.astype(F32)).astype(BF16)
    return jnp.concatenate([hi, lo], axis=0)


def expand(value, e_ref):
    return mm(halves(value), e_ref[...], ((0,), (0,)))


def shift_matrix(within):
    t = lax.broadcasted_iota(jnp.int32, (BLOCK, TAIL + BLOCK), 0)
    i = lax.broadcasted_iota(jnp.int32, (BLOCK, TAIL + BLOCK), 1)
    steps = [((i == t + (TAIL - 3 + k)) & (within >= 3 - k)).astype(F32) for k in range(3)]
    order = [steps[k][r : r + PIECE] for r in range(0, BLOCK, PIECE) for k in range(3)]
    return jnp.concatenate(order, axis=0).astype(BF16)


def conv_pieces(past, own, halfw):
    for r in range(0, BLOCK, PIECE):
        half = halfw[4] + halfw[3] * own[TAIL + r : TAIL + r + PIECE, :].astype(F32)
        for k in range(3):
            at = 3 * r + k * PIECE
            half = half + halfw[k] * past[at : at + PIECE]
        yield slice(r, r + PIECE), silu_of_half(half)


def pipelined(units):
    for u in range(len(units) + 4):
        for phase, lag in ((0, 0), (1, 3), (2, 4)):
            if 0 <= u - lag < len(units):
                units[u - lag][phase]()


def prepare(
    seg_ref, dtp_ref, dtb_ref, dec_ref, skip_ref, wx_ref, bx_ref, wbc_ref, bbc_ref,
    ecarry_ref, shift_ref, mask_ref, tailw_ref, cfac_ref, ends_ref, lower_ref, cols_ref, skip_row, total_d, e_ref,
    hwx_ref, hwbc_ref,
):
    heads, rows = dtp_ref.shape
    groups = total_d.shape[0]
    repeat = heads // groups
    wide = e_ref.shape[1]
    fill_spread(e_ref)
    for g in range(groups):
        cols = slice(g * wide, (g + 1) * wide)
        for k in range(4):
            hwx_ref[g, k : k + 1, :] = 0.5 * wx_ref[k : k + 1, cols]
            hwbc_ref[g, k : k + 1, :] = 0.5 * wbc_ref[k, g : g + 1, :]
        hwx_ref[g, 4:5, :] = 0.5 * bx_ref[0:1, cols]
        hwbc_ref[g, 4:5, :] = 0.5 * bbc_ref[g : g + 1, :]
    skip = jnp.broadcast_to(column(skip_ref[...]), (heads, LANES))
    for g in range(groups):
        skip_row[:, g * wide : (g + 1) * wide] = expand(skip[g * repeat : (g + 1) * repeat], e_ref)[0:8]
    first = lax.axis_index("seq") * rows
    starts = [jnp.int32(0)]
    for j in range(seg_ref.shape[0] - 1):
        starts.append(starts[-1] + seg_ref[j])
    entered = id_of(starts, first - 1)
    bias = column(dtb_ref[...])
    rate = -LOG2E * column(jnp.exp(dec_ref[...]))
    s = lax.broadcasted_iota(jnp.int32, (BLOCK, BLOCK), 0)
    t = lax.broadcasted_iota(jnp.int32, (BLOCK, BLOCK), 1)
    upper = (s <= t).astype(F32).astype(BF16)
    base = jnp.zeros((heads, LANES), F32)
    for b in range(rows // BLOCK):
        cut = slice(b * BLOCK, (b + 1) * BLOCK)
        raw = dtp_ref[:, cut].astype(F32) + bias
        dt = jnp.maximum(raw, 0.0) + jnp.log1p(jnp.exp(-jnp.abs(raw)))
        rest = rate * dt
        parts = []
        for _ in range(3):
            parts.append(rest.astype(BF16))
            rest = rest - parts[-1].astype(F32)
        sums = mm(jnp.concatenate(parts, axis=0), upper)
        cum = sums[0:heads] + (sums[heads : 2 * heads] + sums[2 * heads : 3 * heads])
        at = first + b * BLOCK
        tall = at + s
        tall_id = ids_of(starts, tall)
        row_id = ids_of(starts, at + lax.broadcasted_iota(jnp.int32, (1, LANES), 1))
        before, end = id_of(starts, at - 1), id_of(starts, at + BLOCK - 1)
        same_end = (row_id == end).astype(F32)
        last = jnp.broadcast_to(cum[:, BLOCK - 1 : BLOCK], cum.shape)
        shift_ref[b] = shift_matrix((tall - tall_id)[:, 0:1])
        mask_ref[b] = ((t <= s) & (tall_id == row_id)).astype(F32)
        tailw_ref[b] = jnp.exp2(last - cum) * dt * same_end
        cfac_ref[b] = jnp.exp2(cum) * (row_id == before).astype(F32)
        ecarry_ref[:, cut] = 0.5 * jnp.exp2(base + cum) * (row_id == entered).astype(F32)
        ends_ref[b] = jnp.exp2(last) * (end == before).astype(F32)
        lower_ref[b] = cum - jnp.log2(dt)
        for g in range(groups):
            cols_ref[b * groups + g, :, 0:repeat] = jnp.transpose(cum[g * repeat : (g + 1) * repeat])
        base = base + last
    leaving = id_of(starts, first + rows - 1)
    whole = jnp.exp2(base) * (leaving == entered).astype(F32)
    for g in range(groups):
        total_d[g] = expand(whole[g * repeat : (g + 1) * repeat], e_ref)[0:8]


def states_of(
    g, b, xbuf, bbuf, hwx_ref, hwbc_ref, shift_ref, tailw_ref, ends_ref, e_ref,
    xc, bpart, c_ref, entering, state,
):
    repeat = e_ref.shape[0] // 2
    wide = e_ref.shape[1]
    low = pl.multiple_of(b * BLOCK, BLOCK)
    rows, tall = pl.ds(low, BLOCK), pl.ds(low, TAIL + BLOCK)
    heads = pl.ds(pl.multiple_of(g * repeat, repeat), repeat)
    shared = {}

    def pairs_begin():
        shared["shift"] = shift_ref[b]
        shared["own"] = bbuf[g, tall, :]
        shared["past"] = mm(shared["shift"], shared["own"])
        shared["tail"] = jnp.transpose(halves(tailw_ref[b, heads, :]).astype(F32)).astype(BF16)

    def pairs_work():
        halfw = [hwbc_ref[g, k : k + 1, :] for k in range(5)]
        bc = jnp.concatenate([piece for _, piece in conv_pieces(shared["past"], shared["own"], halfw)], axis=0)
        shared["turned"] = jnp.transpose(bc[:, 0:STATE]).astype(BF16)
        bpart[g, rows, :] = bc[:, 0:STATE].astype(BF16)
        c_ref[g, rows, :] = bc[:, STATE:].astype(BF16)

    def pairs_end():
        pass

    def unit(j):
        cols = slice(j, j + CHUNK)
        mine = {}

        def begin():
            mine["own"] = xbuf[g, tall, cols]
            mine["past"] = mm(shared["shift"], mine["own"])
            mine["spread"] = mm(shared["tail"], e_ref[:, cols])
            mine["decay"] = expand(ends_ref[b, heads, 0:8], e_ref.at[:, cols])

        def work():
            halfw = [hwx_ref[g, k : k + 1, cols] for k in range(5)]
            kept, scaled = [], []
            for cut, piece in conv_pieces(mine["past"], mine["own"], halfw):
                kept.append(piece.astype(BF16))
                scaled.append((piece * mine["spread"][cut]).astype(BF16))
            mine["update"] = mm(shared["turned"], jnp.concatenate(scaled, axis=0))
            xc[g, rows, cols] = jnp.concatenate(kept, axis=0)

        def end():
            old = state[g, :, cols]
            entering[g, b, :, cols] = old.astype(BF16)
            state[g, :, cols] = mine["decay"][0:1] * old + mine["update"]

        return begin, work, end

    return [(pairs_begin, pairs_work, pairs_end)] + [unit(j) for j in range(0, wide, CHUNK)]


def within_of(g, b, xc, bpart, c_ref, entering, mask_ref, cfac_ref, lower_ref, cols_ref, skip_row, e_ref, mid):
    groups = xc.shape[0]
    repeat = e_ref.shape[0] // 2
    wide = e_ref.shape[1]
    rows = pl.ds(pl.multiple_of(b * BLOCK, BLOCK), BLOCK)
    heads = pl.ds(pl.multiple_of(g * repeat, repeat), repeat)
    b_part, c_part = bpart[g, rows, :], c_ref[g, rows, :]
    scores = mm(c_part, b_part, ((1,), (1,))) * mask_ref[b]
    carry = jnp.transpose(halves(cfac_ref[b, heads, :]).astype(F32)).astype(BF16)
    columns = cols_ref[b * groups + g]
    lower = lower_ref[b, heads, :]
    left = lax.broadcasted_iota(jnp.int32, (BLOCK, LANES), 1) < HEAD_DIM
    for j in range(0, wide, CHUNK):
        cols = slice(j, j + CHUNK)
        carried = mm(c_part, entering[g, b, :, cols]) * mm(carry, e_ref[:, cols])
        for k in range(0, CHUNK, LANES):
            sl = slice(j + k, j + k + LANES)
            parts = []
            for h in ((j + k) // HEAD_DIM, (j + k) // HEAD_DIM + 1):
                spread = jnp.minimum(columns[:, h : h + 1] - lower[h : h + 1, :], 80.0)
                parts.append((scores * jnp.exp2(spread)).astype(BF16))
            value = xc[g, rows, sl]
            none = jnp.zeros_like(value)
            pair = jnp.concatenate([jnp.where(left, value, none), jnp.where(left, none, value)], axis=0)
            y = mm(jnp.concatenate(parts, axis=1), pair)
            skip = skip_row[0:1, pl.ds(pl.multiple_of(g * wide + j + k, LANES), LANES)]
            mid[g, rows, sl] = (0.5 * (y + carried[:, k : k + LANES] + skip * value.astype(F32))).astype(BF16)


def stage_times(links):
    times = [0, 2, 6]
    for r in range(max(1, (links - 1).bit_length())):
        times.append(times[-1] + 4 + min(r, 1))
    return times + [times[-1] + 4, times[-1] + 6]


def early_groups(groups, turns, links):
    last = stage_times(links)[-1]
    return sum((g + 1) * turns - 1 + last < (2 * groups + g) * turns for g in range(groups - 1))


def pack_d(d):
    hi = d.astype(BF16).astype(F32)
    return jnp.concatenate([hi, d - hi], axis=0).astype(BF16)


def unpack_d(packed):
    both = packed.astype(F32)
    return both[0:8] + both[8:16]


class Exchange:
    def __init__(self, state, total_d, hin, bufs, sems):
        self.state, self.total_d, self.hin = state, total_d, hin
        (self.give1, self.take1, self.give2, self.take2, self.zgive, self.ztake, self.back2, self.home2,
         self.back1, self.home1, self.half_s, self.half_d, self.e_s, self.e_d, self.p_s, self.p_d) = bufs
        self.sem1, self.sem2, self.semz, self.sem4, self.sem5 = sems
        peers = lax.axis_size("seq")
        me = lax.axis_index("seq")
        self.me, self.peers = me, peers
        self.core, self.pair, self.link, self.links = lax.rem(me, 2), lax.rem(me // 2, 2), me // 4, peers // 4
        self.low1, self.low2 = self.core == 0, self.pair == 0
        self.near, self.far = me + 1 - 2 * self.core, me + 2 - 4 * self.pair
        self.half = state.shape[2] // 2
        self.quarter = self.half // 2
        self.rounds = max(1, (self.links - 1).bit_length())

    def copy(self, src, dst, sems, peer):
        return pltpu.make_async_remote_copy(
            src_ref=src, dst_ref=dst, send_sem=sems.at[0], recv_sem=sems.at[1],
            device_id={"seq": peer}, device_id_type=MESH,
        )

    def copy1(self, g):
        return self.copy(self.give1.at[g], self.take1.at[g], self.sem1.at[g], self.near)

    def copy2(self, g):
        return self.copy(self.give2.at[g], self.take2.at[g], self.sem2.at[g], self.far)

    def copyz(self, r, g):
        return self.copy(self.zgive.at[r, g], self.ztake.at[r, g], self.semz.at[r, g], self.me + (4 << r))

    def copy4(self, g):
        return self.copy(self.back2.at[g], self.home2.at[g], self.sem4.at[g], self.far)

    def copy5(self, g):
        return self.copy(self.back1.at[g], self.home1.at[g], self.sem5.at[g], self.near)

    def greet(self):
        me, link = self.me, self.link
        found = [(None, self.near), (None, self.far), (me >= 1, me - 1), (me + 1 < self.peers, me + 1)]
        for r in range(self.rounds):
            found += [(link >= 1 << r, me - (4 << r)), (link + (1 << r) < self.links, me + (4 << r))]
        barrier = pltpu.get_barrier_semaphore()
        expected = jnp.int32(0)
        for known, peer in found:
            if known is None:
                pl.semaphore_signal(barrier, inc=1, device_id={"seq": peer}, device_id_type=MESH)
                expected = expected + 1
            else:
                expected = expected + known.astype(jnp.int32)

                @pl.when(known)
                def _():
                    pl.semaphore_signal(barrier, inc=1, device_id={"seq": peer}, device_id_type=MESH)

        pl.semaphore_wait(barrier, expected)

    def half_lanes(self, which):
        return pl.ds(pl.multiple_of(which * self.half, LANES), self.half)

    def lanes(self, q):
        return pl.ds(pl.multiple_of(self.core * self.half + q * self.quarter, LANES), self.quarter)

    def inner(self, q):
        return pl.ds(pl.multiple_of(q * self.quarter, LANES), self.quarter)

    def stage(self, k, g):
        if k == 0:
            self.begin(g)
        elif k == 1:
            self.cores(g)
        elif k == 2:
            self.chips(g)
        elif k < 3 + self.rounds:
            self.along(k - 3, g)
            if k == 2 + self.rounds:
                self.enter(g)
        elif k == 3 + self.rounds:
            self.share(g)
        else:
            self.finish(g)

    def begin(self, g):
        other = self.half_lanes(1 - self.core)
        self.give1[g, 0:STATE, :] = self.state[g, :, other].astype(BF16)
        self.give1[g, STATE:, :] = pack_d(self.total_d[g, :, other])
        self.copy1(g).start()

    def of_chip(self, g, q):
        mine, other = self.state[g, :, self.lanes(q)], self.take1[g, 0:STATE, self.inner(q)].astype(F32)
        d_mine, d_other = self.total_d[g, :, self.lanes(q)], unpack_d(self.take1[g, STATE:, self.inner(q)])
        late = jnp.where(self.low1, d_other, d_mine)[0:1]
        total = late * jnp.where(self.low1, mine, other) + jnp.where(self.low1, other, mine)
        return total, d_mine * d_other

    def cores(self, g):
        self.copy1(g).wait()
        total, d = self.of_chip(g, 1 - self.pair)
        self.give2[g, 0:STATE, :] = total.astype(BF16)
        self.give2[g, STATE:, :] = pack_d(d)
        self.copy2(g).start()
        total, d = self.of_chip(g, self.pair)
        self.half_s[g] = total
        self.half_d[g] = d

    def chips(self, g):
        self.copy2(g).wait()
        mine, other = self.half_s[g], self.take2[g, 0:STATE, :].astype(F32)
        d_mine, d_other = self.half_d[g], unpack_d(self.take2[g, STATE:, :])
        late = jnp.where(self.low2, d_other, d_mine)[0:1]
        self.p_s[g] = late * jnp.where(self.low2, mine, other) + jnp.where(self.low2, other, mine)
        self.p_d[g] = d_mine * d_other
        self.e_s[g] = jnp.zeros(self.e_s.shape[1:], F32)
        self.e_d[g] = jnp.ones(self.e_d.shape[1:], F32)
        self.pass_on(0, g)

    def pass_on(self, r, g):
        @pl.when(self.link + (1 << r) < self.links)
        def _():
            self.zgive[r, g, 0:STATE, :] = self.p_s[g].astype(BF16)
            self.zgive[r, g, STATE:, :] = pack_d(self.p_d[g])
            self.copyz(r, g).start()

    def along(self, r, g):
        @pl.when(self.link >= 1 << r)
        def _():
            self.copyz(r, g).wait_recv()
            got, d = self.ztake[r, g, 0:STATE, :].astype(F32), unpack_d(self.ztake[r, g, STATE:, :])
            self.e_s[g] = self.e_d[g, 0:1, :] * got + self.e_s[g]
            self.e_d[g] = self.e_d[g] * d
            if r + 1 < self.rounds:
                self.p_s[g] = self.p_d[g, 0:1, :] * got + self.p_s[g]
                self.p_d[g] = self.p_d[g] * d

        if r + 1 < self.rounds:
            self.pass_on(r + 1, g)

    def hand_over(self, g, q, into):
        mine, other = self.state[g, :, self.lanes(q)], self.take1[g, 0:STATE, self.inner(q)].astype(F32)
        d_mine, d_other = self.total_d[g, :, self.lanes(q)], unpack_d(self.take1[g, STATE:, self.inner(q)])
        early = jnp.where(self.low1, d_mine, d_other)[0:1]
        passed = early * into + jnp.where(self.low1, mine, other)
        self.hin[g, :, self.lanes(q)] = jnp.where(self.low1, into, passed).astype(BF16)
        self.back1[g, :, self.inner(q)] = jnp.where(self.low1, passed, into).astype(BF16)

    def enter(self, g):
        into = self.e_s[g]
        mine, other = self.half_s[g], self.take2[g, 0:STATE, :].astype(F32)
        d_mine, d_other = self.half_d[g], unpack_d(self.take2[g, STATE:, :])
        early = jnp.where(self.low2, d_mine, d_other)[0:1]
        passed = early * into + jnp.where(self.low2, mine, other)
        self.back2[g] = jnp.where(self.low2, passed, into).astype(BF16)
        self.copy4(g).start()
        self.hand_over(g, self.pair, jnp.where(self.low2, into, passed))

    def share(self, g):
        self.copy4(g).wait()
        self.hand_over(g, 1 - self.pair, self.home2[g].astype(F32))
        self.copy5(g).start()

    def finish(self, g):
        self.copy5(g).wait()
        self.hin[g, :, self.half_lanes(1 - self.core)] = self.home1[g]
        for r in range(self.rounds):

            @pl.when(self.link + (1 << r) < self.links)
            def _():
                self.copyz(r, g).wait_send()


def mixer_kernel(
    seg_in, x_ref, bc_ref, z_ref, dtp_in, dtb_in, dec_in, skip_in, wx_in, bx_in, wbc_in, bbc_in, gain_in,
    mid, zlate, c_ref, hin_ref, ecarry_ref, gain_ref,
    seg_ref, dtp_ref, dtb_ref, dec_ref, skip_ref, wx_ref, bx_ref, wbc_ref, bbc_ref,
    xbuf, bbuf, xtail, btail, xc, bpart, entering, state, total_d, held,
    shift_ref, mask_ref, tailw_ref, cfac_ref, ends_ref, lower_ref, cols_ref, skip_row, e_ref, hwx_ref, hwbc_ref,
    give1, take1, give2, take2, zgive, ztake, back2, home2, back1, home1,
    half_s, half_d, e_s, e_d, p_s, p_d,
    sem1, sem2, semz, sem4, sem5, semx, semb, semt, semg, semw,
):
    groups, _, wide = xbuf.shape
    rows = x_ref.shape[0]
    blocks = rows // BLOCK
    step = 2 - blocks % 2
    turns = blocks // step
    repeat = e_ref.shape[0] // 2
    late = zlate.shape[0]
    early = groups - late
    exchange = Exchange(
        state, total_d, hin_ref,
        (give1, take1, give2, take2, zgive, ztake, back2, home2, back1, home1, half_s, half_d, e_s, e_d, p_s, p_d),
        (sem1, sem2, semz, sem4, sem5),
    )
    me, peers = exchange.me, exchange.peers
    times = stage_times(exchange.links)

    def lanes_of(g, width):
        return pl.ds(pl.multiple_of(g * width, LANES), width)

    def load_x(g):
        return pltpu.make_async_copy(
            x_ref.at[:, lanes_of(g, wide)], xbuf.at[g, pl.ds(TAIL, rows), :], semx.at[g]
        )

    def load_b(g):
        return pltpu.make_async_copy(
            bc_ref.at[:, lanes_of(g, 2 * STATE)], bbuf.at[g, pl.ds(TAIL, rows), :], semb.at[g]
        )

    def load_z(g):
        where = zlate.at[g - early] if g >= early else xbuf.at[g, pl.ds(TAIL, rows), :]
        return pltpu.make_async_copy(z_ref.at[:, lanes_of(g, wide)], where, semg.at[g])

    small = [
        pltpu.make_async_copy(src, dst, semw.at[n])
        for n, (src, dst) in enumerate((
            (seg_in, seg_ref), (dtp_in, dtp_ref), (dtb_in, dtb_ref), (dec_in, dec_ref), (skip_in, skip_ref),
            (wx_in, wx_ref), (bx_in, bx_ref), (wbc_in, wbc_ref), (bbc_in, bbc_ref), (gain_in, gain_ref),
        ))
    ]
    for load in small:
        load.start()
    load_b(0).start()
    load_x(0).start()
    tails = [
        exchange.copy(x_ref.at[pl.ds(rows - TAIL, TAIL), :], xtail, semt.at[0], me + 1),
        exchange.copy(bc_ref.at[pl.ds(rows - TAIL, TAIL), :], btail, semt.at[1], me + 1),
    ]
    exchange.greet()

    @pl.when(me + 1 < peers)
    def _():
        for tail in tails:
            tail.start()

    for load in small:
        load.wait()
    prepare(
        seg_ref, dtp_ref, dtb_ref, dec_ref, skip_ref, wx_ref, bx_ref, wbc_ref, bbc_ref,
        ecarry_ref, shift_ref, mask_ref, tailw_ref, cfac_ref, ends_ref, lower_ref, cols_ref, skip_row, total_d, e_ref,
        hwx_ref, hwbc_ref,
    )

    @pl.when(me == 0)
    def _():
        xtail[...] = jnp.zeros(xtail.shape, BF16)
        btail[...] = jnp.zeros(btail.shape, BF16)

    @pl.when(me > 0)
    def _():
        for tail in tails:
            tail.wait_recv()

    def stages(turn, p, which):
        for at in range(turns):
            due = [k for k in which if (turns - 1 + times[k]) % turns == at]
            if not due:
                continue

            @pl.when(p == at)
            def _():
                for k in due:
                    g = turn - (turns - 1 + times[k]) // turns

                    @pl.when((g >= 0) & (g < groups))
                    def _():
                        exchange.stage(k, g)

    def first_part(i, carry):
        g, p = lax.div(i, turns), lax.rem(i, turns)

        @pl.when(p == 0)
        def _():
            @pl.when(g + 1 < groups)
            def _():
                load_b(g + 1).start()
                load_x(g + 1).start()

            state[g] = jnp.zeros(state.shape[1:], F32)
            load_b(g).wait()
            load_x(g).wait()
            xbuf[g, 0:TAIL, :] = xtail[:, lanes_of(g, wide)]
            bbuf[g, 0:TAIL, :] = btail[:, lanes_of(g, 2 * STATE)]

        units = []
        for b in range(step):
            units += states_of(
                g, step * p + b, xbuf, bbuf, hwx_ref, hwbc_ref, shift_ref, tailw_ref, ends_ref, e_ref,
                xc, bpart, c_ref, entering, state,
            )
        pipelined(units)
        stages(g, p, range(len(times)))
        return carry

    def second_part(i, carry):
        g, p = lax.div(i, turns), lax.rem(i, turns)
        for b in range(step):
            within_of(
                g, step * p + b, xc, bpart, c_ref, entering,
                mask_ref, cfac_ref, lower_ref, cols_ref, skip_row, e_ref, mid,
            )
        stages(g + groups, p, range(1, len(times)))
        return carry

    def third_part(i, carry):
        g, p = lax.div(i, turns), lax.rem(i, turns)
        heads = pl.ds(pl.multiple_of(g * repeat, repeat), repeat)
        units = []
        for b in range(step):
            low = (step * p + b) * BLOCK
            tokens = pl.ds(pl.multiple_of(low, BLOCK), BLOCK)
            units += gate(
                mid.at[g, tokens, :], xbuf.at[g, pl.ds(pl.multiple_of(low + TAIL, TAIL), BLOCK), :],
                c_ref.at[g, tokens, :], hin_ref.at[g], ecarry_ref.at[heads, tokens], gain_ref.at[:, lanes_of(g, wide)],
                e_ref, held.at[b * BLOCK : (b + 1) * BLOCK], mid.at[g, tokens, :],
            )
        pipelined(units)
        stages(g + 2 * groups, p, range(1, len(times)))
        return carry

    lax.fori_loop(0, groups * turns, first_part, 0)
    for g in range(groups):
        load_z(g).start()
    lax.fori_loop(0, groups * turns, second_part, 0)
    for g in range(early):
        load_z(g).wait()
    if early:
        lax.fori_loop(0, early * turns, third_part, 0)
    for i in range((2 * groups + early) * turns, groups * turns + times[-1]):
        for k in range(1, len(times)):
            n = i - (turns - 1) - times[k]
            if n >= 0 and n % turns == 0 and n < groups * turns:
                exchange.stage(k, n // turns)
    for g in range(early, groups):
        load_z(g).wait()

    @pl.when(me + 1 < peers)
    def _():
        for tail in tails:
            tail.wait_send()


def gate(y_ref, z_ref, c_ref, hin_ref, weights_ref, gain_ref, e_ref, held_ref, out_ref):
    wide = y_ref.shape[1]
    shared = {"squares": jnp.zeros((BLOCK, LANES), F32)}

    def unit(j):
        cols = slice(j, j + CHUNK)
        mine = {}

        def begin():
            if j == 0:
                shared["turned"] = jnp.transpose(halves(weights_ref[...]).astype(F32)).astype(BF16)
                shared["c"] = c_ref[...]
            mine["read"] = mm(shared["c"], hin_ref[:, cols])
            mine["factor"] = mm(shared["turned"], e_ref[:, cols])

        def work():
            kept = []
            for r in range(0, BLOCK, PIECE):
                here = slice(r, r + PIECE)
                full = y_ref[here, cols].astype(F32) + mine["read"][here] * mine["factor"][here]
                z = z_ref[here, cols]
                scaled = full * z.astype(F32)
                held = scaled + scaled * jnp.tanh((z * BF16(0.5)).astype(F32))
                held_ref[here, cols] = held
                piece = held * held
                kept.append(sum(piece[:, k : k + LANES] for k in range(0, CHUNK, LANES)))
            shared["squares"] = shared["squares"] + jnp.concatenate(kept, axis=0)

        def end():
            pass

        return begin, work, end

    def scale_all():
        mean = jnp.sum(shared["squares"], axis=1, keepdims=True) * (1.0 / wide)
        shared["scale"] = jnp.broadcast_to(lax.rsqrt(mean + 1e-05), (BLOCK, LANES))

    def write():
        for j in range(0, wide, LANES):
            sl = slice(j, j + LANES)
            out_ref[:, sl] = (held_ref[:, sl] * shared["scale"] * gain_ref[0:1, sl]).astype(BF16)

    return [unit(j) for j in range(0, wide, CHUNK)] + [(lambda: None, scale_all, write)]


def output_kernel(
    mid_ref, z_ref, c_ref, hin_ref, ecarry_ref, gain_ref, out_ref, e_ref, obuf, held, semo, semd,
):
    groups, rows, wide = mid_ref.shape
    late, turns, part = obuf.shape[0:3]
    early = groups - late
    repeat = e_ref.shape[0] // 2

    def done(g):
        return pltpu.make_async_copy(mid_ref.at[g], out_ref.at[:, g * wide : (g + 1) * wide], semd.at[g])

    def store(i):
        l, p = lax.div(i, turns), lax.rem(i, turns)
        lanes = pl.ds(pl.multiple_of((early + l) * wide, LANES), wide)
        return pltpu.make_async_copy(
            obuf.at[l, p], out_ref.at[pl.ds(pl.multiple_of(p * part, part), part), lanes], semo.at[i]
        )

    for g in range(early):
        done(g).start()
    fill_spread(e_ref)

    def step(i, carry):
        l, p = lax.div(i, turns), lax.rem(i, turns)
        g = early + l
        heads = pl.ds(pl.multiple_of(g * repeat, repeat), repeat)
        units = []
        for r in range(0, part, BLOCK):
            tokens = pl.ds(pl.multiple_of(p * part + r, BLOCK), BLOCK)
            units += gate(
                mid_ref.at[g, tokens, :], z_ref.at[l, tokens, :], c_ref.at[g, tokens, :], hin_ref.at[g],
                ecarry_ref.at[heads, tokens], gain_ref.at[:, pl.ds(pl.multiple_of(g * wide, LANES), wide)],
                e_ref, held.at[r : r + BLOCK], obuf.at[l, p, r : r + BLOCK, :],
            )
        pipelined(units)
        store(i).start()
        return carry

    lax.fori_loop(0, late * turns, step, 0)
    for i in range(late * turns):
        store(jnp.int32(i)).wait()
    for g in range(early):
        done(g).wait()


def shards(
    x_proj, z_gate, bc_proj, dt_proj, dt_bias, decay_log, skip_gain,
    conv_x, bias_x, conv_bc, bias_bc, norm_gain, seg_lengths,
):
    rows, channels = x_proj.shape
    heads = dt_proj.shape[1]
    groups = bc_proj.shape[1]
    repeat = heads // groups
    wide = channels // groups
    blocks = rows // BLOCK
    step = 2 - blocks % 2
    turns = blocks // step
    links = lax.axis_size("seq") // 4
    rounds = max(1, (links - 1).bit_length())
    bc = bc_proj.reshape(rows, groups * 2 * STATE)
    vmem = pl.BlockSpec(memory_space=pltpu.VMEM)
    anywhere = pl.BlockSpec(memory_space=pl.ANY)
    pin = lambda array: pltpu.with_memory_space_constraint(array, pltpu.HBM)
    outside = pl.BlockSpec(memory_space=pltpu.HBM)
    half, quarter = wide // 2, wide // 4
    scratch = lambda kind, *shape: pltpu.VMEM(shape, kind)
    dma = lambda *shape: pltpu.SemaphoreType.DMA(shape)
    per_block = (blocks, heads, BLOCK)
    early = early_groups(groups, turns, links)
    mid, zlate, c, hin, ecarry, gain = pl.pallas_call(
        mixer_kernel,
        in_specs=[outside, anywhere, anywhere, anywhere] + [outside] * 9,
        out_specs=[vmem] * 6,
        out_shape=[
            jax.ShapeDtypeStruct((groups, rows, wide), BF16),
            jax.ShapeDtypeStruct((groups - early, rows, wide), BF16),
            jax.ShapeDtypeStruct((groups, rows, STATE), BF16),
            jax.ShapeDtypeStruct((groups, STATE, wide), BF16),
            jax.ShapeDtypeStruct((heads, rows), F32),
            jax.ShapeDtypeStruct((1, channels), F32),
        ],
        scratch_shapes=[
            pltpu.SMEM(seg_lengths.shape, jnp.int32), scratch(BF16, heads, rows),
            scratch(F32, 1, heads), scratch(F32, 1, heads), scratch(F32, 1, heads),
            scratch(F32, *conv_x.shape), scratch(F32, 1, channels), scratch(F32, *conv_bc.shape), scratch(F32, *bias_bc.shape),
            scratch(BF16, groups, TAIL + rows, wide), scratch(BF16, groups, TAIL + rows, 2 * STATE),
            scratch(BF16, TAIL, channels), scratch(BF16, TAIL, groups * 2 * STATE),
            scratch(BF16, groups, rows, wide), scratch(BF16, groups, rows, STATE),
            scratch(BF16, groups, blocks, STATE, wide), scratch(F32, groups, STATE, wide), scratch(F32, groups, 8, wide),
            scratch(F32, step * BLOCK, wide),
            scratch(BF16, blocks, 3 * BLOCK, TAIL + BLOCK), scratch(F32, blocks, BLOCK, BLOCK),
            scratch(F32, *per_block), scratch(F32, *per_block), scratch(F32, *per_block), scratch(F32, *per_block),
            scratch(F32, blocks * groups, BLOCK, LANES), scratch(F32, 8, channels), scratch(BF16, 2 * repeat, wide),
            scratch(F32, groups, 8, wide), scratch(F32, groups, 8, 2 * STATE),
            scratch(BF16, groups, STATE + 16, half), scratch(BF16, groups, STATE + 16, half),
            scratch(BF16, groups, STATE + 16, quarter), scratch(BF16, groups, STATE + 16, quarter),
            scratch(BF16, rounds, groups, STATE + 16, quarter), scratch(BF16, rounds, groups, STATE + 16, quarter),
            scratch(BF16, groups, STATE, quarter), scratch(BF16, groups, STATE, quarter),
            scratch(BF16, groups, STATE, half), scratch(BF16, groups, STATE, half),
            scratch(F32, groups, STATE, quarter), scratch(F32, groups, 8, quarter),
            scratch(F32, groups, STATE, quarter), scratch(F32, groups, 8, quarter),
            scratch(F32, groups, STATE, quarter), scratch(F32, groups, 8, quarter),
            dma(groups, 2), dma(groups, 2), dma(rounds, groups, 2), dma(groups, 2), dma(groups, 2),
            dma(groups), dma(groups), dma(2, 2), dma(groups), dma(10),
        ],
        compiler_params=pltpu.CompilerParams(
            collective_id=0, has_side_effects=True, vmem_limit_bytes=FIRST_LIMIT
        ),
        name="mixer",
    )(
        pin(seg_lengths), x_proj, bc, z_gate, pin(dt_proj.T), pin(dt_bias[None]), pin(decay_log[None]), pin(skip_gain[None]),
        pin(conv_x), pin(bias_x[None]), pin(conv_bc), pin(bias_bc), pin(norm_gain[None]),
    )

    late = groups - early
    return pl.pallas_call(
        output_kernel,
        in_specs=[vmem] * 6,
        out_specs=anywhere,
        out_shape=jax.ShapeDtypeStruct((rows, channels), BF16),
        scratch_shapes=[
            scratch(BF16, 2 * repeat, wide), scratch(BF16, late, turns, step * BLOCK, wide),
            scratch(F32, step * BLOCK, wide), dma(late * turns), dma(groups),
        ],
        compiler_params=pltpu.CompilerParams(vmem_limit_bytes=SECOND_LIMIT),
        name="outputs",
    )(mid, zlate, c, hin, ecarry, gain)


def solution(mesh):
    return jax.shard_map(
        shards,
        mesh=mesh,
        in_specs=(
            P(("groups", "seq"), "head"),
            P(("groups", "seq"), "head"),
            P(("groups", "seq"), "head", None),
            P(("groups", "seq"), "head"),
            P("head"),
            P("head"),
            P("head"),
            P(None, "head"),
            P("head"),
            P(None, "head", None),
            P("head", None),
            P("head"),
            P("groups"),
        ),
        out_specs=P(("groups", "seq"), "head"),
        check_vma=False,
    )
```

```python
import functools

import jax
import jax.numpy as jnp
from jax import lax
from jax.experimental import pallas as pl
from jax.experimental.pallas import tpu as pltpu
from jax.sharding import PartitionSpec as P

HEAD_DIM = 64
STATE = 128
BLOCK = 128
LANES = 128
TAIL = 16
CHUNK = 256
PIECE = 16
FIRST_LIMIT = 40 << 20
SECOND_LIMIT = 32 << 20
LOG2E = 1.4426950408889634
MESH = pl.DeviceIdType.MESH
F32 = jnp.float32
BF16 = jnp.bfloat16


def silu_of_half(half):
    return half + half * jnp.tanh(half)


def mm(a, b, dims=((1,), (0,))):
    return lax.dot_general(a, b, (dims, ((), ())), preferred_element_type=F32)


def ids_of(starts, positions):
    found = jnp.full(positions.shape, -1, jnp.int32)
    for start in starts:
        found = jnp.where(positions >= start, start, found)
    return found


def id_of(starts, position):
    found = jnp.int32(-1)
    for start in starts:
        found = jnp.where(position >= start, start, found)
    return found


def column(row):
    n = row.shape[1]
    i = lax.broadcasted_iota(jnp.int32, (n, n), 0)
    j = lax.broadcasted_iota(jnp.int32, (n, n), 1)
    return jnp.sum(jnp.where(i == j, row, 0.0), axis=1, keepdims=True)


def fill_spread(e_ref):
    twice, wide = e_ref.shape
    row = lax.broadcasted_iota(jnp.int32, (twice, wide), 0)
    lane = lax.broadcasted_iota(jnp.int32, (twice, wide), 1)
    e_ref[...] = (lane // HEAD_DIM == row % (twice // 2)).astype(F32).astype(BF16)


def halves(value):
    hi = value.astype(BF16)
    lo = (value - hi.astype(F32)).astype(BF16)
    return jnp.concatenate([hi, lo], axis=0)


def expand(value, e_ref):
    return mm(halves(value), e_ref[...], ((0,), (0,)))


def shift_matrix(within):
    t = lax.broadcasted_iota(jnp.int32, (BLOCK, TAIL + BLOCK), 0)
    i = lax.broadcasted_iota(jnp.int32, (BLOCK, TAIL + BLOCK), 1)
    steps = [((i == t + (TAIL - 3 + k)) & (within >= 3 - k)).astype(F32) for k in range(3)]
    order = [steps[k][r : r + PIECE] for r in range(0, BLOCK, PIECE) for k in range(3)]
    return jnp.concatenate(order, axis=0).astype(BF16)


def conv_pieces(past, own, halfw):
    for r in range(0, BLOCK, PIECE):
        half = halfw[4] + halfw[3] * own[TAIL + r : TAIL + r + PIECE, :].astype(F32)
        for k in range(3):
            at = 3 * r + k * PIECE
            half = half + halfw[k] * past[at : at + PIECE]
        yield slice(r, r + PIECE), silu_of_half(half)


def pipelined(units):
    for u in range(len(units) + 4):
        for phase, lag in ((0, 0), (1, 3), (2, 4)):
            if 0 <= u - lag < len(units):
                units[u - lag][phase]()


def prepare(
    seg_ref, dtp_ref, dtb_ref, dec_ref, skip_ref, wx_ref, bx_ref, wbc_ref, bbc_ref,
    ecarry_ref, shift_ref, mask_ref, tailw_ref, cfac_ref, ends_ref, lower_ref, cols_ref, skip_row, total_d, e_ref,
    hwx_ref, hwbc_ref,
):
    heads, rows = dtp_ref.shape
    groups = total_d.shape[0]
    repeat = heads // groups
    wide = e_ref.shape[1]
    fill_spread(e_ref)
    for g in range(groups):
        cols = slice(g * wide, (g + 1) * wide)
        for k in range(4):
            hwx_ref[g, k : k + 1, :] = 0.5 * wx_ref[k : k + 1, cols]
            hwbc_ref[g, k : k + 1, :] = 0.5 * wbc_ref[k, g : g + 1, :]
        hwx_ref[g, 4:5, :] = 0.5 * bx_ref[0:1, cols]
        hwbc_ref[g, 4:5, :] = 0.5 * bbc_ref[g : g + 1, :]
    skip = jnp.broadcast_to(column(skip_ref[...]), (heads, LANES))
    for g in range(groups):
        skip_row[:, g * wide : (g + 1) * wide] = 0.5 * expand(skip[g * repeat : (g + 1) * repeat, 0:8], e_ref)
    first = lax.axis_index("seq") * rows
    starts = [jnp.int32(0)]
    for j in range(seg_ref.shape[0] - 1):
        starts.append(starts[-1] + seg_ref[j])
    entered = id_of(starts, first - 1)
    bias = column(dtb_ref[...])
    rate = -LOG2E * column(jnp.exp(dec_ref[...]))
    s = lax.broadcasted_iota(jnp.int32, (BLOCK, BLOCK), 0)
    t = lax.broadcasted_iota(jnp.int32, (BLOCK, BLOCK), 1)
    upper = (s <= t).astype(F32).astype(BF16)
    base = jnp.zeros((heads, LANES), F32)
    for b in range(rows // BLOCK):
        cut = slice(b * BLOCK, (b + 1) * BLOCK)
        raw = dtp_ref[:, cut].astype(F32) + bias
        dt = jnp.maximum(raw, 0.0) + jnp.log1p(jnp.exp(-jnp.abs(raw)))
        rest = rate * dt
        parts = []
        for _ in range(3):
            parts.append(rest.astype(BF16))
            rest = rest - parts[-1].astype(F32)
        sums = mm(jnp.concatenate(parts, axis=0), upper)
        cum = sums[0:heads] + (sums[heads : 2 * heads] + sums[2 * heads : 3 * heads])
        at = first + b * BLOCK
        tall = at + s
        tall_id = ids_of(starts, tall)
        row_id = ids_of(starts, at + lax.broadcasted_iota(jnp.int32, (1, LANES), 1))
        before, end = id_of(starts, at - 1), id_of(starts, at + BLOCK - 1)
        same_end = (row_id == end).astype(F32)
        last = jnp.broadcast_to(cum[:, BLOCK - 1 : BLOCK], cum.shape)
        shift_ref[b] = shift_matrix((tall - tall_id)[:, 0:1])
        mask_ref[b] = ((t <= s) & (tall_id == row_id)).astype(F32)
        tailw_ref[b] = jnp.exp2(last - cum) * dt * same_end
        cfac_ref[b] = 0.5 * jnp.exp2(cum) * (row_id == before).astype(F32)
        ecarry_ref[:, cut] = 0.5 * jnp.exp2(base + cum) * (row_id == entered).astype(F32)
        ends_ref[b] = jnp.exp2(last) * (end == before).astype(F32)
        lower_ref[b] = cum - (jnp.log2(dt) - 1.0)
        for g in range(groups):
            cols_ref[b * groups + g, :, 0:repeat] = jnp.transpose(cum[g * repeat : (g + 1) * repeat])
        base = base + last
    leaving = id_of(starts, first + rows - 1)
    whole = jnp.exp2(base) * (leaving == entered).astype(F32)
    for g in range(groups):
        total_d[g] = expand(whole[g * repeat : (g + 1) * repeat, 0:8], e_ref)


def states_of(
    g, b, xbuf, bbuf, hwx_ref, hwbc_ref, shift_ref, tailw_ref, ends_ref, e_ref,
    xc, bpart, c_ref, entering, state,
):
    repeat = e_ref.shape[0] // 2
    wide = e_ref.shape[1]
    low = pl.multiple_of(b * BLOCK, BLOCK)
    rows, tall = pl.ds(low, BLOCK), pl.ds(low, TAIL + BLOCK)
    heads = pl.ds(pl.multiple_of(g * repeat, repeat), repeat)
    shared = {}

    def pairs_begin():
        shared["shift"] = shift_ref[b]
        shared["own"] = bbuf[g, tall, :]
        shared["past"] = mm(shared["shift"], shared["own"])
        shared["tail"] = jnp.transpose(halves(tailw_ref[b, heads, :]).astype(F32)).astype(BF16)

    def pairs_work():
        halfw = [hwbc_ref[g, k : k + 1, :] for k in range(5)]
        bc = jnp.concatenate([piece for _, piece in conv_pieces(shared["past"], shared["own"], halfw)], axis=0)
        shared["turned"] = jnp.transpose(bc[:, 0:STATE]).astype(BF16)
        bpart[g, rows, :] = bc[:, 0:STATE].astype(BF16)
        c_ref[g, rows, :] = bc[:, STATE:].astype(BF16)

    def pairs_end():
        pass

    def unit(j):
        cols = slice(j, j + CHUNK)
        mine = {}

        def begin():
            mine["own"] = xbuf[g, tall, cols]
            mine["past"] = mm(shared["shift"], mine["own"])
            mine["spread"] = mm(shared["tail"], e_ref[:, cols])
            mine["decay"] = expand(ends_ref[b, heads, 0:8], e_ref.at[:, cols])

        def work():
            halfw = [hwx_ref[g, k : k + 1, cols] for k in range(5)]
            kept, scaled = [], []
            for cut, piece in conv_pieces(mine["past"], mine["own"], halfw):
                kept.append(piece.astype(BF16))
                scaled.append((piece * mine["spread"][cut]).astype(BF16))
            mine["update"] = mm(shared["turned"], jnp.concatenate(scaled, axis=0))
            xc[g, rows, cols] = jnp.concatenate(kept, axis=0)

        def end():
            old = state[g, :, cols]
            entering[g, b, :, cols] = old.astype(BF16)
            state[g, :, cols] = mine["decay"][0:1] * old + mine["update"]

        return begin, work, end

    return [(pairs_begin, pairs_work, pairs_end)] + [unit(j) for j in range(0, wide, CHUNK)]


def within_of(g, b, xc, bpart, c_ref, entering, mask_ref, cfac_ref, lower_ref, cols_ref, skip_row, e_ref, mid):
    groups = xc.shape[0]
    repeat = e_ref.shape[0] // 2
    wide = e_ref.shape[1]
    rows = pl.ds(pl.multiple_of(b * BLOCK, BLOCK), BLOCK)
    heads = pl.ds(pl.multiple_of(g * repeat, repeat), repeat)
    b_part, c_part = bpart[g, rows, :], c_ref[g, rows, :]
    scores = mm(c_part, b_part, ((1,), (1,)))
    allowed = mask_ref[b].astype(BF16) > BF16(0.5)
    carry = jnp.transpose(halves(cfac_ref[b, heads, :]).astype(F32)).astype(BF16)
    columns = cols_ref[b * groups + g]
    lower = lower_ref[b, heads, :]
    left = lax.broadcasted_iota(jnp.int32, (BLOCK, LANES), 1) < HEAD_DIM
    for j in range(0, wide, CHUNK):
        cols = slice(j, j + CHUNK)
        carried = mm(c_part, entering[g, b, :, cols]) * mm(carry, e_ref[:, cols])
        for k in range(0, CHUNK, LANES):
            sl = slice(j + k, j + k + LANES)
            parts = []
            for h in ((j + k) // HEAD_DIM, (j + k) // HEAD_DIM + 1):
                spread = columns[:, h : h + 1] - lower[h : h + 1, :]
                part = (scores * jnp.exp2(spread)).astype(BF16)
                parts.append(jnp.where(allowed, part, jnp.zeros_like(part)))
            value = xc[g, rows, sl]
            none = jnp.zeros_like(value)
            pair = jnp.concatenate([jnp.where(left, value, none), jnp.where(left, none, value)], axis=0)
            y = mm(jnp.concatenate(parts, axis=1), pair)
            skip = skip_row[0:1, pl.ds(pl.multiple_of(g * wide + j + k, LANES), LANES)]
            mid[g, rows, sl] = (y + carried[:, k : k + LANES] + skip * value.astype(F32)).astype(BF16)


def stage_times(links):
    times = [0, 2, 5]
    for r in range(max(1, (links - 1).bit_length())):
        times.append(times[-1] + 5)
    return times + [times[-1] + 4, times[-1] + 6]


def early_groups(groups, turns, links):
    last = stage_times(links)[-1]
    return sum((g + 1) * turns - 1 + last < (2 * groups + g) * turns for g in range(groups - 1))


def pack_d(d):
    hi = d.astype(BF16).astype(F32)
    return jnp.concatenate([hi, d - hi], axis=0).astype(BF16)


def unpack_d(packed):
    both = packed.astype(F32)
    return both[0:8] + both[8:16]


class Exchange:
    def __init__(self, state, total_d, hin, bufs, sems):
        self.state, self.total_d, self.hin = state, total_d, hin
        (self.give1, self.take1, self.give2, self.take2, self.zgive, self.ztake, self.back2, self.home2,
         self.back1, self.home1, self.half_s, self.half_d, self.e_s, self.e_d, self.p_s, self.p_d) = bufs
        self.sem1, self.sem2, self.semz, self.sem4, self.sem5 = sems
        peers = lax.axis_size("seq")
        me = lax.axis_index("seq")
        self.me, self.peers = me, peers
        self.core, self.pair, self.link, self.links = lax.rem(me, 2), lax.rem(me // 2, 2), me // 4, peers // 4
        self.low1, self.low2 = self.core == 0, self.pair == 0
        self.near, self.far = me + 1 - 2 * self.core, me + 2 - 4 * self.pair
        self.half = state.shape[2] // 2
        self.quarter = self.half // 2
        self.rounds = max(1, (self.links - 1).bit_length())

    def copy(self, src, dst, sems, peer):
        return pltpu.make_async_remote_copy(
            src_ref=src, dst_ref=dst, send_sem=sems.at[0], recv_sem=sems.at[1],
            device_id={"seq": peer}, device_id_type=MESH,
        )

    def copy1(self, g):
        return self.copy(self.give1.at[g], self.take1.at[g], self.sem1.at[g], self.near)

    def copy2(self, g):
        return self.copy(self.give2.at[g], self.take2.at[g], self.sem2.at[g], self.far)

    def copyz(self, r, g):
        return self.copy(self.zgive.at[r, g], self.ztake.at[r, g], self.semz.at[r, g], self.me + (4 << r))

    def copy4(self, g):
        return self.copy(self.back2.at[g], self.home2.at[g], self.sem4.at[g], self.far)

    def copy5(self, g):
        return self.copy(self.back1.at[g], self.home1.at[g], self.sem5.at[g], self.near)

    def greet(self):
        me, link = self.me, self.link
        found = [(None, self.near), (None, self.far), (me >= 1, me - 1), (me + 1 < self.peers, me + 1)]
        for r in range(self.rounds):
            found += [(link >= 1 << r, me - (4 << r)), (link + (1 << r) < self.links, me + (4 << r))]
        barrier = pltpu.get_barrier_semaphore()
        expected = jnp.int32(0)
        for known, peer in found:
            if known is None:
                pl.semaphore_signal(barrier, inc=1, device_id={"seq": peer}, device_id_type=MESH)
                expected = expected + 1
            else:
                expected = expected + known.astype(jnp.int32)

                @pl.when(known)
                def _():
                    pl.semaphore_signal(barrier, inc=1, device_id={"seq": peer}, device_id_type=MESH)

        pl.semaphore_wait(barrier, expected)

    def half_lanes(self, which):
        return pl.ds(pl.multiple_of(which * self.half, LANES), self.half)

    def lanes(self, q):
        return pl.ds(pl.multiple_of(self.core * self.half + q * self.quarter, LANES), self.quarter)

    def inner(self, q):
        return pl.ds(pl.multiple_of(q * self.quarter, LANES), self.quarter)

    def stage(self, k, g):
        if k == 0:
            self.begin(g)
        elif k == 1:
            self.cores(g)
        elif k == 2:
            self.chips(g)
        elif k < 3 + self.rounds:
            self.along(k - 3, g)
            if k == 2 + self.rounds:
                self.enter(g)
        elif k == 3 + self.rounds:
            self.share(g)
        else:
            self.finish(g)

    def begin(self, g):
        other = self.half_lanes(1 - self.core)
        self.give1[g, 0:STATE, :] = self.state[g, :, other].astype(BF16)
        self.give1[g, STATE:, :] = pack_d(self.total_d[g, :, other])
        self.copy1(g).start()

    def of_chip(self, g, q):
        mine, other = self.state[g, :, self.lanes(q)], self.take1[g, 0:STATE, self.inner(q)].astype(F32)
        d_mine, d_other = self.total_d[g, :, self.lanes(q)], unpack_d(self.take1[g, STATE:, self.inner(q)])
        late = jnp.where(self.low1, d_other, d_mine)[0:1]
        total = late * jnp.where(self.low1, mine, other) + jnp.where(self.low1, other, mine)
        return total, d_mine * d_other

    def cores(self, g):
        self.copy1(g).wait()
        total, d = self.of_chip(g, 1 - self.pair)
        self.give2[g, 0:STATE, :] = total.astype(BF16)
        self.give2[g, STATE:, :] = pack_d(d)
        self.copy2(g).start()
        total, d = self.of_chip(g, self.pair)
        self.half_s[g] = total
        self.half_d[g] = d

    def chips(self, g):
        self.copy2(g).wait()
        mine, other = self.half_s[g], self.take2[g, 0:STATE, :].astype(F32)
        d_mine, d_other = self.half_d[g], unpack_d(self.take2[g, STATE:, :])
        late = jnp.where(self.low2, d_other, d_mine)[0:1]
        self.p_s[g] = late * jnp.where(self.low2, mine, other) + jnp.where(self.low2, other, mine)
        self.p_d[g] = d_mine * d_other
        self.e_s[g] = jnp.zeros(self.e_s.shape[1:], F32)
        self.e_d[g] = jnp.ones(self.e_d.shape[1:], F32)
        self.pass_on(0, g)

    def pass_on(self, r, g):
        @pl.when(self.link + (1 << r) < self.links)
        def _():
            self.zgive[r, g, 0:STATE, :] = self.p_s[g].astype(BF16)
            self.zgive[r, g, STATE:, :] = pack_d(self.p_d[g])
            self.copyz(r, g).start()

    def along(self, r, g):
        @pl.when(self.link >= 1 << r)
        def _():
            self.copyz(r, g).wait_recv()
            got, d = self.ztake[r, g, 0:STATE, :].astype(F32), unpack_d(self.ztake[r, g, STATE:, :])
            self.e_s[g] = self.e_d[g, 0:1, :] * got + self.e_s[g]
            self.e_d[g] = self.e_d[g] * d
            if r + 1 < self.rounds:
                self.p_s[g] = self.p_d[g, 0:1, :] * got + self.p_s[g]
                self.p_d[g] = self.p_d[g] * d

        if r + 1 < self.rounds:
            self.pass_on(r + 1, g)

    def hand_over(self, g, q, into):
        mine, other = self.state[g, :, self.lanes(q)], self.take1[g, 0:STATE, self.inner(q)].astype(F32)
        d_mine, d_other = self.total_d[g, :, self.lanes(q)], unpack_d(self.take1[g, STATE:, self.inner(q)])
        early = jnp.where(self.low1, d_mine, d_other)[0:1]
        passed = early * into + jnp.where(self.low1, mine, other)
        self.hin[g, :, self.lanes(q)] = jnp.where(self.low1, into, passed).astype(BF16)
        self.back1[g, :, self.inner(q)] = jnp.where(self.low1, passed, into).astype(BF16)

    def enter(self, g):
        into = self.e_s[g]
        mine, other = self.half_s[g], self.take2[g, 0:STATE, :].astype(F32)
        d_mine, d_other = self.half_d[g], unpack_d(self.take2[g, STATE:, :])
        early = jnp.where(self.low2, d_mine, d_other)[0:1]
        passed = early * into + jnp.where(self.low2, mine, other)
        self.back2[g] = jnp.where(self.low2, passed, into).astype(BF16)
        self.copy4(g).start()
        self.hand_over(g, self.pair, jnp.where(self.low2, into, passed))

    def share(self, g):
        self.copy4(g).wait()
        self.hand_over(g, 1 - self.pair, self.home2[g].astype(F32))
        self.copy5(g).start()

    def finish(self, g):
        self.copy5(g).wait()
        self.hin[g, :, self.half_lanes(1 - self.core)] = self.home1[g]
        for r in range(self.rounds):

            @pl.when(self.link + (1 << r) < self.links)
            def _():
                self.copyz(r, g).wait_send()


def mixer_kernel(
    seg_in, x_ref, bc_ref, z_ref, dtp_in, dtb_in, dec_in, skip_in, wx_in, bx_in, wbc_in, bbc_in, gain_in,
    mid, zlate, c_ref, hin_ref, ecarry_ref, gain_ref,
    seg_ref, dtp_ref, dtb_ref, dec_ref, skip_ref, wx_ref, bx_ref, wbc_ref, bbc_ref,
    xbuf, bbuf, xtail, btail, xc, bpart, entering, state, total_d, held,
    shift_ref, mask_ref, tailw_ref, cfac_ref, ends_ref, lower_ref, cols_ref, skip_row, e_ref, hwx_ref, hwbc_ref,
    give1, take1, give2, take2, zgive, ztake, back2, home2, back1, home1,
    half_s, half_d, e_s, e_d, p_s, p_d,
    sem1, sem2, semz, sem4, sem5, semx, semb, semt, semg, semw,
):
    groups, _, wide = xbuf.shape
    rows = x_ref.shape[0]
    blocks = rows // BLOCK
    step = 2 - blocks % 2
    turns = blocks // step
    repeat = e_ref.shape[0] // 2
    late = zlate.shape[0]
    early = groups - late
    exchange = Exchange(
        state, total_d, hin_ref,
        (give1, take1, give2, take2, zgive, ztake, back2, home2, back1, home1, half_s, half_d, e_s, e_d, p_s, p_d),
        (sem1, sem2, semz, sem4, sem5),
    )
    me, peers = exchange.me, exchange.peers
    times = stage_times(exchange.links)

    def lanes_of(g, width):
        return pl.ds(pl.multiple_of(g * width, LANES), width)

    def load_x(g):
        return pltpu.make_async_copy(
            x_ref.at[:, lanes_of(g, wide)], xbuf.at[g, pl.ds(TAIL, rows), :], semx.at[g]
        )

    def load_b(g):
        return pltpu.make_async_copy(
            bc_ref.at[:, lanes_of(g, 2 * STATE)], bbuf.at[g, pl.ds(TAIL, rows), :], semb.at[g]
        )

    def load_z(g):
        where = zlate.at[g - early] if g >= early else xbuf.at[g, pl.ds(TAIL, rows), :]
        return pltpu.make_async_copy(z_ref.at[:, lanes_of(g, wide)], where, semg.at[g])

    small = [
        pltpu.make_async_copy(src, dst, semw.at[n])
        for n, (src, dst) in enumerate((
            (seg_in, seg_ref), (dtp_in, dtp_ref), (dtb_in, dtb_ref), (dec_in, dec_ref), (skip_in, skip_ref),
            (wx_in, wx_ref), (bx_in, bx_ref), (wbc_in, wbc_ref), (bbc_in, bbc_ref), (gain_in, gain_ref),
        ))
    ]
    for load in small:
        load.start()
    load_b(0).start()
    load_x(0).start()
    tails = [
        exchange.copy(x_ref.at[pl.ds(rows - TAIL, TAIL), :], xtail, semt.at[0], me + 1),
        exchange.copy(bc_ref.at[pl.ds(rows - TAIL, TAIL), :], btail, semt.at[1], me + 1),
    ]
    exchange.greet()

    @pl.when(me + 1 < peers)
    def _():
        for tail in tails:
            tail.start()

    for load in small:
        load.wait()
    prepare(
        seg_ref, dtp_ref, dtb_ref, dec_ref, skip_ref, wx_ref, bx_ref, wbc_ref, bbc_ref,
        ecarry_ref, shift_ref, mask_ref, tailw_ref, cfac_ref, ends_ref, lower_ref, cols_ref, skip_row, total_d, e_ref,
        hwx_ref, hwbc_ref,
    )

    @pl.when(me == 0)
    def _():
        xtail[...] = jnp.zeros(xtail.shape, BF16)
        btail[...] = jnp.zeros(btail.shape, BF16)

    @pl.when(me > 0)
    def _():
        for tail in tails:
            tail.wait_recv()

    def stages(turn, p, which):
        for at in range(turns):
            due = [k for k in which if (turns - 1 + times[k]) % turns == at]
            if not due:
                continue

            @pl.when(p == at)
            def _():
                for k in due:
                    g = turn - (turns - 1 + times[k]) // turns

                    @pl.when((g >= 0) & (g < groups))
                    def _():
                        exchange.stage(k, g)

    def first_part(i, carry):
        g, p = lax.div(i, turns), lax.rem(i, turns)

        @pl.when(p == 0)
        def _():
            @pl.when(g + 1 < groups)
            def _():
                load_b(g + 1).start()
                load_x(g + 1).start()

            state[g] = jnp.zeros(state.shape[1:], F32)
            load_b(g).wait()
            load_x(g).wait()
            xbuf[g, 0:TAIL, :] = xtail[:, lanes_of(g, wide)]
            bbuf[g, 0:TAIL, :] = btail[:, lanes_of(g, 2 * STATE)]

        units = []
        for b in range(step):
            units += states_of(
                g, step * p + b, xbuf, bbuf, hwx_ref, hwbc_ref, shift_ref, tailw_ref, ends_ref, e_ref,
                xc, bpart, c_ref, entering, state,
            )
        pipelined(units)
        stages(g, p, range(len(times)))
        return carry

    def second_part(i, carry):
        g, p = lax.div(i, turns), lax.rem(i, turns)
        for b in range(step):
            within_of(
                g, step * p + b, xc, bpart, c_ref, entering,
                mask_ref, cfac_ref, lower_ref, cols_ref, skip_row, e_ref, mid,
            )
        stages(g + groups, p, range(1, len(times)))
        return carry

    def third_part(i, carry):
        g, p = lax.div(i, turns), lax.rem(i, turns)
        heads = pl.ds(pl.multiple_of(g * repeat, repeat), repeat)
        units = []
        for b in range(step):
            low = (step * p + b) * BLOCK
            tokens = pl.ds(pl.multiple_of(low, BLOCK), BLOCK)
            units += gate(
                mid.at[g, tokens, :], xbuf.at[g, pl.ds(pl.multiple_of(low + TAIL, TAIL), BLOCK), :],
                c_ref.at[g, tokens, :], hin_ref.at[g], ecarry_ref.at[heads, tokens], gain_ref.at[:, lanes_of(g, wide)],
                e_ref, held.at[b * BLOCK : (b + 1) * BLOCK], mid.at[g, tokens, :],
            )
        pipelined(units)
        stages(g + 2 * groups, p, range(1, len(times)))
        return carry

    lax.fori_loop(0, groups * turns, first_part, 0)
    for g in range(groups):
        load_z(g).start()
    lax.fori_loop(0, groups * turns, second_part, 0)
    for g in range(early):
        load_z(g).wait()
    if early:
        lax.fori_loop(0, early * turns, third_part, 0)
    for i in range((2 * groups + early) * turns, groups * turns + times[-1]):
        for k in range(1, len(times)):
            n = i - (turns - 1) - times[k]
            if n >= 0 and n % turns == 0 and n < groups * turns:
                exchange.stage(k, n // turns)
    for g in range(early, groups):
        load_z(g).wait()

    @pl.when(me + 1 < peers)
    def _():
        for tail in tails:
            tail.wait_send()


def gate(y_ref, z_ref, c_ref, hin_ref, weights_ref, gain_ref, e_ref, held_ref, out_ref):
    wide = y_ref.shape[1]
    shared = {"squares": jnp.zeros((BLOCK, LANES), F32)}

    def unit(j):
        cols = slice(j, j + CHUNK)
        mine = {}

        def begin():
            if j == 0:
                shared["turned"] = jnp.transpose(halves(weights_ref[...]).astype(F32)).astype(BF16)
                shared["c"] = c_ref[...]
            pass

        def work():
            mine["read"] = mm(shared["c"], hin_ref[:, cols])
            mine["factor"] = mm(shared["turned"], e_ref[:, cols])
            kept = []
            for r in range(0, BLOCK, PIECE):
                here = slice(r, r + PIECE)
                full = y_ref[here, cols].astype(F32) + mine["read"][here] * mine["factor"][here]
                z = z_ref[here, cols]
                scaled = full * z.astype(F32)
                held = scaled + scaled * jnp.tanh((z * BF16(0.5)).astype(F32))
                held_ref[here, cols] = held
                piece = held * held
                kept.append(piece[:, 0:LANES] + piece[:, LANES:CHUNK])
            shared["squares"] = shared["squares"] + jnp.concatenate(kept, axis=0)

        def end():
            pass

        return begin, work, end

    def scale_all():
        mean = jnp.sum(shared["squares"], axis=1, keepdims=True) * (1.0 / wide)
        shared["scale"] = jnp.broadcast_to(lax.rsqrt(mean + 1e-05), (BLOCK, LANES))

    def write():
        for j in range(0, wide, LANES):
            sl = slice(j, j + LANES)
            out_ref[:, sl] = (held_ref[:, sl] * shared["scale"] * gain_ref[0:1, sl]).astype(BF16)

    return [unit(j) for j in range(0, wide, CHUNK)] + [(lambda: None, scale_all, write)]


def output_kernel(
    mid_ref, z_ref, c_ref, hin_ref, ecarry_ref, gain_ref, out_ref, e_ref, obuf, held, semo, semd,
):
    groups, rows, wide = mid_ref.shape
    late, turns, part = obuf.shape[0:3]
    early = groups - late
    repeat = e_ref.shape[0] // 2

    def done(g):
        return pltpu.make_async_copy(mid_ref.at[g], out_ref.at[:, g * wide : (g + 1) * wide], semd.at[g])

    def store(i):
        l, p = lax.div(i, turns), lax.rem(i, turns)
        lanes = pl.ds(pl.multiple_of((early + l) * wide, LANES), wide)
        return pltpu.make_async_copy(
            obuf.at[l, p], out_ref.at[pl.ds(pl.multiple_of(p * part, part), part), lanes], semo.at[i]
        )

    for g in range(early):
        done(g).start()
    fill_spread(e_ref)

    def step(i, carry):
        l, p = lax.div(i, turns), lax.rem(i, turns)
        g = early + l
        heads = pl.ds(pl.multiple_of(g * repeat, repeat), repeat)
        units = []
        for r in range(0, part, BLOCK):
            tokens = pl.ds(pl.multiple_of(p * part + r, BLOCK), BLOCK)
            units += gate(
                mid_ref.at[g, tokens, :], z_ref.at[l, tokens, :], c_ref.at[g, tokens, :], hin_ref.at[g],
                ecarry_ref.at[heads, tokens], gain_ref.at[:, pl.ds(pl.multiple_of(g * wide, LANES), wide)],
                e_ref, held.at[r : r + BLOCK], obuf.at[l, p, r : r + BLOCK, :],
            )
        pipelined(units)
        store(i).start()
        return carry

    lax.fori_loop(0, late * turns, step, 0)
    for i in range(late * turns):
        store(jnp.int32(i)).wait()
    for g in range(early):
        done(g).wait()


def shards(
    x_proj, z_gate, bc_proj, dt_proj, dt_bias, decay_log, skip_gain,
    conv_x, bias_x, conv_bc, bias_bc, norm_gain, seg_lengths,
):
    rows, channels = x_proj.shape
    heads = dt_proj.shape[1]
    groups = bc_proj.shape[1]
    repeat = heads // groups
    wide = channels // groups
    blocks = rows // BLOCK
    step = 2 - blocks % 2
    turns = blocks // step
    links = lax.axis_size("seq") // 4
    rounds = max(1, (links - 1).bit_length())
    bc = bc_proj.reshape(rows, groups * 2 * STATE)
    vmem = pl.BlockSpec(memory_space=pltpu.VMEM)
    anywhere = pl.BlockSpec(memory_space=pl.ANY)
    pin = lambda array: pltpu.with_memory_space_constraint(array, pltpu.HBM)
    outside = pl.BlockSpec(memory_space=pltpu.HBM)
    half, quarter = wide // 2, wide // 4
    scratch = lambda kind, *shape: pltpu.VMEM(shape, kind)
    dma = lambda *shape: pltpu.SemaphoreType.DMA(shape)
    per_block = (blocks, heads, BLOCK)
    early = early_groups(groups, turns, links)
    mid, zlate, c, hin, ecarry, gain = pl.pallas_call(
        mixer_kernel,
        in_specs=[outside, anywhere, anywhere, anywhere] + [outside] * 9,
        out_specs=[vmem] * 6,
        out_shape=[
            jax.ShapeDtypeStruct((groups, rows, wide), BF16),
            jax.ShapeDtypeStruct((groups - early, rows, wide), BF16),
            jax.ShapeDtypeStruct((groups, rows, STATE), BF16),
            jax.ShapeDtypeStruct((groups, STATE, wide), BF16),
            jax.ShapeDtypeStruct((heads, rows), F32),
            jax.ShapeDtypeStruct((1, channels), F32),
        ],
        scratch_shapes=[
            pltpu.SMEM(seg_lengths.shape, jnp.int32), scratch(BF16, heads, rows),
            scratch(F32, 1, heads), scratch(F32, 1, heads), scratch(F32, 1, heads),
            scratch(F32, *conv_x.shape), scratch(F32, 1, channels), scratch(F32, *conv_bc.shape), scratch(F32, *bias_bc.shape),
            scratch(BF16, groups, TAIL + rows, wide), scratch(BF16, groups, TAIL + rows, 2 * STATE),
            scratch(BF16, TAIL, channels), scratch(BF16, TAIL, groups * 2 * STATE),
            scratch(BF16, groups, rows, wide), scratch(BF16, groups, rows, STATE),
            scratch(BF16, groups, blocks, STATE, wide), scratch(F32, groups, STATE, wide), scratch(F32, groups, 8, wide),
            scratch(F32, step * BLOCK, wide),
            scratch(BF16, blocks, 3 * BLOCK, TAIL + BLOCK), scratch(F32, blocks, BLOCK, BLOCK),
            scratch(F32, *per_block), scratch(F32, *per_block), scratch(F32, *per_block), scratch(F32, *per_block),
            scratch(F32, blocks * groups, BLOCK, LANES), scratch(F32, 8, channels), scratch(BF16, 2 * repeat, wide),
            scratch(F32, groups, 8, wide), scratch(F32, groups, 8, 2 * STATE),
            scratch(BF16, groups, STATE + 16, half), scratch(BF16, groups, STATE + 16, half),
            scratch(BF16, groups, STATE + 16, quarter), scratch(BF16, groups, STATE + 16, quarter),
            scratch(BF16, rounds, groups, STATE + 16, quarter), scratch(BF16, rounds, groups, STATE + 16, quarter),
            scratch(BF16, groups, STATE, quarter), scratch(BF16, groups, STATE, quarter),
            scratch(BF16, groups, STATE, half), scratch(BF16, groups, STATE, half),
            scratch(F32, groups, STATE, quarter), scratch(F32, groups, 8, quarter),
            scratch(F32, groups, STATE, quarter), scratch(F32, groups, 8, quarter),
            scratch(F32, groups, STATE, quarter), scratch(F32, groups, 8, quarter),
            dma(groups, 2), dma(groups, 2), dma(rounds, groups, 2), dma(groups, 2), dma(groups, 2),
            dma(groups), dma(groups), dma(2, 2), dma(groups), dma(10),
        ],
        compiler_params=pltpu.CompilerParams(
            collective_id=0, has_side_effects=True, vmem_limit_bytes=FIRST_LIMIT
        ),
        name="mixer",
    )(
        pin(seg_lengths), x_proj, bc, z_gate, pin(dt_proj.T), pin(dt_bias[None]), pin(decay_log[None]), pin(skip_gain[None]),
        pin(conv_x), pin(bias_x[None]), pin(conv_bc), pin(bias_bc), pin(norm_gain[None]),
    )

    late = groups - early
    return pl.pallas_call(
        output_kernel,
        in_specs=[vmem] * 6,
        out_specs=anywhere,
        out_shape=jax.ShapeDtypeStruct((rows, channels), BF16),
        scratch_shapes=[
            scratch(BF16, 2 * repeat, wide), scratch(BF16, late, turns, step * BLOCK, wide),
            scratch(F32, step * BLOCK, wide), dma(late * turns), dma(groups),
        ],
        compiler_params=pltpu.CompilerParams(vmem_limit_bytes=SECOND_LIMIT),
        name="outputs",
    )(mid, zlate, c, hin, ecarry, gain)


def solution(mesh):
    return jax.shard_map(
        shards,
        mesh=mesh,
        in_specs=(
            P(("groups", "seq"), "head"),
            P(("groups", "seq"), "head"),
            P(("groups", "seq"), "head", None),
            P(("groups", "seq"), "head"),
            P("head"),
            P("head"),
            P("head"),
            P(None, "head"),
            P("head"),
            P(None, "head", None),
            P("head", None),
            P("head"),
            P("groups"),
        ),
        out_specs=P(("groups", "seq"), "head"),
        check_vma=False,
    )
```

```python
import functools

import jax
import jax.numpy as jnp
from jax import lax
from jax.experimental import pallas as pl
from jax.experimental.pallas import tpu as pltpu
from jax.sharding import PartitionSpec as P

HEAD_DIM = 64
STATE = 128
BLOCK = 128
LANES = 128
TAIL = 16
CHUNK = 256
PIECE = 16
FIRST_LIMIT = 40 << 20
SECOND_LIMIT = 32 << 20
LOG2E = 1.4426950408889634
MESH = pl.DeviceIdType.MESH
F32 = jnp.float32
BF16 = jnp.bfloat16


def silu_of_half(half):
    return half + half * jnp.tanh(half)


def mm(a, b, dims=((1,), (0,))):
    return lax.dot_general(a, b, (dims, ((), ())), preferred_element_type=F32)


def ids_of(starts, positions):
    found = jnp.full(positions.shape, -1, jnp.int32)
    for start in starts:
        found = jnp.where(positions >= start, start, found)
    return found


def id_of(starts, position):
    found = jnp.int32(-1)
    for start in starts:
        found = jnp.where(position >= start, start, found)
    return found


def column(row):
    n = row.shape[1]
    i = lax.broadcasted_iota(jnp.int32, (n, n), 0)
    j = lax.broadcasted_iota(jnp.int32, (n, n), 1)
    return jnp.sum(jnp.where(i == j, row, 0.0), axis=1, keepdims=True)


def fill_spread(e_ref):
    twice, wide = e_ref.shape
    row = lax.broadcasted_iota(jnp.int32, (twice, wide), 0)
    lane = lax.broadcasted_iota(jnp.int32, (twice, wide), 1)
    e_ref[...] = (lane // HEAD_DIM == row % (twice // 2)).astype(F32).astype(BF16)


def halves(value):
    hi = value.astype(BF16)
    lo = (value - hi.astype(F32)).astype(BF16)
    return jnp.concatenate([hi, lo], axis=0)


def expand(value, e_ref):
    return mm(halves(value), e_ref[...], ((0,), (0,)))


def shift_matrix(within):
    t = lax.broadcasted_iota(jnp.int32, (BLOCK, TAIL + BLOCK), 0)
    i = lax.broadcasted_iota(jnp.int32, (BLOCK, TAIL + BLOCK), 1)
    steps = [((i == t + (TAIL - 3 + k)) & (within >= 3 - k)).astype(F32) for k in range(3)]
    order = [steps[k][r : r + PIECE] for r in range(0, BLOCK, PIECE) for k in range(3)]
    return jnp.concatenate(order, axis=0).astype(BF16)


def conv_pieces(past, own, halfw):
    for r in range(0, BLOCK, PIECE):
        half = halfw[4] + halfw[3] * own[TAIL + r : TAIL + r + PIECE, :].astype(F32)
        for k in range(3):
            at = 3 * r + k * PIECE
            half = half + halfw[k] * past[at : at + PIECE]
        yield slice(r, r + PIECE), silu_of_half(half)


def pipelined(units):
    for u in range(len(units) + 4):
        for phase, lag in ((0, 0), (1, 3), (2, 4)):
            if 0 <= u - lag < len(units):
                units[u - lag][phase]()


def prepare(
    seg_ref, dtp_ref, dtb_ref, dec_ref, skip_ref, wx_ref, bx_ref, wbc_ref, bbc_ref,
    ecarry_ref, shift_ref, mask_ref, tailw_ref, cfac_ref, ends_ref, lower_ref, cols_ref, skip_row, total_d, e_ref,
    hwx_ref, hwbc_ref,
):
    heads, rows = dtp_ref.shape
    groups = total_d.shape[0]
    repeat = heads // groups
    wide = e_ref.shape[1]
    fill_spread(e_ref)
    for g in range(groups):
        cols = slice(g * wide, (g + 1) * wide)
        for k in range(4):
            hwx_ref[g, k : k + 1, :] = 0.5 * wx_ref[k : k + 1, cols]
            hwbc_ref[g, k : k + 1, :] = 0.5 * wbc_ref[k, g : g + 1, :]
        hwx_ref[g, 4:5, :] = 0.5 * bx_ref[0:1, cols]
        hwbc_ref[g, 4:5, :] = 0.5 * bbc_ref[g : g + 1, :]
    skip = jnp.broadcast_to(column(skip_ref[...]), (heads, LANES))
    for g in range(groups):
        skip_row[:, g * wide : (g + 1) * wide] = 0.5 * expand(skip[g * repeat : (g + 1) * repeat, 0:8], e_ref)
    first = lax.axis_index("seq") * rows
    starts = [jnp.int32(0)]
    for j in range(seg_ref.shape[0] - 1):
        starts.append(starts[-1] + seg_ref[j])
    entered = id_of(starts, first - 1)
    bias = column(dtb_ref[...])
    rate = -LOG2E * column(jnp.exp(dec_ref[...]))
    s = lax.broadcasted_iota(jnp.int32, (BLOCK, BLOCK), 0)
    t = lax.broadcasted_iota(jnp.int32, (BLOCK, BLOCK), 1)
    upper = (s <= t).astype(F32).astype(BF16)
    base = jnp.zeros((heads, LANES), F32)
    for b in range(rows // BLOCK):
        cut = slice(b * BLOCK, (b + 1) * BLOCK)
        raw = dtp_ref[:, cut].astype(F32) + bias
        dt = jnp.maximum(raw, 0.0) + jnp.log1p(jnp.exp(-jnp.abs(raw)))
        rest = rate * dt
        parts = []
        for _ in range(3):
            parts.append(rest.astype(BF16))
            rest = rest - parts[-1].astype(F32)
        sums = mm(jnp.concatenate(parts, axis=0), upper)
        cum = sums[0:heads] + (sums[heads : 2 * heads] + sums[2 * heads : 3 * heads])
        at = first + b * BLOCK
        tall = at + s
        tall_id = ids_of(starts, tall)
        row_id = ids_of(starts, at + lax.broadcasted_iota(jnp.int32, (1, LANES), 1))
        before, end = id_of(starts, at - 1), id_of(starts, at + BLOCK - 1)
        same_end = (row_id == end).astype(F32)
        last = jnp.broadcast_to(cum[:, BLOCK - 1 : BLOCK], cum.shape)
        shift_ref[b] = shift_matrix((tall - tall_id)[:, 0:1])
        mask_ref[b] = ((t <= s) & (tall_id == row_id)).astype(F32)
        tailw_ref[b] = jnp.exp2(last - cum) * dt * same_end
        cfac_ref[b] = 0.5 * jnp.exp2(cum) * (row_id == before).astype(F32)
        ecarry_ref[:, cut] = 0.5 * jnp.exp2(base + cum) * (row_id == entered).astype(F32)
        ends_ref[b] = jnp.exp2(last) * (end == before).astype(F32)
        lower_ref[b] = cum - (jnp.log2(dt) - 1.0)
        for g in range(groups):
            cols_ref[b * groups + g, :, 0:repeat] = jnp.transpose(cum[g * repeat : (g + 1) * repeat])
        base = base + last
    leaving = id_of(starts, first + rows - 1)
    whole = jnp.exp2(base) * (leaving == entered).astype(F32)
    for g in range(groups):
        total_d[g] = expand(whole[g * repeat : (g + 1) * repeat, 0:8], e_ref)


def states_of(
    g, b, xbuf, bbuf, hwx_ref, hwbc_ref, shift_ref, tailw_ref, ends_ref, e_ref,
    xc, bpart, c_ref, entering, state,
):
    repeat = e_ref.shape[0] // 2
    wide = e_ref.shape[1]
    low = pl.multiple_of(b * BLOCK, BLOCK)
    rows, tall = pl.ds(low, BLOCK), pl.ds(low, TAIL + BLOCK)
    heads = pl.ds(pl.multiple_of(g * repeat, repeat), repeat)
    shared = {}

    def pairs_begin():
        shared["shift"] = shift_ref[b]
        shared["own"] = bbuf[g, tall, :]
        shared["past"] = mm(shared["shift"], shared["own"])
        both = jnp.concatenate([halves(tailw_ref[b, heads, :]), halves(ends_ref[b, heads, :])], axis=1)
        shared["tail"] = jnp.transpose(both.astype(F32)).astype(BF16)[0 : BLOCK + PIECE]

    def pairs_work():
        halfw = [hwbc_ref[g, k : k + 1, :] for k in range(5)]
        bc = jnp.concatenate([piece for _, piece in conv_pieces(shared["past"], shared["own"], halfw)], axis=0)
        shared["turned"] = jnp.transpose(bc[:, 0:STATE]).astype(BF16)
        bpart[g, rows, :] = bc[:, 0:STATE].astype(BF16)
        c_ref[g, rows, :] = bc[:, STATE:].astype(BF16)

    def pairs_end():
        pass

    def unit(j):
        cols = slice(j, j + CHUNK)
        mine = {}

        def begin():
            mine["own"] = xbuf[g, tall, cols]
            mine["past"] = mm(shared["shift"], mine["own"])
            mine["spread"] = mm(shared["tail"], e_ref[:, cols])
            mine["decay"] = mine["spread"][BLOCK : BLOCK + 8]

        def work():
            halfw = [hwx_ref[g, k : k + 1, cols] for k in range(5)]
            kept, scaled = [], []
            for cut, piece in conv_pieces(mine["past"], mine["own"], halfw):
                kept.append(piece.astype(BF16))
                scaled.append((piece * mine["spread"][cut]).astype(BF16))
            mine["update"] = mm(shared["turned"], jnp.concatenate(scaled, axis=0))
            xc[g, rows, cols] = jnp.concatenate(kept, axis=0)

        def end():
            old = state[g, :, cols]
            entering[g, b, :, cols] = old.astype(BF16)
            state[g, :, cols] = mine["decay"][0:1] * old + mine["update"]

        return begin, work, end

    return [(pairs_begin, pairs_work, pairs_end)] + [unit(j) for j in range(0, wide, CHUNK)]


def within_of(g, b, xc, bpart, c_ref, entering, mask_ref, cfac_ref, lower_ref, cols_ref, skip_row, e_ref, mid):
    groups = xc.shape[0]
    repeat = e_ref.shape[0] // 2
    wide = e_ref.shape[1]
    rows = pl.ds(pl.multiple_of(b * BLOCK, BLOCK), BLOCK)
    heads = pl.ds(pl.multiple_of(g * repeat, repeat), repeat)
    b_part, c_part = bpart[g, rows, :], c_ref[g, rows, :]
    scores = mm(c_part, b_part, ((1,), (1,)))
    allowed = mask_ref[b].astype(BF16) > BF16(0.5)
    carry = jnp.transpose(halves(cfac_ref[b, heads, :]).astype(F32)).astype(BF16)
    columns = cols_ref[b * groups + g]
    lower = lower_ref[b, heads, :]
    left = lax.broadcasted_iota(jnp.int32, (BLOCK, LANES), 1) < HEAD_DIM
    for j in range(0, wide, CHUNK):
        cols = slice(j, j + CHUNK)
        carried = mm(c_part, entering[g, b, :, cols]) * mm(carry, e_ref[:, cols])
        for k in range(0, CHUNK, LANES):
            sl = slice(j + k, j + k + LANES)
            parts = []
            for h in ((j + k) // HEAD_DIM, (j + k) // HEAD_DIM + 1):
                spread = columns[:, h : h + 1] - lower[h : h + 1, :]
                part = (scores * jnp.exp2(spread)).astype(BF16)
                parts.append(jnp.where(allowed, part, jnp.zeros_like(part)))
            value = xc[g, rows, sl]
            none = jnp.zeros_like(value)
            pair = jnp.concatenate([jnp.where(left, value, none), jnp.where(left, none, value)], axis=0)
            y = mm(jnp.concatenate(parts, axis=1), pair)
            skip = skip_row[0:1, pl.ds(pl.multiple_of(g * wide + j + k, LANES), LANES)]
            mid[g, rows, sl] = (y + carried[:, k : k + LANES] + skip * value.astype(F32)).astype(BF16)


def stage_times(links):
    times = [0, 2, 5]
    for r in range(max(1, (links - 1).bit_length())):
        times.append(times[-1] + 5)
    return times + [times[-1] + 4, times[-1] + 6]


def early_groups(groups, turns, links):
    last = stage_times(links)[-1]
    return sum((g + 1) * turns - 1 + last < (2 * groups + g) * turns for g in range(groups - 1))


def pack_d(d):
    hi = d.astype(BF16).astype(F32)
    return jnp.concatenate([hi, d - hi], axis=0).astype(BF16)


def unpack_d(packed):
    both = packed.astype(F32)
    return both[0:8] + both[8:16]


class Exchange:
    def __init__(self, state, total_d, hin, bufs, sems):
        self.state, self.total_d, self.hin = state, total_d, hin
        (self.give1, self.take1, self.give2, self.take2, self.zgive, self.ztake, self.back2, self.home2,
         self.back1, self.home1, self.half_s, self.half_d, self.e_s, self.e_d, self.p_s, self.p_d) = bufs
        self.sem1, self.sem2, self.semz, self.sem4, self.sem5 = sems
        peers = lax.axis_size("seq")
        me = lax.axis_index("seq")
        self.me, self.peers = me, peers
        self.core, self.pair, self.link, self.links = lax.rem(me, 2), lax.rem(me // 2, 2), me // 4, peers // 4
        self.low1, self.low2 = self.core == 0, self.pair == 0
        self.near, self.far = me + 1 - 2 * self.core, me + 2 - 4 * self.pair
        self.half = state.shape[2] // 2
        self.quarter = self.half // 2
        self.rounds = max(1, (self.links - 1).bit_length())

    def copy(self, src, dst, sems, peer):
        return pltpu.make_async_remote_copy(
            src_ref=src, dst_ref=dst, send_sem=sems.at[0], recv_sem=sems.at[1],
            device_id={"seq": peer}, device_id_type=MESH,
        )

    def copy1(self, g):
        return self.copy(self.give1.at[g], self.take1.at[g], self.sem1.at[g], self.near)

    def copy2(self, g):
        return self.copy(self.give2.at[g], self.take2.at[g], self.sem2.at[g], self.far)

    def copyz(self, r, g):
        return self.copy(self.zgive.at[r, g], self.ztake.at[r, g], self.semz.at[r, g], self.me + (4 << r))

    def copy4(self, g):
        return self.copy(self.back2.at[g], self.home2.at[g], self.sem4.at[g], self.far)

    def copy5(self, g):
        return self.copy(self.back1.at[g], self.home1.at[g], self.sem5.at[g], self.near)

    def greet(self):
        me, link = self.me, self.link
        found = [(None, self.near), (None, self.far), (me >= 1, me - 1), (me + 1 < self.peers, me + 1)]
        for r in range(self.rounds):
            found += [(link >= 1 << r, me - (4 << r)), (link + (1 << r) < self.links, me + (4 << r))]
        barrier = pltpu.get_barrier_semaphore()
        expected = jnp.int32(0)
        for known, peer in found:
            if known is None:
                pl.semaphore_signal(barrier, inc=1, device_id={"seq": peer}, device_id_type=MESH)
                expected = expected + 1
            else:
                expected = expected + known.astype(jnp.int32)

                @pl.when(known)
                def _():
                    pl.semaphore_signal(barrier, inc=1, device_id={"seq": peer}, device_id_type=MESH)

        pl.semaphore_wait(barrier, expected)

    def half_lanes(self, which):
        return pl.ds(pl.multiple_of(which * self.half, LANES), self.half)

    def lanes(self, q):
        return pl.ds(pl.multiple_of(self.core * self.half + q * self.quarter, LANES), self.quarter)

    def inner(self, q):
        return pl.ds(pl.multiple_of(q * self.quarter, LANES), self.quarter)

    def stage(self, k, g):
        if k == 0:
            self.begin(g)
        elif k == 1:
            self.cores(g)
        elif k == 2:
            self.chips(g)
        elif k < 3 + self.rounds:
            self.along(k - 3, g)
            if k == 2 + self.rounds:
                self.enter(g)
        elif k == 3 + self.rounds:
            self.share(g)
        else:
            self.finish(g)

    def begin(self, g):
        other = self.half_lanes(1 - self.core)
        self.give1[g, 0:STATE, :] = self.state[g, :, other].astype(BF16)
        self.give1[g, STATE:, :] = pack_d(self.total_d[g, :, other])
        self.copy1(g).start()

    def of_chip(self, g, q):
        mine, other = self.state[g, :, self.lanes(q)], self.take1[g, 0:STATE, self.inner(q)].astype(F32)
        d_mine, d_other = self.total_d[g, :, self.lanes(q)], unpack_d(self.take1[g, STATE:, self.inner(q)])
        late = jnp.where(self.low1, d_other, d_mine)[0:1]
        total = late * jnp.where(self.low1, mine, other) + jnp.where(self.low1, other, mine)
        return total, d_mine * d_other

    def cores(self, g):
        self.copy1(g).wait()
        total, d = self.of_chip(g, 1 - self.pair)
        self.give2[g, 0:STATE, :] = total.astype(BF16)
        self.give2[g, STATE:, :] = pack_d(d)
        self.copy2(g).start()
        total, d = self.of_chip(g, self.pair)
        self.half_s[g] = total
        self.half_d[g] = d

    def chips(self, g):
        self.copy2(g).wait()
        mine, other = self.half_s[g], self.take2[g, 0:STATE, :].astype(F32)
        d_mine, d_other = self.half_d[g], unpack_d(self.take2[g, STATE:, :])
        late = jnp.where(self.low2, d_other, d_mine)[0:1]
        self.p_s[g] = late * jnp.where(self.low2, mine, other) + jnp.where(self.low2, other, mine)
        self.p_d[g] = d_mine * d_other
        self.e_s[g] = jnp.zeros(self.e_s.shape[1:], F32)
        self.e_d[g] = jnp.ones(self.e_d.shape[1:], F32)
        self.pass_on(0, g)

    def pass_on(self, r, g):
        @pl.when(self.link + (1 << r) < self.links)
        def _():
            self.zgive[r, g, 0:STATE, :] = self.p_s[g].astype(BF16)
            self.zgive[r, g, STATE:, :] = pack_d(self.p_d[g])
            self.copyz(r, g).start()

    def along(self, r, g):
        @pl.when(self.link >= 1 << r)
        def _():
            self.copyz(r, g).wait_recv()
            got, d = self.ztake[r, g, 0:STATE, :].astype(F32), unpack_d(self.ztake[r, g, STATE:, :])
            self.e_s[g] = self.e_d[g, 0:1, :] * got + self.e_s[g]
            self.e_d[g] = self.e_d[g] * d
            if r + 1 < self.rounds:
                self.p_s[g] = self.p_d[g, 0:1, :] * got + self.p_s[g]
                self.p_d[g] = self.p_d[g] * d

        if r + 1 < self.rounds:
            self.pass_on(r + 1, g)

    def hand_over(self, g, q, into):
        mine, other = self.state[g, :, self.lanes(q)], self.take1[g, 0:STATE, self.inner(q)].astype(F32)
        d_mine, d_other = self.total_d[g, :, self.lanes(q)], unpack_d(self.take1[g, STATE:, self.inner(q)])
        early = jnp.where(self.low1, d_mine, d_other)[0:1]
        passed = early * into + jnp.where(self.low1, mine, other)
        self.hin[g, :, self.lanes(q)] = jnp.where(self.low1, into, passed).astype(BF16)
        self.back1[g, :, self.inner(q)] = jnp.where(self.low1, passed, into).astype(BF16)

    def enter(self, g):
        into = self.e_s[g]
        mine, other = self.half_s[g], self.take2[g, 0:STATE, :].astype(F32)
        d_mine, d_other = self.half_d[g], unpack_d(self.take2[g, STATE:, :])
        early = jnp.where(self.low2, d_mine, d_other)[0:1]
        passed = early * into + jnp.where(self.low2, mine, other)
        self.back2[g] = jnp.where(self.low2, passed, into).astype(BF16)
        self.copy4(g).start()
        self.hand_over(g, self.pair, jnp.where(self.low2, into, passed))

    def share(self, g):
        self.copy4(g).wait()
        self.hand_over(g, 1 - self.pair, self.home2[g].astype(F32))
        self.copy5(g).start()

    def finish(self, g):
        self.copy5(g).wait()
        self.hin[g, :, self.half_lanes(1 - self.core)] = self.home1[g]
        for r in range(self.rounds):

            @pl.when(self.link + (1 << r) < self.links)
            def _():
                self.copyz(r, g).wait_send()


def mixer_kernel(
    seg_in, x_ref, bc_ref, z_ref, dtp_in, dtb_in, dec_in, skip_in, wx_in, bx_in, wbc_in, bbc_in, gain_in,
    mid, zlate, c_ref, hin_ref, ecarry_ref, gain_ref,
    seg_ref, dtp_ref, dtb_ref, dec_ref, skip_ref, wx_ref, bx_ref, wbc_ref, bbc_ref,
    xbuf, bbuf, xtail, btail, xc, bpart, entering, state, total_d, held,
    shift_ref, mask_ref, tailw_ref, cfac_ref, ends_ref, lower_ref, cols_ref, skip_row, e_ref, hwx_ref, hwbc_ref,
    give1, take1, give2, take2, zgive, ztake, back2, home2, back1, home1,
    half_s, half_d, e_s, e_d, p_s, p_d,
    sem1, sem2, semz, sem4, sem5, semx, semb, semt, semg, semw,
):
    groups, _, wide = xbuf.shape
    rows = x_ref.shape[0]
    blocks = rows // BLOCK
    step = 2 - blocks % 2
    turns = blocks // step
    repeat = e_ref.shape[0] // 2
    late = zlate.shape[0]
    early = groups - late
    exchange = Exchange(
        state, total_d, hin_ref,
        (give1, take1, give2, take2, zgive, ztake, back2, home2, back1, home1, half_s, half_d, e_s, e_d, p_s, p_d),
        (sem1, sem2, semz, sem4, sem5),
    )
    me, peers = exchange.me, exchange.peers
    times = stage_times(exchange.links)

    def lanes_of(g, width):
        return pl.ds(pl.multiple_of(g * width, LANES), width)

    def load_x(g):
        return pltpu.make_async_copy(
            x_ref.at[:, lanes_of(g, wide)], xbuf.at[g, pl.ds(TAIL, rows), :], semx.at[g]
        )

    def load_b(g):
        return pltpu.make_async_copy(
            bc_ref.at[:, lanes_of(g, 2 * STATE)], bbuf.at[g, pl.ds(TAIL, rows), :], semb.at[g]
        )

    def load_z(g):
        where = zlate.at[g - early] if g >= early else xbuf.at[g, pl.ds(TAIL, rows), :]
        return pltpu.make_async_copy(z_ref.at[:, lanes_of(g, wide)], where, semg.at[g])

    small = [
        pltpu.make_async_copy(src, dst, semw.at[n])
        for n, (src, dst) in enumerate((
            (seg_in, seg_ref), (dtp_in, dtp_ref), (dtb_in, dtb_ref), (dec_in, dec_ref), (skip_in, skip_ref),
            (wx_in, wx_ref), (bx_in, bx_ref), (wbc_in, wbc_ref), (bbc_in, bbc_ref), (gain_in, gain_ref),
        ))
    ]
    for load in small:
        load.start()
    load_b(0).start()
    load_x(0).start()
    tails = [
        exchange.copy(x_ref.at[pl.ds(rows - TAIL, TAIL), :], xtail, semt.at[0], me + 1),
        exchange.copy(bc_ref.at[pl.ds(rows - TAIL, TAIL), :], btail, semt.at[1], me + 1),
    ]
    exchange.greet()

    @pl.when(me + 1 < peers)
    def _():
        for tail in tails:
            tail.start()

    for load in small:
        load.wait()
    prepare(
        seg_ref, dtp_ref, dtb_ref, dec_ref, skip_ref, wx_ref, bx_ref, wbc_ref, bbc_ref,
        ecarry_ref, shift_ref, mask_ref, tailw_ref, cfac_ref, ends_ref, lower_ref, cols_ref, skip_row, total_d, e_ref,
        hwx_ref, hwbc_ref,
    )

    @pl.when(me == 0)
    def _():
        xtail[...] = jnp.zeros(xtail.shape, BF16)
        btail[...] = jnp.zeros(btail.shape, BF16)

    @pl.when(me > 0)
    def _():
        for tail in tails:
            tail.wait_recv()

    def stages(turn, p, which):
        for at in range(turns):
            due = [k for k in which if (turns - 1 + times[k]) % turns == at]
            if not due:
                continue

            @pl.when(p == at)
            def _():
                for k in due:
                    g = turn - (turns - 1 + times[k]) // turns

                    @pl.when((g >= 0) & (g < groups))
                    def _():
                        exchange.stage(k, g)

    def first_part(i, carry):
        g, p = lax.div(i, turns), lax.rem(i, turns)

        @pl.when(p == 0)
        def _():
            @pl.when(g + 1 < groups)
            def _():
                load_b(g + 1).start()
                load_x(g + 1).start()

            state[g] = jnp.zeros(state.shape[1:], F32)
            load_b(g).wait()
            load_x(g).wait()
            xbuf[g, 0:TAIL, :] = xtail[:, lanes_of(g, wide)]
            bbuf[g, 0:TAIL, :] = btail[:, lanes_of(g, 2 * STATE)]

        units = []
        for b in range(step):
            units += states_of(
                g, step * p + b, xbuf, bbuf, hwx_ref, hwbc_ref, shift_ref, tailw_ref, ends_ref, e_ref,
                xc, bpart, c_ref, entering, state,
            )
        pipelined(units)
        stages(g, p, range(len(times)))
        return carry

    def second_part(i, carry):
        g, p = lax.div(i, turns), lax.rem(i, turns)
        for b in range(step):
            within_of(
                g, step * p + b, xc, bpart, c_ref, entering,
                mask_ref, cfac_ref, lower_ref, cols_ref, skip_row, e_ref, mid,
            )
        stages(g + groups, p, range(1, len(times)))
        return carry

    def third_part(i, carry):
        g, p = lax.div(i, turns), lax.rem(i, turns)
        heads = pl.ds(pl.multiple_of(g * repeat, repeat), repeat)
        units = []
        for b in range(step):
            low = (step * p + b) * BLOCK
            tokens = pl.ds(pl.multiple_of(low, BLOCK), BLOCK)
            units += gate(
                mid.at[g, tokens, :], xbuf.at[g, pl.ds(pl.multiple_of(low + TAIL, TAIL), BLOCK), :],
                c_ref.at[g, tokens, :], hin_ref.at[g], ecarry_ref.at[heads, tokens], gain_ref.at[:, lanes_of(g, wide)],
                e_ref, held.at[b * BLOCK : (b + 1) * BLOCK], mid.at[g, tokens, :],
            )
        pipelined(units)
        stages(g + 2 * groups, p, range(1, len(times)))
        return carry

    lax.fori_loop(0, groups * turns, first_part, 0)
    for g in range(groups):
        load_z(g).start()
    lax.fori_loop(0, groups * turns, second_part, 0)
    for g in range(early):
        load_z(g).wait()
    if early:
        lax.fori_loop(0, early * turns, third_part, 0)
    for i in range((2 * groups + early) * turns, groups * turns + times[-1]):
        for k in range(1, len(times)):
            n = i - (turns - 1) - times[k]
            if n >= 0 and n % turns == 0 and n < groups * turns:
                exchange.stage(k, n // turns)
    for g in range(early, groups):
        load_z(g).wait()

    @pl.when(me + 1 < peers)
    def _():
        for tail in tails:
            tail.wait_send()


def gate(y_ref, z_ref, c_ref, hin_ref, weights_ref, gain_ref, e_ref, held_ref, out_ref):
    wide = y_ref.shape[1]
    shared = {"squares": jnp.zeros((BLOCK, LANES), F32)}

    def unit(j):
        cols = slice(j, j + CHUNK)
        mine = {}

        def begin():
            if j == 0:
                shared["turned"] = jnp.transpose(halves(weights_ref[...]).astype(F32)).astype(BF16)
                shared["c"] = c_ref[...]
            pass

        def work():
            mine["read"] = mm(shared["c"], hin_ref[:, cols])
            mine["factor"] = mm(shared["turned"], e_ref[:, cols])
            kept = []
            for r in range(0, BLOCK, PIECE):
                here = slice(r, r + PIECE)
                full = y_ref[here, cols].astype(F32) + mine["read"][here] * mine["factor"][here]
                z = z_ref[here, cols]
                scaled = full * z.astype(F32)
                held = scaled + scaled * jnp.tanh((z * BF16(0.5)).astype(F32))
                held_ref[here, cols] = held
                piece = held * held
                kept.append(piece[:, 0:LANES] + piece[:, LANES:CHUNK])
            shared["squares"] = shared["squares"] + jnp.concatenate(kept, axis=0)

        def end():
            pass

        return begin, work, end

    def scale_all():
        mean = jnp.sum(shared["squares"], axis=1, keepdims=True) * (1.0 / wide)
        shared["scale"] = jnp.broadcast_to(lax.rsqrt(mean + 1e-05), (BLOCK, LANES))

    def write():
        for j in range(0, wide, LANES):
            sl = slice(j, j + LANES)
            out_ref[:, sl] = (held_ref[:, sl] * shared["scale"] * gain_ref[0:1, sl]).astype(BF16)

    return [unit(j) for j in range(0, wide, CHUNK)] + [(lambda: None, scale_all, write)]


def output_kernel(
    mid_ref, z_ref, c_ref, hin_ref, ecarry_ref, gain_ref, out_ref, e_ref, obuf, held, semo, semd,
):
    groups, rows, wide = mid_ref.shape
    late, turns, part = obuf.shape[0:3]
    early = groups - late
    repeat = e_ref.shape[0] // 2

    def done(g):
        return pltpu.make_async_copy(mid_ref.at[g], out_ref.at[:, g * wide : (g + 1) * wide], semd.at[g])

    def store(i):
        l, p = lax.div(i, turns), lax.rem(i, turns)
        lanes = pl.ds(pl.multiple_of((early + l) * wide, LANES), wide)
        return pltpu.make_async_copy(
            obuf.at[l, p], out_ref.at[pl.ds(pl.multiple_of(p * part, part), part), lanes], semo.at[i]
        )

    for g in range(early):
        done(g).start()
    fill_spread(e_ref)

    def step(i, carry):
        l, p = lax.div(i, turns), lax.rem(i, turns)
        g = early + l
        heads = pl.ds(pl.multiple_of(g * repeat, repeat), repeat)
        units = []
        for r in range(0, part, BLOCK):
            tokens = pl.ds(pl.multiple_of(p * part + r, BLOCK), BLOCK)
            units += gate(
                mid_ref.at[g, tokens, :], z_ref.at[l, tokens, :], c_ref.at[g, tokens, :], hin_ref.at[g],
                ecarry_ref.at[heads, tokens], gain_ref.at[:, pl.ds(pl.multiple_of(g * wide, LANES), wide)],
                e_ref, held.at[r : r + BLOCK], obuf.at[l, p, r : r + BLOCK, :],
            )
        pipelined(units)
        store(i).start()
        return carry

    lax.fori_loop(0, late * turns, step, 0)
    for i in range(late * turns):
        store(jnp.int32(i)).wait()
    for g in range(early):
        done(g).wait()


def shards(
    x_proj, z_gate, bc_proj, dt_proj, dt_bias, decay_log, skip_gain,
    conv_x, bias_x, conv_bc, bias_bc, norm_gain, seg_lengths,
):
    rows, channels = x_proj.shape
    heads = dt_proj.shape[1]
    groups = bc_proj.shape[1]
    repeat = heads // groups
    wide = channels // groups
    blocks = rows // BLOCK
    step = 2 - blocks % 2
    turns = blocks // step
    links = lax.axis_size("seq") // 4
    rounds = max(1, (links - 1).bit_length())
    bc = bc_proj.reshape(rows, groups * 2 * STATE)
    vmem = pl.BlockSpec(memory_space=pltpu.VMEM)
    anywhere = pl.BlockSpec(memory_space=pl.ANY)
    pin = lambda array: pltpu.with_memory_space_constraint(array, pltpu.HBM)
    outside = pl.BlockSpec(memory_space=pltpu.HBM)
    half, quarter = wide // 2, wide // 4
    scratch = lambda kind, *shape: pltpu.VMEM(shape, kind)
    dma = lambda *shape: pltpu.SemaphoreType.DMA(shape)
    per_block = (blocks, heads, BLOCK)
    early = early_groups(groups, turns, links)
    mid, zlate, c, hin, ecarry, gain = pl.pallas_call(
        mixer_kernel,
        in_specs=[outside, anywhere, anywhere, anywhere] + [outside] * 9,
        out_specs=[vmem] * 6,
        out_shape=[
            jax.ShapeDtypeStruct((groups, rows, wide), BF16),
            jax.ShapeDtypeStruct((groups - early, rows, wide), BF16),
            jax.ShapeDtypeStruct((groups, rows, STATE), BF16),
            jax.ShapeDtypeStruct((groups, STATE, wide), BF16),
            jax.ShapeDtypeStruct((heads, rows), F32),
            jax.ShapeDtypeStruct((1, channels), F32),
        ],
        scratch_shapes=[
            pltpu.SMEM(seg_lengths.shape, jnp.int32), scratch(BF16, heads, rows),
            scratch(F32, 1, heads), scratch(F32, 1, heads), scratch(F32, 1, heads),
            scratch(F32, *conv_x.shape), scratch(F32, 1, channels), scratch(F32, *conv_bc.shape), scratch(F32, *bias_bc.shape),
            scratch(BF16, groups, TAIL + rows, wide), scratch(BF16, groups, TAIL + rows, 2 * STATE),
            scratch(BF16, TAIL, channels), scratch(BF16, TAIL, groups * 2 * STATE),
            scratch(BF16, groups, rows, wide), scratch(BF16, groups, rows, STATE),
            scratch(BF16, groups, blocks, STATE, wide), scratch(F32, groups, STATE, wide), scratch(F32, groups, 8, wide),
            scratch(F32, step * BLOCK, wide),
            scratch(BF16, blocks, 3 * BLOCK, TAIL + BLOCK), scratch(F32, blocks, BLOCK, BLOCK),
            scratch(F32, *per_block), scratch(F32, *per_block), scratch(F32, *per_block), scratch(F32, *per_block),
            scratch(F32, blocks * groups, BLOCK, LANES), scratch(F32, 8, channels), scratch(BF16, 2 * repeat, wide),
            scratch(F32, groups, 8, wide), scratch(F32, groups, 8, 2 * STATE),
            scratch(BF16, groups, STATE + 16, half), scratch(BF16, groups, STATE + 16, half),
            scratch(BF16, groups, STATE + 16, quarter), scratch(BF16, groups, STATE + 16, quarter),
            scratch(BF16, rounds, groups, STATE + 16, quarter), scratch(BF16, rounds, groups, STATE + 16, quarter),
            scratch(BF16, groups, STATE, quarter), scratch(BF16, groups, STATE, quarter),
            scratch(BF16, groups, STATE, half), scratch(BF16, groups, STATE, half),
            scratch(F32, groups, STATE, quarter), scratch(F32, groups, 8, quarter),
            scratch(F32, groups, STATE, quarter), scratch(F32, groups, 8, quarter),
            scratch(F32, groups, STATE, quarter), scratch(F32, groups, 8, quarter),
            dma(groups, 2), dma(groups, 2), dma(rounds, groups, 2), dma(groups, 2), dma(groups, 2),
            dma(groups), dma(groups), dma(2, 2), dma(groups), dma(10),
        ],
        compiler_params=pltpu.CompilerParams(
            collective_id=0, has_side_effects=True, vmem_limit_bytes=FIRST_LIMIT
        ),
        name="mixer",
    )(
        pin(seg_lengths), x_proj, bc, z_gate, pin(dt_proj.T), pin(dt_bias[None]), pin(decay_log[None]), pin(skip_gain[None]),
        pin(conv_x), pin(bias_x[None]), pin(conv_bc), pin(bias_bc), pin(norm_gain[None]),
    )

    late = groups - early
    return pl.pallas_call(
        output_kernel,
        in_specs=[vmem] * 6,
        out_specs=anywhere,
        out_shape=jax.ShapeDtypeStruct((rows, channels), BF16),
        scratch_shapes=[
            scratch(BF16, 2 * repeat, wide), scratch(BF16, late, turns, step * BLOCK, wide),
            scratch(F32, step * BLOCK, wide), dma(late * turns), dma(groups),
        ],
        compiler_params=pltpu.CompilerParams(vmem_limit_bytes=SECOND_LIMIT),
        name="outputs",
    )(mid, zlate, c, hin, ecarry, gain)


def solution(mesh):
    return jax.shard_map(
        shards,
        mesh=mesh,
        in_specs=(
            P(("groups", "seq"), "head"),
            P(("groups", "seq"), "head"),
            P(("groups", "seq"), "head", None),
            P(("groups", "seq"), "head"),
            P("head"),
            P("head"),
            P("head"),
            P(None, "head"),
            P("head"),
            P(None, "head", None),
            P("head", None),
            P("head"),
            P("groups"),
        ),
        out_specs=P(("groups", "seq"), "head"),
        check_vma=False,
    )
```
